32 devices in a mesh: dir: 2 (over y), dp: 16 (over z, x, core).
Axes of the slice: x: 2, y: 2, z: 4, core: 2. Of those that a mesh axis runs over, the one named last changes fastest.
Arguments:
- tokens: bfloat16 [16, 1024, 768], P('dp', 'dir'), may hold values from -6 to 6
- norm_gain: float32 [768], replicated, may hold values from 0.5 to 1.5
- w_zx: bfloat16 [768, 3072], P('dp'), may hold values from -0.21875 to 0.21875
- w_bc: bfloat16 [768, 128], P('dp'), may hold values from -0.21875 to 0.21875
- w_dt: bfloat16 [768, 48], P('dp'), may hold values from -0.21875 to 0.21875
- conv_w: float32 [4, 1664], replicated, may hold values from -3 to 3
- conv_b: float32 [1664], replicated, may hold values from -1.75 to 1.75
- dt_bias: float32 [48], replicated, may hold values from -4.5 to -2
- a_log: float32 [48], replicated, may hold values from -2.5 to 1.5
- d_skip: float32 [24], replicated, may hold values from 0.5 to 1.5
- out_gain: float32 [1536], replicated, may hold values from 0.5 to 1.5
- w_out: bfloat16 [1536, 768], P('dp'), may hold values from -0.15625 to 0.15625
- doc_lengths: int32 [16, 4], P('dp'), may hold values from 1 to 512, 1024 in all within a row
- out_grad: bfloat16 [16, 1024, 768], P('dp', 'dir'), may hold values from -6 to 6
Outputs:
- block_out: bfloat16 [16, 1024, 768], P('dp', 'dir')
- grad_tokens: bfloat16 [16, 1024, 768], P('dp', 'dir')
- grad_norm_gain: float32 [768], replicated
- grad_w_zx: float32 [768, 3072], replicated
- grad_w_bc: float32 [768, 128], replicated
- grad_w_dt: float32 [768, 48], replicated
- grad_conv_w: float32 [4, 1664], replicated
- grad_conv_b: float32 [1664], replicated
- grad_dt_bias: float32 [48], replicated
- grad_a_log: float32 [48], replicated
- grad_d_skip: float32 [24], replicated
- grad_out_gain: float32 [1536], replicated
- grad_w_out: float32 [1536, 768], replicated
The draws below stay inside these ranges and needn't reach their ends.
Inputs may be any that keep to these rules, and one draw needn't show every extreme that they name: `doc_lengths`: in each row the 4 lengths sum to 1024, and the longest is exactly 512.
All inputs are finite; a program needn't handle non-finite values.
Results may differ from the reference program's by a relative error of at most 0.014.
Values may be sent and summed in bfloat16 or wider, within the bound.
No kernel may reach another device: no remote copies, remote signals or barrier semaphores. Data moves between devices by JAX's collectives and lax.ppermute only.
A program may use at most 192 MiB of HBM per device.

```python
import math
from functools import partial
import jax
import jax.numpy as jnp
import numpy as np
from jax import lax

D = 768
HEADS = 24
HEADDIM = 64
STATE = 64
INNER = 1536
BLOCK = 128
CONV = 4
LEN = 1024
NDOC = 4
MOSTDOC = 512
ROWS = 16


def shard_levels(key, extent, cuts, low, largest):
    loudness, own = 1.0, jax.random.fold_in(key, 6)
    for position, blocks in cuts:
        heights = jnp.exp(jax.random.uniform(jax.random.fold_in(own, position), (blocks,), jnp.float32, low / len(cuts), largest / len(cuts)))
        loudness = loudness * jnp.repeat(heights, extent[position] // blocks).reshape([-1 if axis == position else 1 for axis in range(len(extent))])
    return loudness


def split_up(amount, total, bound, skew):
    portions = [(1 << 20) // math.isqrt(standing ** skew) + 1 for standing in range(2, amount + 1)]
    spare, counts = total - bound - (amount - 1), [1] * (amount - 1)
    while spare > 0:
        free = [i for i in range(amount - 1) if counts[i] < bound]
        mass, left = sum([portions[i] for i in free]), spare
        for i in free:
            addition = min(bound - counts[i], max(1, left * portions[i] // mass), spare)
            counts[i] = counts[i] + addition
            spare = spare - addition
    return np.array([bound] + counts)


def ragged_sizes(stream_key, amount, total, bound, skew):
    if amount == 2:
        one = jax.random.randint(stream_key, (), max(1, total - bound), min(bound, total - 1) + 1)
        return jnp.stack([one, total - one])
    tallies = jnp.asarray(split_up(amount, total, bound, skew), jnp.int32)
    twos = (amount - 1) // 2
    source_of, taker = tallies[1:1 + 2 * twos:2], tallies[2:2 + 2 * twos:2]
    margin = jnp.minimum(source_of - 1, bound - taker)
    moved = jax.random.randint(jax.random.fold_in(stream_key, 1), (twos,), 0, 1 << 20) % (margin + 1)
    tallies = tallies.at[1:1 + 2 * twos:2].set(source_of - moved).at[2:2 + 2 * twos:2].set(taker + moved)
    return tallies[jax.random.permutation(jax.random.fold_in(stream_key, 2), amount)]


def noise(stream_key, shape, width, most, shards=(), kind=jnp.bfloat16):
    values = width * jax.random.normal(stream_key, shape, jnp.float32)
    if shards:
        values = values * shard_levels(stream_key, shape, shards, -0.22, 0.18)
    return jnp.clip(values, -most, most).astype(kind)


def setup_inputs(seed: int = 0) -> dict:
    splits = jax.random.split(jax.random.key(seed), 15)
    tokens = noise(splits[0], (ROWS, LEN, D), 1.0, 6.0, ((0, 16), (1, 2)))
    norm_gain = jnp.clip(1.0 + 0.1 * jax.random.normal(splits[1], (D,), jnp.float32), 0.5, 1.5)
    w_zx = noise(splits[2], (D, 2 * INNER), D ** -0.5, 0.21875, ((0, 16),))
    w_bc = noise(splits[3], (D, 2 * STATE), D ** -0.5, 0.21875, ((0, 16),))
    w_dt = noise(splits[4], (D, 2 * HEADS), D ** -0.5, 0.21875, ((0, 16),))
    conv_w = noise(splits[5], (CONV, INNER + 2 * STATE), CONV ** -0.5, 3.0, (), jnp.float32)
    conv_b = noise(splits[6], (INNER + 2 * STATE,), 0.3, 1.75, (), jnp.float32)
    dt_bias = jnp.clip(jax.random.uniform(splits[7], (2 * HEADS,), jnp.float32, -4.5, -2.0), -4.5, -2.0)
    a_log = jnp.clip(jax.random.uniform(splits[8], (2 * HEADS,), jnp.float32, -2.5, 1.5), -2.5, 1.5)
    d_skip = jnp.clip(jax.random.uniform(splits[9], (HEADS,), jnp.float32, 0.5, 1.5), 0.5, 1.5)
    out_gain = jnp.clip(1.0 + 0.1 * jax.random.normal(splits[10], (INNER,), jnp.float32), 0.5, 1.5)
    w_out = noise(splits[11], (INNER, D), INNER ** -0.5, 0.15625, ((0, 16),))
    doc_lengths = jax.vmap(lambda own: ragged_sizes(own, NDOC, LEN, MOSTDOC, 1))(jax.random.split(splits[12], ROWS)).reshape((ROWS, NDOC)).astype(jnp.int32)
    out_grad = noise(splits[13], (ROWS, LEN, D), 1.0, 6.0, ((0, 16), (1, 2)))
    return dict(tokens=tokens, norm_gain=norm_gain, w_zx=w_zx, w_bc=w_bc, w_dt=w_dt, conv_w=conv_w, conv_b=conv_b, dt_bias=dt_bias, a_log=a_log, d_skip=d_skip, out_gain=out_gain, w_out=w_out, doc_lengths=doc_lengths, out_grad=out_grad)


@jax.custom_vjp
def low(v):
    return lax.optimization_barrier(v.astype(jnp.bfloat16)).astype(jnp.float32)

@jax.custom_vjp
def low_back(v):
    return v

def low_keep(v):
    return (low(v), None)

def low_pass(kept, grad):
    return (grad,)

def back_keep(v):
    return (v, None)

def back_low(kept, grad):
    return (low(grad),)
low.defvjp(low_keep, low_pass)
low_back.defvjp(back_keep, back_low)
highest = lax.Precision.HIGHEST
epsilon = 1e-05

def segment_ids(lengths_row, length):
    doc_ends = jnp.cumsum(lengths_row).astype(jnp.int32)
    places = jnp.arange(length, dtype=jnp.int32)
    return lax.optimization_barrier(jnp.sum((places[:, None] >= doc_ends[None, :]).astype(jnp.int32), axis=1)).astype(jnp.int32)

def conv_silu(pre_conv, seg_row, conv_w, conv_b):
    tap_count = conv_w.shape[0]
    summed = conv_b[None, :] + conv_w[tap_count - 1][None, :] * pre_conv
    for offset in range(1, tap_count):
        shifted = jnp.concatenate([jnp.zeros((offset, pre_conv.shape[1]), pre_conv.dtype), pre_conv[:-offset]], axis=0)
        seg_shift = jnp.concatenate([jnp.full((offset,), -1, jnp.int32), seg_row[:-offset]], axis=0)
        same_doc = (seg_shift == seg_row)[:, None]
        summed = summed + jnp.where(same_doc, conv_w[tap_count - 1 - offset][None, :] * shifted, 0.0)
    return jax.nn.silu(summed)

def block_step(a_neg, carried, inputs):
    states, prev_seg = carried
    x_block, b_block, c_block, dt_block, seg_block = inputs
    block_len = x_block.shape[0]
    log_rates = dt_block * a_neg[None, :]
    cumul = jnp.cumsum(log_rates, axis=0)
    cum_heads = cumul.T
    gap_log = cum_heads[:, :, None] - cum_heads[:, None, :]
    places = jnp.arange(block_len, dtype=jnp.int32)
    strictly = places[:, None] > places[None, :]
    same_doc = seg_block[:, None] == seg_block[None, :]
    decays = jnp.where((strictly & same_doc)[None], jnp.exp(jnp.minimum(gap_log, 0.0)), 0.0)
    scores = jnp.dot(c_block, b_block.T, precision=highest)
    inputs_dt = x_block * dt_block[:, :, None]
    y_inner = jnp.einsum('hts,shp->thp', decays * scores[None], inputs_dt, precision=highest)
    carried_in = jnp.where((seg_block == prev_seg)[:, None], jnp.exp(cumul), 0.0)
    y_carry = jnp.einsum('tn,hpn->thp', c_block, states, precision=highest) * carried_in[:, :, None]
    last_seg = seg_block[block_len - 1]
    tail_weights = jnp.where((seg_block == last_seg)[:, None], jnp.exp(cumul[block_len - 1][None, :] - cumul), 0.0)
    carry_keep = jnp.where(last_seg == prev_seg, jnp.exp(cumul[block_len - 1]), 0.0)
    new_states = states * carry_keep[:, None, None] + jnp.einsum('shp,sn->hpn', inputs_dt * tail_weights[:, :, None], b_block, precision=highest)
    return ((new_states, last_seg), y_inner + y_carry)

def scan_dir(x_row, b_row, c_row, dt_row, a_neg, seg_row):
    length = x_row.shape[0]
    block_count = length // BLOCK
    head_count = dt_row.shape[1]
    head_width = x_row.shape[1] // head_count
    state_width = b_row.shape[1]
    sliced = (x_row.reshape(block_count, BLOCK, head_count, head_width), b_row.reshape(block_count, BLOCK, state_width), c_row.reshape(block_count, BLOCK, state_width), dt_row.reshape(block_count, BLOCK, head_count), seg_row.reshape(block_count, BLOCK))
    initial = (jnp.zeros((head_count, head_width, state_width), x_row.dtype), jnp.array(-1, jnp.int32))
    advance = jax.checkpoint(partial(block_step, a_neg))
    _, results = lax.scan(advance, initial, sliced)
    return results.reshape(length, head_count * head_width)

def row_forward(params, x_row, lengths_row):
    norm_gain, w_zx, w_bc, w_dt, conv_w, conv_b, dt_bias, a_log, d_skip, out_gain, w_out = params
    seg_row = segment_ids(lengths_row, LEN)
    normed = low(x_row * lax.rsqrt(lax.optimization_barrier(jnp.mean(x_row * x_row, axis=1, keepdims=True)) + epsilon) * norm_gain[None, :])
    zx_proj = low_back(jnp.dot(normed, w_zx, precision=highest))
    bc_proj = low_back(jnp.dot(normed, w_bc, precision=highest))
    dt_proj = low(low_back(jnp.dot(normed, w_dt, precision=highest)))
    gate_z = zx_proj[:, :INNER]
    pre_conv = low(jnp.concatenate([zx_proj[:, INNER:], bc_proj], axis=1))
    conv_out = conv_silu(pre_conv, seg_row, conv_w, conv_b)
    x_in = conv_out[:, :INNER]
    b_in = conv_out[:, INNER:INNER + STATE]
    c_in = conv_out[:, INNER + STATE:]
    dt_fwd = jax.nn.softplus(dt_proj[:, :HEADS] + dt_bias[None, :HEADS])
    dt_rev = jax.nn.softplus(dt_proj[:, HEADS:] + dt_bias[None, HEADS:])
    a_neg = -jnp.exp(a_log)
    y_fwd = scan_dir(x_in, b_in, c_in, dt_fwd, a_neg[:HEADS], seg_row)
    y_rev = jnp.flip(scan_dir(jnp.flip(x_in, axis=0), jnp.flip(b_in, axis=0), jnp.flip(c_in, axis=0), jnp.flip(dt_rev, axis=0), a_neg[HEADS:], jnp.flip(seg_row, axis=0)), axis=0)
    skip_term = x_in * jnp.repeat(d_skip, HEADDIM)[None, :]
    mixed = low_back(y_fwd + y_rev + skip_term)
    gated = mixed * jax.nn.silu(gate_z)
    normed_out = low(gated * lax.rsqrt(lax.optimization_barrier(jnp.mean(gated * gated, axis=1, keepdims=True)) + epsilon) * out_gain[None, :])
    return x_row + jnp.dot(normed_out, w_out, precision=highest)

def reference(tokens, norm_gain, w_zx, w_bc, w_dt, conv_w, conv_b, dt_bias, a_log, d_skip, out_gain, w_out, doc_lengths, out_grad):
    params = (norm_gain, w_zx.astype(jnp.float32), w_bc.astype(jnp.float32), w_dt.astype(jnp.float32), conv_w, conv_b, dt_bias, a_log, d_skip, out_gain, w_out.astype(jnp.float32))
    x_all = tokens.astype(jnp.float32)

    def forward(param_set, x_values):

        def one_row(row_pair):
            return row_forward(param_set, row_pair[0], row_pair[1])
        return lax.map(jax.checkpoint(one_row), (x_values, doc_lengths))
    result, pullback = jax.vjp(forward, params, x_all)
    grad_params, grad_x = pullback(out_grad.astype(jnp.float32))
    return (result.astype(jnp.bfloat16), grad_x.astype(jnp.bfloat16), grad_params[0], grad_params[1], grad_params[2], grad_params[3], grad_params[4], grad_params[5], grad_params[6], grad_params[7], grad_params[8], grad_params[9], grad_params[10])
```

```python
import functools

import jax
import jax.numpy as jnp
from jax import lax
from jax.experimental import pallas as pl
from jax.experimental.pallas import tpu as pltpu
from jax.sharding import PartitionSpec as P

D = 768
HEADS = 24
HEADDIM = 64
STATE = 64
INNER = 1536
CONV = 4
NDOC = 4
PAIRS = HEADS // 2
HALO = 16
CH = 256
NCH = 7
SMALL_AT = (CONV + 2) * NCH - 1
SMALL = 64
EPS = 1e-05
LOG2E = 1.4426950408889634
BF = jnp.bfloat16
F32 = jnp.float32
HI = lax.Precision.HIGHEST


def nn(a, b):
    return lax.dot_general(a, b, (((1,), (0,)), ((), ())), preferred_element_type=F32)


def nt(a, b):
    return lax.dot_general(a, b, (((1,), (1,)), ((), ())), preferred_element_type=F32)


def iota(shape, axis):
    return lax.broadcasted_iota(jnp.int32, shape, axis)


def sigm(v):
    return 1.0 / (1.0 + jnp.exp(-v))


def lane_pair(col_a, col_b, rows):
    return jnp.where(iota((rows, 128), 1) < 64, col_a, col_b)


def params(mib=60):
    return pltpu.CompilerParams(
        dimension_semantics=("arbitrary",), vmem_limit_bytes=mib * 1024 * 1024
    )


def full(shape):
    return pl.BlockSpec(shape, lambda i: tuple(0 for _ in shape))


SMEM_SPEC = pl.BlockSpec(memory_space=pltpu.SMEM)


def doc_ids(flag, places):
    total = jnp.zeros(places.shape, jnp.int32)
    end = 0
    for k in range(NDOC):
        end = end + flag[1 + k]
        total = total + jnp.where(places >= end, 1, 0)
    return jnp.where(places < 0, -1, total)


def doc_at(flag, place):
    total = 0
    end = 0
    for k in range(NDOC):
        end = end + flag[1 + k]
        total = total + jnp.where(place >= end, 1, 0)
    return total


def doc_col(flag, T, lead=0):
    return doc_ids(flag, iota((T + lead, 1), 0) + (flag[0] * T - lead))


def doc_row(flag, T):
    return doc_ids(flag, iota((1, T), 1) + flag[0] * T)


def project_kernel(T, flag, tok, halo, gain, w, cw, cb, bias, alog,
                   norm_o, nh_o, pre_o, z_o, act_o, rows_o, wrc_o, b_o, bt_o, c_o, ct_o, st_o, ncat, pf, segc):
    step = pl.program_id(0)

    @pl.when(step == 0)
    def _():
        def norm(v):
            v = v.astype(F32)
            ms = jnp.mean(v * v, axis=1, keepdims=True)
            return (v * lax.rsqrt(ms + EPS) * gain[...]).astype(BF)

        nh = norm(halo[...])
        own = norm(tok[...])
        nh_o[...] = nh
        norm_o[...] = own
        ncat[0:HALO, :] = nh
        ncat[HALO:, :] = own
        segc[...] = doc_col(flag, T, HALO)

    proj = nn(ncat[...], w[...]).astype(BF)
    pre_o[...] = proj
    pf[...] = proj.astype(F32)
    segs = segc[...]
    here = segs[HALO:, :]
    z = cb[...] + cw[CONV - 1 : CONV, :] * pf[HALO:, :]
    for k in range(1, CONV):
        same = segs[HALO - k : HALO + T - k, :] == here
        z = z + jnp.where(same, cw[CONV - 1 - k : CONV - k, :] * pf[HALO - k : HALO + T - k, :], 0.0)
    z_o[...] = z.astype(BF)
    act = z * sigm(z)
    act_o[...] = act.astype(BF)

    @pl.when(step == 0)
    def _():
        bc = act[:, :128]
        b_o[...] = bc[:, :64].astype(BF)
        c_o[...] = bc[:, 64:].astype(BF)
        bct = bc.T
        bt_o[...] = bct[:64, :].astype(BF)
        ct_o[...] = bct[64:, :].astype(BF)
        v = pf[HALO:, 128:] + bias[...]
        dt = jnp.maximum(v, 0.0) + jnp.log1p(jnp.exp(-jnp.abs(v)))
        rate = dt * (-LOG2E * jnp.exp(alog[...]))
        rate_t = rate.T
        dt_t = dt.T
        upto = (iota((T, T), 0) <= iota((T, T), 1)).astype(F32)
        inc = lax.dot_general(rate_t, upto, (((1,), (0,)), ((), ())), precision=HI, preferred_element_type=F32)
        isf = iota((128, T), 0) < HEADS
        cum = jnp.where(isf, inc, inc - rate_t)
        ldt = jnp.log2(jnp.maximum(dt_t, 1e-37))
        key = jnp.where(isf, cum - ldt, cum + ldt)
        segv = doc_row(flag, T)
        left, right = doc_at(flag, T - 1), doc_at(flag, T)
        send_f = jnp.where(segv == left, jnp.exp2(cum[:, T - 1 :] - key), 0.0)
        send_b = jnp.where(segv == right, jnp.exp2(key), 0.0)
        recv_f = jnp.where(segv == left, jnp.exp2(cum), 0.0)
        recv_b = jnp.where(segv == right, jnp.exp2(inc[:, T - 1 :] - cum), 0.0)
        first = flag[0] == 0
        send = jnp.where(first, send_f[0:HEADS], send_b[HEADS : 2 * HEADS])
        recv = jnp.where(first, recv_b[HEADS : 2 * HEADS], recv_f[0:HEADS])
        for p in range(PAIRS):
            f, r = 2 * p, HEADS + 2 * p
            rows_o[p, 0:2, :] = cum[f : f + 2]
            rows_o[p, 2:4, :] = cum[r : r + 2]
            rows_o[p, 4:6, :] = key[f : f + 2]
            rows_o[p, 6:8, :] = key[r : r + 2]
            rows_o[p, 8:10, :] = send[f : f + 2]
            rows_o[p, 10:12, :] = recv[f : f + 2]
            rows_o[p, 12:16, :] = jnp.zeros((4, T), F32)
        recv_pad = jnp.concatenate([recv, jnp.zeros((128 - HEADS, T), F32)], axis=0)
        wrc_o[...] = recv_pad.T.astype(BF)

    @pl.when(step > 0)
    def _():
        for j in range(CH // 128):
            cols = rows_o[2 * (step - 1) + j, 8:16, :].T
            wide = lane_pair(cols[:, 0:1], cols[:, 1:2], T)
            xw = (act[:, 128 * j : 128 * (j + 1)] * wide).astype(BF)
            st_o[:, 128 * j : 128 * (j + 1)] = nn(bt_o[...], xw).astype(BF)


def project(flag, tok, halo, gain, w1, conv_w, conv_b, bias, alog):
    T = tok.shape[0]
    E = T + HALO
    chunk = lambda i: lax.rem(i + NCH - 1, NCH)
    xchunk = lambda i: jnp.maximum(i - 1, 0)
    col = lambda rows: pl.BlockSpec((rows, CH), lambda i: (0, chunk(i)))
    shapes = [
        ((T, D), BF), ((HALO, D), BF), ((E, NCH * CH), BF), ((T, NCH * CH), BF), ((T, NCH * CH), BF),
        ((PAIRS, 16, T), F32), ((T, 128), BF), ((T, 64), BF), ((64, T), BF), ((T, 64), BF), ((64, T), BF),
        ((64, INNER), BF),
    ]
    out_specs = [
        full((T, D)), full((HALO, D)), col(E), col(T), col(T), full((PAIRS, 16, T)), full((T, 128)), full((T, 64)),
        full((64, T)), full((T, 64)), full((64, T)), pl.BlockSpec((64, CH), lambda i: (0, xchunk(i))),
    ]
    return pl.pallas_call(
        functools.partial(project_kernel, T),
        grid=(NCH,),
        in_specs=[SMEM_SPEC, full((T, D)), full((HALO, D)), full((1, D)), col(D), col(CONV), col(1),
                  full((1, 128)), full((1, 128))],
        out_specs=out_specs,
        out_shape=[jax.ShapeDtypeStruct(s, d) for s, d in shapes],
        scratch_shapes=[pltpu.VMEM((E, D), BF), pltpu.VMEM((E, CH), F32), pltpu.VMEM((E, 1), jnp.int32)],
        compiler_params=params(),
        name="project",
    )(flag, tok, halo, gain, w1, conv_w, conv_b, bias, alog)


def same_doc(flag, T):
    return (doc_col(flag, T) == doc_row(flag, T)) & (iota((T, T), 0) != iota((T, T), 1))


def mix_kernel(T, flag, b, c, rows, x, skip, y_o, sc):
    Q = 128

    @pl.when(pl.program_id(0) == 0)
    def _():
        s = nt(c[...], b[...])
        sc[...] = jnp.where(same_doc(flag, T), s, 0.0)

    r = rows[0]
    cols = r[0:8].T
    x2 = x[...]
    later = iota((Q, Q), 0) > iota((Q, Q), 1)
    lane = iota((Q, 128), 1) < 64
    for i in range(T // Q):
        lo, hi = i * Q, (i + 1) * Q
        outs = []
        for h in range(2):
            cf = cols[lo:hi, h : h + 1]
            cr = cols[lo:hi, 2 + h : 3 + h]
            kf = r[4 + h : 5 + h]
            kr = r[6 + h : 7 + h]
            parts = []
            if i > 0:
                parts.append(cf - kf[:, :lo])
            parts.append(jnp.where(later, cf - kf[:, lo:hi], kr[:, lo:hi] - cr))
            if hi < T:
                parts.append(kr[:, hi:] - cr)
            e = jnp.concatenate(parts, axis=1)
            m = (sc[lo:hi, :] * jnp.exp2(e)).astype(BF)
            outs.append(nn(m, x2))
        y_o[lo:hi, :] = jnp.where(lane, outs[0], outs[1]) + skip[...] * x2[lo:hi, :].astype(F32)


def mix(flag, b, c, rows, act, skip):
    T = b.shape[0]
    blk = pl.BlockSpec((T, 128), lambda i: (0, i))
    return pl.pallas_call(
        functools.partial(mix_kernel, T),
        grid=(PAIRS,),
        in_specs=[SMEM_SPEC, full((T, 64)), full((T, 64)),
                  pl.BlockSpec((1, 16, T), lambda i: (i, 0, 0)), blk, pl.BlockSpec((1, 128), lambda i: (0, i))],
        out_specs=blk,
        out_shape=jax.ShapeDtypeStruct((T, INNER), F32),
        scratch_shapes=[pltpu.VMEM((T, T), F32)],
        compiler_params=params(),
        name="mix",
    )(flag, b, c, rows, act, skip)


def gate_kernel(shard, flag, y, wrc, c, ct, st, normed, rest, tok, og, gain,
                no_o, bo_o, gg_o, gm_o, gn_o, dcs_o, dlr_o, dst_o, ggain_o, acc):
    step = pl.program_id(0)
    rb = y.shape[0]
    spread = (lax.div(iota((128, INNER), 1), 64) == iota((128, INNER), 0)).astype(BF)
    wide = nn(wrc[...], spread)
    seam = nn(c[...], st[...]) * wide
    mixed = y[...] + seam
    half = INNER // 2
    wl = rest[:, :shard, :].reshape(D, half)
    wr = rest[:, shard : 2 * shard, :].reshape(D, half)
    wo = rest[:, 2 * shard :, :].reshape(INNER, D)
    own = normed[...]
    gz = jnp.concatenate([nn(own, wl), nn(own, wr)], axis=1)
    sig = sigm(gz)
    sil = gz * sig
    gated = mixed * sil
    rho = lax.rsqrt(jnp.mean(gated * gated, axis=1, keepdims=True) + EPS)
    no = (gated * rho * gain[...]).astype(BF)
    no_o[...] = no
    bo_o[...] = (tok[...].astype(F32) + nn(no, wo)).astype(BF)
    gno = nt(og[...], wo)
    e = gno * gain[...]
    part = jnp.sum(gno * gated * rho, axis=0, keepdims=True)
    mean_eg = jnp.mean(e * gated, axis=1, keepdims=True)
    ggated = rho * e - gated * (rho * rho * rho * mean_eg)
    gg = (ggated * mixed * sig * (1.0 + gz * (1.0 - sig))).astype(BF)
    gg_o[...] = gg
    gm = (ggated * sil).astype(BF)
    gm_o[...] = gm
    gn_o[...] = nt(gg[:, :half], wl) + nt(gg[:, half:], wr)
    gm32 = gm.astype(F32)
    gw = (gm32 * wide).astype(BF)
    dcs_o[...] = nt(gw, st[...])
    shift = jnp.where(flag[0] == 0, HEADS, 0)
    gather = (lax.div(iota((INNER, 128), 0), 64) + shift == iota((INNER, 128), 1)).astype(BF)
    dlr_o[...] = nn((gm32 * seam).astype(BF), gather)
    dst = nn(ct[...], gw)

    @pl.when(step == 0)
    def _():
        acc[...] = dst
        ggain_o[...] = part

    @pl.when(step > 0)
    def _():
        acc[...] += dst
        ggain_o[...] += part

    dst_o[...] = acc[...].astype(BF)


def gate(flag, y, wrc, c, ct, st, normed, rest, tok, og, gain, rb=128):
    T = y.shape[0]
    row = lambda n: pl.BlockSpec((rb, n), lambda i: (i, 0))
    shapes = [((T, INNER), BF), ((T, D), BF), ((T, INNER), BF), ((T, INNER), BF), ((T, D), F32), ((T, 64), F32),
              ((T, 128), F32), ((64, INNER), BF), ((1, INNER), F32)]
    return pl.pallas_call(
        functools.partial(gate_kernel, rest.shape[1] // 4),
        grid=(T // rb,),
        in_specs=[SMEM_SPEC, row(INNER), row(128), row(64), pl.BlockSpec((64, rb), lambda i: (0, i)), full((64, INNER)),
                  row(D), full(rest.shape), row(D), row(D), full((1, INNER))],
        out_specs=[row(INNER), row(D), row(INNER), row(INNER), row(D), row(64), row(128), full((64, INNER)), full((1, INNER))],
        out_shape=[jax.ShapeDtypeStruct(s, d) for s, d in shapes],
        scratch_shapes=[pltpu.VMEM((64, INNER), F32)],
        compiler_params=params(),
        name="gate",
    )(flag, y, wrc, c, ct, st, normed, rest, tok, og, gain)


def unmix_kernel(T, flag, b, c, rows, x, g, dx_o, rsum_o, csum_o, dbc_o, sc, dsc):
    step = pl.program_id(0)
    Q = 128

    @pl.when(step == 0)
    def _():
        sc[...] = jnp.where(same_doc(flag, T), nt(b[...], c[...]), 0.0)
        dsc[...] = jnp.zeros((T, T), F32)
        csum_o[...] = jnp.zeros((T, 128), F32)
        rsum_o[...] = jnp.zeros((128, T), F32)

    r = rows[0]
    cols = r[0:8].T
    x2 = x[...]
    g2 = g[...]
    earlier = iota((Q, Q), 0) < iota((Q, Q), 1)
    lane = iota((Q, 128), 1)
    half = lane < 64
    base = 2 * step
    totals = [[None, None], [None, None]]
    for j in range(T // Q):
        lo, hi = j * Q, (j + 1) * Q
        outs = []
        xs = x2[lo:hi, :]
        stat = jnp.zeros((Q, 128), F32)
        for h in range(2):
            kf = cols[lo:hi, 4 + h : 5 + h]
            kr = cols[lo:hi, 6 + h : 7 + h]
            cf = r[h : h + 1]
            cr = r[2 + h : 3 + h]
            keep = half if h == 0 else ~half
            gt = nt(jnp.where(keep, xs, jnp.zeros_like(xs)), g2)
            parts = []
            if j > 0:
                parts.append(kr - cr[:, :lo])
            parts.append(jnp.where(earlier, cf[:, lo:hi] - kf, kr - cr[:, lo:hi]))
            if hi < T:
                parts.append(cf[:, hi:] - kf)
            d = jnp.exp2(jnp.concatenate(parts, axis=1))
            m = sc[lo:hi, :] * d
            outs.append(nn(m.astype(BF), g2))
            dsc[lo:hi, :] += gt * d
            w = gt * m
            wd = w[:, lo:hi]
            wdf = jnp.where(earlier, wd, 0.0)
            wf = [wdf] + ([w[:, hi:]] if hi < T else [])
            wr = ([w[:, :lo]] if j > 0 else []) + [wd - wdf]
            wf = jnp.concatenate([jnp.zeros((Q, lo), F32)] * (j > 0) + wf, axis=1)
            wr = jnp.concatenate(wr + [jnp.zeros((Q, T - hi), F32)] * (hi < T), axis=1)
            cfs = jnp.sum(wf, axis=1, keepdims=True)
            crs = jnp.sum(wr, axis=1, keepdims=True)
            stat = stat + jnp.where(lane == base + h, cfs, 0.0) + jnp.where(lane == HEADS + base + h, crs, 0.0)
            for q, part in ((0, wf), (1, wr)):
                s = jnp.sum(part, axis=0, keepdims=True)
                totals[q][h] = s if totals[q][h] is None else totals[q][h] + s
        dx_o[lo:hi, :] = jnp.where(half, outs[0], outs[1])
        csum_o[lo:hi, :] += stat
    for q in range(2):
        for h in range(2):
            rsum_o[pl.ds(HEADS * q + base + h, 1), :] = totals[q][h]

    @pl.when(step == PAIRS - 1)
    def _():
        ds = jnp.where(same_doc(flag, T), dsc[...], 0.0)
        dbc_o[:, 0:64] = nn(ds.astype(BF), c[...])
        dbc_o[:, 64:128] = nn(ds.T.astype(BF), b[...])


def unmix(flag, b, c, rows, act, g):
    T = b.shape[0]
    blk = pl.BlockSpec((T, 128), lambda i: (0, i))
    shapes = [((T, INNER), F32), ((128, T), F32), ((T, 128), F32), ((T, 128), F32)]
    return pl.pallas_call(
        functools.partial(unmix_kernel, T),
        grid=(PAIRS,),
        in_specs=[SMEM_SPEC, full((T, 64)), full((T, 64)),
                  pl.BlockSpec((1, 16, T), lambda i: (i, 0, 0)), blk, blk],
        out_specs=[blk, full((128, T)), full((T, 128)), full((T, 128))],
        out_shape=[jax.ShapeDtypeStruct(s, d) for s, d in shapes],
        scratch_shapes=[pltpu.VMEM((T, T), F32), pltpu.VMEM((T, T), F32)],
        compiler_params=params(),
        name="unmix",
    )(flag, b, c, rows, act, g)


def unproject_kernel(T, flag, dx, g, act, z, pre, w, cw, rows, dst, b, normed, nh, skip, bias, alog,
                     rsum, csum, dbc, dcs, dlr, gn_in, tok, halo, ggain,
                     dw_o, gn_o, gnh_o, small_o,
                     nt_s, ht_s, pre_s, shift_s, hd_s, dbs, dls, small, segc):
    step = pl.program_id(0)
    E = T + HALO

    @pl.when(step == 0)
    def _():
        segc[...] = doc_col(flag, T, HALO)
        small[...] = jnp.zeros((SMALL, CH), F32)
        nt_s[...] = normed[...].astype(F32).T.astype(BF)
        pad = jnp.concatenate([nh[...].astype(F32), jnp.zeros((128 - HALO, D), F32)], axis=0)
        ht_s[...] = pad.T.astype(BF)
        hd_s[...] = jnp.zeros((128, CH), BF)
        shift_s[...] = jnp.zeros((E + 8, CH), F32)
        gn_o[...] = gn_in[...]
        gnh_o[...] = jnp.zeros((HALO, D), F32)
        dbs[...] = jnp.zeros((T, 64), F32)
        dls[...] = jnp.zeros((T, 128), F32)

    def through_conv(dact):
        zz = z[...].astype(F32)
        sg = sigm(zz)
        dz = dact * sg * (1.0 + zz * (1.0 - sg))
        small[pl.ds(CONV * NCH + step, 1), :] = jnp.sum(dz, axis=0, keepdims=True)
        pre_s[...] = pre[...].astype(F32)
        here = segc[HALO:, :]
        total = jnp.zeros((E, CH), F32)
        for k in range(CONV):
            tap = slice(CONV - 1 - k, CONV - k)
            dk = dz if k == 0 else jnp.where(segc[HALO - k : E - k, :] == here, dz, 0.0)
            small[pl.ds(CONV * step + CONV - 1 - k, 1), :] = jnp.sum(dk * pre_s[HALO - k : E - k, :], axis=0, keepdims=True)
            shift_s[HALO:E, :] = dk
            total = total + cw[tap, :] * shift_s[k : E + k, :]
        return total

    def emit(local, halo):
        local = local.astype(BF)
        hd_s[0:HALO, :] = halo.astype(BF)
        dw_o[0] = (nn(nt_s[...], local) + nn(ht_s[...], hd_s[...])).astype(BF)
        gn_o[...] += nt(local, w[...])
        gnh_o[...] += nt(hd_s[0:HALO, :], w[...])

    @pl.when(step < NCH - 1)
    def _():
        wides = []
        for j in range(CH // 128):
            cols = rows[2 * step + j, 8:16, :].T
            wides.append(lane_pair(cols[:, 0:1], cols[:, 1:2], T))
        wide = jnp.concatenate(wides, axis=1)
        x32 = act[...].astype(F32)
        g32 = g[...].astype(F32)
        wq = wide * nn(b[...], dst[...])
        dbs[...] += nt((x32 * wide).astype(BF), dst[...])
        base = 4 * step + jnp.where(flag[0] == 0, 0, HEADS)
        sel = (lax.div(iota((CH, 128), 0), 64) + base == iota((CH, 128), 1)).astype(BF)
        dls[...] += nn((x32 * wq).astype(BF), sel)
        small[pl.ds((CONV + 1) * NCH + step, 1), :] = jnp.sum(g32 * x32, axis=0, keepdims=True)
        total = through_conv(dx[...] + wq + skip[...] * g32)
        emit(total[HALO:], total[:HALO])

    @pl.when(step == NCH - 1)
    def _():
        dact = dbc[...] + jnp.concatenate([dbs[...], dcs[...]], axis=1)
        total = through_conv(jnp.concatenate([dact, jnp.zeros((T, 128), F32)], axis=1))
        v = pre_s[HALO:, 128:] + bias[...]
        dt = jnp.maximum(v, 0.0) + jnp.log1p(jnp.exp(-jnp.abs(v)))
        sg = sigm(v)
        a = -jnp.exp(alog[...])
        ratio = jnp.where(v < -15.0, 1.0, sg / jnp.maximum(dt, 1e-30))
        isf = iota((T, 128), 1) < HEADS
        rs = rsum[...].T
        cs = csum[...]
        first = flag[0] == 0
        seam = dls[...] + dlr[...]
        dp = jnp.where(isf, rs - cs, cs - rs) + jnp.where(first, -1.0, 1.0) * seam
        tot = jnp.where(first, 1.0, 0.0) * jnp.sum(seam, axis=0, keepdims=True)
        after = (iota((T, T), 0) <= iota((T, T), 1)).astype(F32)
        inc = lax.dot_general(after, dp, (((1,), (0,)), ((), ())), precision=HI, preferred_element_type=F32)
        dl = jnp.where(isf, inc, inc - dp) + tot
        dv = dl * a * sg + (cs + dls[...]) * ratio
        emit(jnp.concatenate([total[HALO:, :128], dv], axis=1), total[:HALO])

        def unit(v):
            v = v.astype(F32)
            return v * lax.rsqrt(jnp.mean(v * v, axis=1, keepdims=True) + EPS)

        at = SMALL_AT
        small[at : at + 1, 0:128] = jnp.sum(dv, axis=0, keepdims=True)
        small[at : at + 1, 128:] = jnp.sum(dl * dt * a, axis=0, keepdims=True)
        for q in range(INNER // CH):
            small[at + 1 + q : at + 2 + q, :] = ggain[:, CH * q : CH * (q + 1)]
        part = jnp.sum(gn_o[...] * unit(tok[...]), axis=0, keepdims=True)
        part = part + jnp.sum(gnh_o[...] * unit(halo[...]), axis=0, keepdims=True)
        for q in range(D // CH):
            small[at + 7 + q : at + 8 + q, :] = part[:, CH * q : CH * (q + 1)]
        small_o[...] = small[...].astype(BF)


def unproject(flag, dx, g, act, z, pre, w1, conv_w, rows, dst, b, normed, nh, skip, bias, alog,
              rsum, csum, dbc, dcs, dlr, gn, tok, halo, ggain):
    T = dx.shape[0]
    E = T + HALO
    col = lambda rows: pl.BlockSpec((rows, CH), lambda i: (0, i))
    xcol = lambda rows: pl.BlockSpec((rows, CH), lambda i: (0, jnp.minimum(i, NCH - 2)))
    shapes = [((NCH, D, CH), BF), ((T, D), F32), ((HALO, D), F32), ((SMALL, CH), BF)]
    return pl.pallas_call(
        functools.partial(unproject_kernel, T),
        grid=(NCH,),
        in_specs=[SMEM_SPEC, xcol(T), xcol(T), xcol(T), col(T), col(E), col(D), col(CONV), full((PAIRS, 16, T)),
                  xcol(64), full((T, 64)), full((T, D)), full((HALO, D)), xcol(1), full((1, 128)), full((1, 128)),
                  full((128, T)), full((T, 128)), full((T, 128)), full((T, 64)), full((T, 128)), full((T, D)),
                  full((T, D)), full((HALO, D)), full((1, INNER))],
        out_specs=[pl.BlockSpec((1, D, CH), lambda i: (i, 0, 0)), full((T, D)), full((HALO, D)),
                   full((SMALL, CH))],
        out_shape=[jax.ShapeDtypeStruct(s, d) for s, d in shapes],
        scratch_shapes=[pltpu.VMEM((D, T), BF), pltpu.VMEM((D, 128), BF), pltpu.VMEM((E, CH), F32),
                        pltpu.VMEM((E + 8, CH), F32), pltpu.VMEM((128, CH), BF), pltpu.VMEM((T, 64), F32),
                        pltpu.VMEM((T, 128), F32), pltpu.VMEM((SMALL, CH), F32), pltpu.VMEM((E, 1), jnp.int32)],
        compiler_params=params(),
        name="unproject",
    )(flag, dx, g, act, z, pre, w1, conv_w, rows, dst, b, normed, nh, skip, bias, alog, rsum, csum, dbc, dcs, dlr, gn, tok, halo, ggain)


def flip(v, axis, bit):
    size = lax.axis_size(axis)
    return lax.ppermute(v, axis, [(i, i ^ (1 << bit)) for i in range(size)])


def bit_of(axis, bit):
    return lax.rem(lax.div(lax.axis_index(axis), 1 << bit), 2)


def width(axis):
    return lax.axis_size(axis).bit_length() - 1


def gather_rows(shard, ready, rest):
    out = shard
    done = 0
    for bit in reversed(range(width("dp"))):
        other = flip(out, "dp", bit)
        low = bit_of("dp", bit) == 0
        out = jnp.stack([jnp.where(low, out, other), jnp.where(low, other, out)], axis=done)
        done += 1
        if done == 1:
            out, ready = lax.optimization_barrier((out, ready))
        if done == 2:
            out, rest = lax.optimization_barrier((out, rest))
    return out.reshape((-1,) + shard.shape[1:]), ready, rest


def halves(v, mine):
    n = v.shape[0] // 2
    return lax.dynamic_slice_in_dim(v, mine * n, n), lax.dynamic_slice_in_dim(v, (1 - mine) * n, n)


def add(p, q):
    return (p.astype(F32) + q.astype(F32)).astype(BF)


def reduce_all(main, small):
    order = [("dir", 0)] + [("dp", bit) for bit in range(1, width("dp"))]
    order = [o for o in order if o[1] < width(o[0])]
    paired = width("dp") > 0
    if paired:
        mine = bit_of("dp", 0)
        (keep, send), (keep_s, send_s) = halves(main, mine), halves(small, mine)
        main, small = add(keep, flip(send, "dp", 0)), add(keep_s, flip(send_s, "dp", 0))
    rows = main.shape[0]
    buf = jnp.concatenate([main, small], axis=0)
    for axis, bit in order:
        keep, send = halves(buf, bit_of(axis, bit))
        buf = add(keep, flip(send, axis, bit))
    for axis, bit in reversed(order):
        got = flip(buf, axis, bit)
        low = bit_of(axis, bit) == 0
        buf = jnp.concatenate([jnp.where(low, buf, got), jnp.where(low, got, buf)], axis=0)
    if not paired:
        return buf[:rows], buf[rows:]
    got = flip(buf, "dp", 0)
    low = bit_of("dp", 0) == 0
    lo, hi = jnp.where(low, buf, got), jnp.where(low, got, buf)
    return jnp.concatenate([lo[:rows], hi[:rows]], axis=0), jnp.concatenate([lo[rows:], hi[rows:]], axis=0)


def assemble_kernel(wg, x, last, wo, small, zx_o, bc_o, dt_o, wo_o, cw_o):
    step = pl.program_id(0)
    wo_o[...] = wo[...].astype(F32)

    @pl.when(step < INNER // CH)
    def _():
        zx_o[...] = wg[...].astype(F32)

    @pl.when(step >= INNER // CH)
    def _():
        zx_o[...] = x[0].astype(F32)

    @pl.when(step == 0)
    def _():
        tail = last[0].astype(F32)
        bc_o[...] = tail[:, :128]
        dt_o[...] = tail[:, 128 : 128 + 2 * HEADS]
        sm = small[...].astype(F32)
        for q in range(NCH - 1):
            cw_o[:, CH * q : CH * (q + 1)] = sm[CONV * q : CONV * (q + 1), :]
        cw_o[:, INNER:] = sm[CONV * (NCH - 1) : CONV * NCH, :128]


def assemble(wg, main, wo, small):
    n = INNER // CH
    taps = INNER + 2 * STATE
    rb = INNER // (2 * n)
    shapes = [(D, 2 * INNER), (D, 2 * STATE), (D, 2 * HEADS), (INNER, D), (CONV, taps)]
    return pl.pallas_call(
        assemble_kernel,
        grid=(2 * n,),
        in_specs=[pl.BlockSpec((D, CH), lambda i: (0, jnp.minimum(i, n - 1))),
                  pl.BlockSpec((1, D, CH), lambda i: (jnp.maximum(i - n, 0), 0, 0)),
                  pl.BlockSpec((1, D, CH), lambda i: (NCH - 1, 0, 0)),
                  pl.BlockSpec((rb, D), lambda i: (i, 0)), full(small.shape)],
        out_specs=[pl.BlockSpec((D, CH), lambda i: (0, i)), full(shapes[1]), full(shapes[2]),
                   pl.BlockSpec((rb, D), lambda i: (i, 0)), full(shapes[4])],
        out_shape=[jax.ShapeDtypeStruct(s, F32) for s in shapes],
        compiler_params=params(),
        name="assemble",
    )(wg, main, main, wo, small)


def body(tokens, norm_gain, w_zx, w_bc, w_dt, conv_w, conv_b, dt_bias, a_log, d_skip, out_gain, w_out, doc_lengths, out_grad):
    T = tokens.shape[1]
    devices = lax.axis_size("dir") * lax.axis_size("dp")
    side = lax.axis_index("dir")
    swap = lambda v: flip(v, "dir", 0)
    tok = tokens.reshape(T, D)
    og = out_grad.reshape(T, D)
    shard = w_zx.shape[0]
    half = INNER // 2
    mine = jnp.concatenate([w_zx[:, INNER:], w_bc, w_dt, jnp.zeros((shard, 128 - 2 * HEADS), BF)], axis=1)
    rest = jnp.concatenate([w_zx[:, :half], w_zx[:, half:INNER], w_out], axis=0)
    halo = lax.ppermute(tok[T - HALO :], "dir", [(0, 1)])
    flag = jnp.concatenate([side[None].astype(jnp.int32), doc_lengths[0]])
    wide = NCH * CH
    cw = jnp.pad(conv_w, ((0, 0), (0, wide - conv_w.shape[1])))
    cb = jnp.pad(conv_b, (0, wide - conv_b.shape[0]))[None]
    lanes = lambda v: jnp.pad(v, (0, 128 - v.shape[0]))[None]
    skip = jnp.repeat(d_skip, HEADDIM)[None]
    ready = (halo, flag, cw, cb, lanes(dt_bias), lanes(a_log), skip, norm_gain[None], out_gain[None])
    w1, ready, rest = gather_rows(mine, ready, rest)
    halo, flag, cw, cb, bias, alog, skip, gain_in, gain_out = ready
    rest = lax.all_gather(rest, "dp", axis=0, tiled=False)
    if shard % 16:
        rest = jnp.concatenate([rest[:, :shard].reshape(D, D), rest[:, shard : 2 * shard].reshape(D, D),
                                rest[:, 2 * shard :].reshape(INNER, D)], axis=0)[None]
    normed, nh, pre, z, act, rows, wrc, b, bt, c, ct, st = project(flag, tok, halo, gain_in, w1, cw, cb, bias, alog)
    st_in = swap(st)
    y = mix(flag, b, c, rows, act, skip)
    no, bo, gg, gm, gn, dcs, dlr, dst, ggain = gate(flag, y, wrc, c, ct, st_in, normed, rest, tok, og, gain_out)
    tn = lambda p, q: lax.dot_general(p, q, (((0,), (0,)), ((), ())), preferred_element_type=F32).astype(BF)
    dwo, dwg = tn(no, og), tn(normed, gg)
    dwo, dwg, gm = lax.optimization_barrier((dwo, dwg, gm))
    dwo, dwg = lax.psum((dwo, dwg), ("dir", "dp"))
    def finish(v):
        (flag, b, c, rows, act, gm, z, pre, w1, cw, dst, normed, nh, skip, bias, alog, dcs, dlr, gn, tok, halo, ggain, og, gain_in) = v
        dst_in = swap(dst)
        dx, rsum, csum, dbc = unmix(flag, b, c, rows, act, gm)
        dw1, gn, gnh, small = unproject(flag, dx, gm, act, z, pre, w1, cw, rows, dst_in, b, normed, nh, skip, bias, alog,
                                        rsum, csum, dbc, dcs, dlr, gn, tok, halo, ggain)
        back = lax.ppermute(gnh, "dir", [(1, 0)])
        main = dw1.reshape(NCH * D, CH)
        total = -(-(main.shape[0] + SMALL) // (16 * devices)) * 16 * devices
        small = jnp.pad(small, ((0, total - main.shape[0] - SMALL), (0, 0)))
        main, small = reduce_all(main, small)
        gn = gn + jnp.pad(back, ((T - HALO, 0), (0, 0)))
        x32 = tok.astype(F32)
        rho = lax.rsqrt(jnp.mean(x32 * x32, axis=1, keepdims=True) + EPS)
        e_in = gn * gain_in
        gx = rho * e_in - x32 * (rho * rho * rho * jnp.mean(e_in * x32, axis=1, keepdims=True))
        grad_tokens = (og.astype(F32) + gx).astype(BF)
        return main, small, grad_tokens

    def nothing(v):
        return tuple(jnp.zeros(o.shape, o.dtype) for o in jax.eval_shape(finish, v))

    args = (flag, b, c, rows, act, gm, z, pre, w1, cw, dst, normed, nh, skip, bias, alog, dcs, dlr, gn, tok, halo, ggain, og, gain_in)
    main, small, grad_tokens = lax.cond(flag[1] >= 0, finish, nothing, args)
    gw_zx, gw_bc, gw_dt, gw_out, g_cw = assemble(dwg, main.reshape(NCH, D, CH), dwo, small)
    small = small.astype(F32)
    g_cb = small[CONV * NCH : (CONV + 1) * NCH].reshape(wide)[: INNER + 2 * STATE]
    g_skip = jnp.sum(small[(CONV + 1) * NCH : SMALL_AT].reshape(HEADS, HEADDIM), axis=1)
    g_bias = small[SMALL_AT, : 2 * HEADS]
    g_alog = small[SMALL_AT, 128 : 128 + 2 * HEADS]
    g_out = small[SMALL_AT + 1 : SMALL_AT + 7].reshape(INNER)
    g_in = small[SMALL_AT + 7 : SMALL_AT + 10].reshape(D)
    return (bo.reshape(tokens.shape), grad_tokens.reshape(tokens.shape), g_in, gw_zx, gw_bc, gw_dt, g_cw, g_cb, g_bias,
            g_alog, g_skip, g_out, gw_out)


def solution(mesh):
    rows, weight, whole = P("dp", "dir", None), P("dp", None), P()
    placed = (rows, whole, weight, weight, weight, whole, whole, whole, whole, whole, whole, weight, weight, rows)
    return jax.shard_map(body, mesh=mesh, in_specs=placed, out_specs=(rows, rows) + (whole,) * 11, check_vma=False)
```

```python
import functools

import jax
import jax.numpy as jnp
from jax import lax
from jax.experimental import pallas as pl
from jax.experimental.pallas import tpu as pltpu
from jax.sharding import PartitionSpec as P

D = 768
HEADS = 24
HEADDIM = 64
STATE = 64
INNER = 1536
CONV = 4
NDOC = 4
PAIRS = HEADS // 2
HALO = 16
CH = 256
NCH = 7
SMALL_AT = (CONV + 1) * NCH
SMALL = 64
EPS = 1e-05
LOG2E = 1.4426950408889634
BF = jnp.bfloat16
F32 = jnp.float32
HI = lax.Precision.HIGHEST


def nn(a, b):
    return lax.dot_general(a, b, (((1,), (0,)), ((), ())), preferred_element_type=F32)


def nt(a, b):
    return lax.dot_general(a, b, (((1,), (1,)), ((), ())), preferred_element_type=F32)


def iota(shape, axis):
    return lax.broadcasted_iota(jnp.int32, shape, axis)


def sigm(v):
    return 1.0 / (1.0 + jnp.exp(-v))


def lane_pair(col_a, col_b, rows):
    return jnp.where(iota((rows, 128), 1) < 64, col_a, col_b)


def params(mib=60):
    return pltpu.CompilerParams(
        dimension_semantics=("arbitrary",), vmem_limit_bytes=mib * 1024 * 1024
    )


def full(shape):
    return pl.BlockSpec(shape, lambda i: tuple(0 for _ in shape))


SMEM_SPEC = pl.BlockSpec(memory_space=pltpu.SMEM)


def doc_ids(flag, places):
    total = jnp.zeros(places.shape, jnp.int32)
    end = 0
    for k in range(NDOC):
        end = end + flag[1 + k]
        total = total + jnp.where(places >= end, 1, 0)
    return jnp.where(places < 0, -1, total)


def doc_at(flag, place):
    total = 0
    end = 0
    for k in range(NDOC):
        end = end + flag[1 + k]
        total = total + jnp.where(place >= end, 1, 0)
    return total


def doc_col(flag, T, lead=0):
    return doc_ids(flag, iota((T + lead, 1), 0) + (flag[0] * T - lead))


def doc_row(flag, T):
    return doc_ids(flag, iota((1, T), 1) + flag[0] * T)


def project_kernel(T, flag, tok, halo, gain, w, cw, cb, bias, alog,
                   norm_o, nh_o, pre_o, z_o, act_o, rows_o, wrc_o, b_o, bt_o, c_o, ct_o, st_o, ncat, pf, segc):
    step = pl.program_id(0)

    @pl.when(step == 0)
    def _():
        def norm(v):
            v = v.astype(F32)
            ms = jnp.mean(v * v, axis=1, keepdims=True)
            return (v * lax.rsqrt(ms + EPS) * gain[...]).astype(BF)

        nh = norm(halo[...])
        own = norm(tok[...])
        nh_o[...] = nh
        norm_o[...] = own
        ncat[0:HALO, :] = nh
        ncat[HALO:, :] = own
        segc[...] = doc_col(flag, T, HALO)

    proj = nn(ncat[...], w[...]).astype(BF)
    pre_o[...] = proj
    pf[...] = proj.astype(F32)
    segs = segc[...]
    here = segs[HALO:, :]
    z = cb[...] + cw[CONV - 1 : CONV, :] * pf[HALO:, :]
    for k in range(1, CONV):
        same = segs[HALO - k : HALO + T - k, :] == here
        z = z + jnp.where(same, cw[CONV - 1 - k : CONV - k, :] * pf[HALO - k : HALO + T - k, :], 0.0)
    z_o[...] = z.astype(BF)
    act = z * sigm(z)
    act_o[...] = act.astype(BF)

    @pl.when(step == 0)
    def _():
        bc = act[:, :128]
        b_o[...] = bc[:, :64].astype(BF)
        c_o[...] = bc[:, 64:].astype(BF)
        bct = bc.T
        bt_o[...] = bct[:64, :].astype(BF)
        ct_o[...] = bct[64:, :].astype(BF)
        v = pf[HALO:, 128:] + bias[...]
        dt = jnp.maximum(v, 0.0) + jnp.log1p(jnp.exp(-jnp.abs(v)))
        rate = dt * (-LOG2E * jnp.exp(alog[...]))
        rate_t = rate.T
        dt_t = dt.T
        upto = (iota((T, T), 0) <= iota((T, T), 1)).astype(F32)
        inc = lax.dot_general(rate_t, upto, (((1,), (0,)), ((), ())), precision=HI, preferred_element_type=F32)
        isf = iota((128, T), 0) < HEADS
        cum = jnp.where(isf, inc, inc - rate_t)
        ldt = jnp.log2(jnp.maximum(dt_t, 1e-37))
        key = jnp.where(isf, cum - ldt, cum + ldt)
        segv = doc_row(flag, T)
        left, right = doc_at(flag, T - 1), doc_at(flag, T)
        send_f = jnp.where(segv == left, jnp.exp2(cum[:, T - 1 :] - key), 0.0)
        send_b = jnp.where(segv == right, jnp.exp2(key), 0.0)
        recv_f = jnp.where(segv == left, jnp.exp2(cum), 0.0)
        recv_b = jnp.where(segv == right, jnp.exp2(inc[:, T - 1 :] - cum), 0.0)
        first = flag[0] == 0
        send = jnp.where(first, send_f[0:HEADS], send_b[HEADS : 2 * HEADS])
        recv = jnp.where(first, recv_b[HEADS : 2 * HEADS], recv_f[0:HEADS])
        for p in range(PAIRS):
            f, r = 2 * p, HEADS + 2 * p
            rows_o[p, 0:2, :] = cum[f : f + 2]
            rows_o[p, 2:4, :] = cum[r : r + 2]
            rows_o[p, 4:6, :] = key[f : f + 2]
            rows_o[p, 6:8, :] = key[r : r + 2]
            rows_o[p, 8:10, :] = send[f : f + 2]
            rows_o[p, 10:12, :] = recv[f : f + 2]
            rows_o[p, 12:16, :] = jnp.zeros((4, T), F32)
        recv_pad = jnp.concatenate([recv, jnp.zeros((128 - HEADS, T), F32)], axis=0)
        wrc_o[...] = recv_pad.T.astype(BF)

    @pl.when(step > 0)
    def _():
        for j in range(CH // 128):
            cols = rows_o[2 * (step - 1) + j, 8:16, :].T
            wide = lane_pair(cols[:, 0:1], cols[:, 1:2], T)
            xw = (act[:, 128 * j : 128 * (j + 1)] * wide).astype(BF)
            st_o[:, 128 * j : 128 * (j + 1)] = nn(bt_o[...], xw).astype(BF)


def project(flag, tok, halo, gain, w1, conv_w, conv_b, bias, alog):
    T = tok.shape[0]
    E = T + HALO
    chunk = lambda i: lax.rem(i + NCH - 1, NCH)
    xchunk = lambda i: jnp.maximum(i - 1, 0)
    col = lambda rows: pl.BlockSpec((rows, CH), lambda i: (0, chunk(i)))
    shapes = [
        ((T, D), BF), ((HALO, D), BF), ((E, NCH * CH), BF), ((T, NCH * CH), BF), ((T, NCH * CH), BF),
        ((PAIRS, 16, T), F32), ((T, 128), BF), ((T, 64), BF), ((64, T), BF), ((T, 64), BF), ((64, T), BF),
        ((64, INNER), BF),
    ]
    out_specs = [
        full((T, D)), full((HALO, D)), col(E), col(T), col(T), full((PAIRS, 16, T)), full((T, 128)), full((T, 64)),
        full((64, T)), full((T, 64)), full((64, T)), pl.BlockSpec((64, CH), lambda i: (0, xchunk(i))),
    ]
    return pl.pallas_call(
        functools.partial(project_kernel, T),
        grid=(NCH,),
        in_specs=[SMEM_SPEC, full((T, D)), full((HALO, D)), full((1, D)), col(D), col(CONV), col(1),
                  full((1, 128)), full((1, 128))],
        out_specs=out_specs,
        out_shape=[jax.ShapeDtypeStruct(s, d) for s, d in shapes],
        scratch_shapes=[pltpu.VMEM((E, D), BF), pltpu.VMEM((E, CH), F32), pltpu.VMEM((E, 1), jnp.int32)],
        compiler_params=params(),
        name="project",
    )(flag, tok, halo, gain, w1, conv_w, conv_b, bias, alog)


def same_doc(flag, T):
    return (doc_col(flag, T) == doc_row(flag, T)) & (iota((T, T), 0) != iota((T, T), 1))


def mix_kernel(T, flag, b, c, rows, x, skip, y_o, sc):
    Q = 128

    @pl.when(pl.program_id(0) == 0)
    def _():
        s = nt(c[...], b[...])
        sc[...] = jnp.where(same_doc(flag, T), s, 0.0)

    r = rows[0]
    cols = r[0:8].T
    x2 = x[...]
    later = iota((Q, Q), 0) > iota((Q, Q), 1)
    lane = iota((Q, 128), 1) < 64
    for i in range(T // Q):
        lo, hi = i * Q, (i + 1) * Q
        outs = []
        for h in range(2):
            cf = cols[lo:hi, h : h + 1]
            cr = cols[lo:hi, 2 + h : 3 + h]
            kf = r[4 + h : 5 + h]
            kr = r[6 + h : 7 + h]
            parts = []
            if i > 0:
                parts.append(cf - kf[:, :lo])
            parts.append(jnp.where(later, cf - kf[:, lo:hi], kr[:, lo:hi] - cr))
            if hi < T:
                parts.append(kr[:, hi:] - cr)
            e = jnp.concatenate(parts, axis=1)
            m = (sc[lo:hi, :] * jnp.exp2(e)).astype(BF)
            outs.append(nn(m, x2))
        y_o[lo:hi, :] = jnp.where(lane, outs[0], outs[1]) + skip[...] * x2[lo:hi, :].astype(F32)


def mix(flag, b, c, rows, act, skip):
    T = b.shape[0]
    blk = pl.BlockSpec((T, 128), lambda i: (0, i))
    return pl.pallas_call(
        functools.partial(mix_kernel, T),
        grid=(PAIRS,),
        in_specs=[SMEM_SPEC, full((T, 64)), full((T, 64)),
                  pl.BlockSpec((1, 16, T), lambda i: (i, 0, 0)), blk, pl.BlockSpec((1, 128), lambda i: (0, i))],
        out_specs=blk,
        out_shape=jax.ShapeDtypeStruct((T, INNER), F32),
        scratch_shapes=[pltpu.VMEM((T, T), F32)],
        compiler_params=params(),
        name="mix",
    )(flag, b, c, rows, act, skip)


def gate_kernel(shard, flag, y, wrc, c, ct, st, normed, rest, tok, og, gain,
                no_o, bo_o, gg_o, gm_o, gn_o, dcs_o, dlr_o, dst_o, ggain_o, acc):
    step = pl.program_id(0)
    rb = y.shape[0]
    spread = (lax.div(iota((128, INNER), 1), 64) == iota((128, INNER), 0)).astype(BF)
    wide = nn(wrc[...], spread)
    seam = nn(c[...], st[...]) * wide
    mixed = y[...] + seam
    half = INNER // 2
    wl = rest[:, :shard, :].reshape(D, half)
    wr = rest[:, shard : 2 * shard, :].reshape(D, half)
    wo = rest[:, 2 * shard :, :].reshape(INNER, D)
    own = normed[...]
    gz = jnp.concatenate([nn(own, wl), nn(own, wr)], axis=1)
    sig = sigm(gz)
    sil = gz * sig
    gated = mixed * sil
    rho = lax.rsqrt(jnp.mean(gated * gated, axis=1, keepdims=True) + EPS)
    no = (gated * rho * gain[...]).astype(BF)
    no_o[...] = no
    bo_o[...] = (tok[...].astype(F32) + nn(no, wo)).astype(BF)
    gno = nt(og[...], wo)
    e = gno * gain[...]
    part = jnp.sum(gno * gated * rho, axis=0, keepdims=True)
    mean_eg = jnp.mean(e * gated, axis=1, keepdims=True)
    ggated = rho * e - gated * (rho * rho * rho * mean_eg)
    gg = (ggated * mixed * sig * (1.0 + gz * (1.0 - sig))).astype(BF)
    gg_o[...] = gg
    gm = (ggated * sil).astype(BF)
    gm_o[...] = gm
    gn_o[...] = nt(gg[:, :half], wl) + nt(gg[:, half:], wr)
    gm32 = gm.astype(F32)
    gw = (gm32 * wide).astype(BF)
    dcs_o[...] = nt(gw, st[...])
    shift = jnp.where(flag[0] == 0, HEADS, 0)
    gather = (lax.div(iota((INNER, 128), 0), 64) + shift == iota((INNER, 128), 1)).astype(BF)
    dlr_o[...] = nn((gm32 * seam).astype(BF), gather)
    dst = nn(ct[...], gw)

    @pl.when(step == 0)
    def _():
        acc[...] = dst
        ggain_o[...] = part

    @pl.when(step > 0)
    def _():
        acc[...] += dst
        ggain_o[...] += part

    dst_o[...] = acc[...].astype(BF)


def gate(flag, y, wrc, c, ct, st, normed, rest, tok, og, gain, rb=256):
    T = y.shape[0]
    row = lambda n: pl.BlockSpec((rb, n), lambda i: (i, 0))
    shapes = [((T, INNER), BF), ((T, D), BF), ((T, INNER), BF), ((T, INNER), BF), ((T, D), F32), ((T, 64), F32),
              ((T, 128), F32), ((64, INNER), BF), ((1, INNER), F32)]
    return pl.pallas_call(
        functools.partial(gate_kernel, rest.shape[1] // 4),
        grid=(T // rb,),
        in_specs=[SMEM_SPEC, row(INNER), row(128), row(64), pl.BlockSpec((64, rb), lambda i: (0, i)), full((64, INNER)),
                  row(D), full(rest.shape), row(D), row(D), full((1, INNER))],
        out_specs=[row(INNER), row(D), row(INNER), row(INNER), row(D), row(64), row(128), full((64, INNER)), full((1, INNER))],
        out_shape=[jax.ShapeDtypeStruct(s, d) for s, d in shapes],
        scratch_shapes=[pltpu.VMEM((64, INNER), F32)],
        compiler_params=params(),
        name="gate",
    )(flag, y, wrc, c, ct, st, normed, rest, tok, og, gain)


def unmix_kernel(T, flag, b, c, rows, x, g, dx_o, rsum_o, csum_o, dbc_o, sc, dsc):
    step = pl.program_id(0)
    Q = 128

    @pl.when(step == 0)
    def _():
        sc[...] = jnp.where(same_doc(flag, T), nt(b[...], c[...]), 0.0)
        dsc[...] = jnp.zeros((T, T), F32)
        csum_o[...] = jnp.zeros((T, 128), F32)
        rsum_o[...] = jnp.zeros((128, T), F32)

    r = rows[0]
    cols = r[0:8].T
    x2 = x[...]
    g2 = g[...]
    earlier = iota((Q, Q), 0) < iota((Q, Q), 1)
    lane = iota((Q, 128), 1)
    half = lane < 64
    base = 2 * step
    totals = [[None, None], [None, None]]
    for j in range(T // Q):
        lo, hi = j * Q, (j + 1) * Q
        outs = []
        xs = x2[lo:hi, :]
        stat = jnp.zeros((Q, 128), F32)
        for h in range(2):
            kf = cols[lo:hi, 4 + h : 5 + h]
            kr = cols[lo:hi, 6 + h : 7 + h]
            cf = r[h : h + 1]
            cr = r[2 + h : 3 + h]
            keep = half if h == 0 else ~half
            gt = nt(jnp.where(keep, xs, jnp.zeros_like(xs)), g2)
            parts = []
            if j > 0:
                parts.append(kr - cr[:, :lo])
            parts.append(jnp.where(earlier, cf[:, lo:hi] - kf, kr - cr[:, lo:hi]))
            if hi < T:
                parts.append(cf[:, hi:] - kf)
            d = jnp.exp2(jnp.concatenate(parts, axis=1))
            m = sc[lo:hi, :] * d
            outs.append(nn(m.astype(BF), g2))
            dsc[lo:hi, :] += gt * d
            w = gt * m
            wd = w[:, lo:hi]
            wdf = jnp.where(earlier, wd, 0.0)
            wf = [wdf] + ([w[:, hi:]] if hi < T else [])
            wr = ([w[:, :lo]] if j > 0 else []) + [wd - wdf]
            wf = jnp.concatenate([jnp.zeros((Q, lo), F32)] * (j > 0) + wf, axis=1)
            wr = jnp.concatenate(wr + [jnp.zeros((Q, T - hi), F32)] * (hi < T), axis=1)
            cfs = jnp.sum(wf, axis=1, keepdims=True)
            crs = jnp.sum(wr, axis=1, keepdims=True)
            stat = stat + jnp.where(lane == base + h, cfs, 0.0) + jnp.where(lane == HEADS + base + h, crs, 0.0)
            for q, part in ((0, wf), (1, wr)):
                s = jnp.sum(part, axis=0, keepdims=True)
                totals[q][h] = s if totals[q][h] is None else totals[q][h] + s
        dx_o[lo:hi, :] = jnp.where(half, outs[0], outs[1])
        csum_o[lo:hi, :] += stat
    for q in range(2):
        for h in range(2):
            rsum_o[pl.ds(HEADS * q + base + h, 1), :] = totals[q][h]

    @pl.when(step == PAIRS - 1)
    def _():
        ds = jnp.where(same_doc(flag, T), dsc[...], 0.0)
        dbc_o[:, 0:64] = nn(ds.astype(BF), c[...])
        dbc_o[:, 64:128] = nn(ds.T.astype(BF), b[...])


def unmix(flag, b, c, rows, act, g):
    T = b.shape[0]
    blk = pl.BlockSpec((T, 128), lambda i: (0, i))
    shapes = [((T, INNER), F32), ((128, T), F32), ((T, 128), F32), ((T, 128), F32)]
    return pl.pallas_call(
        functools.partial(unmix_kernel, T),
        grid=(PAIRS,),
        in_specs=[SMEM_SPEC, full((T, 64)), full((T, 64)),
                  pl.BlockSpec((1, 16, T), lambda i: (i, 0, 0)), blk, blk],
        out_specs=[blk, full((128, T)), full((T, 128)), full((T, 128))],
        out_shape=[jax.ShapeDtypeStruct(s, d) for s, d in shapes],
        scratch_shapes=[pltpu.VMEM((T, T), F32), pltpu.VMEM((T, T), F32)],
        compiler_params=params(),
        name="unmix",
    )(flag, b, c, rows, act, g)


def unproject_kernel(T, flag, dx, g, act, z, pre, w, cw, rows, dst, b, normed, nh, skip, bias, alog,
                     rsum, csum, dbc, dcs, dlr, gn_in, tok, halo, ggain,
                     dw_o, gn_o, gnh_o, small_o,
                     nt_s, ht_s, pre_s, shift_s, hd_s, dbs, dls, small, segc):
    step = pl.program_id(0)
    E = T + HALO

    @pl.when(step == 0)
    def _():
        segc[...] = doc_col(flag, T, HALO)
        small[...] = jnp.zeros((SMALL, CH), F32)
        nt_s[...] = normed[...].astype(F32).T.astype(BF)
        pad = jnp.concatenate([nh[...].astype(F32), jnp.zeros((128 - HALO, D), F32)], axis=0)
        ht_s[...] = pad.T.astype(BF)
        hd_s[...] = jnp.zeros((128, CH), BF)
        shift_s[...] = jnp.zeros((E + 8, CH), F32)
        gn_o[...] = gn_in[...]
        gnh_o[...] = jnp.zeros((HALO, D), F32)
        dbs[...] = jnp.zeros((T, 64), F32)
        dls[...] = jnp.zeros((T, 128), F32)

    def through_conv(dact):
        zz = z[...].astype(F32)
        sg = sigm(zz)
        dz = dact * sg * (1.0 + zz * (1.0 - sg))
        small[pl.ds(CONV * NCH + step, 1), :] = jnp.sum(dz, axis=0, keepdims=True)
        pre_s[...] = pre[...].astype(F32)
        here = segc[HALO:, :]
        total = jnp.zeros((E, CH), F32)
        for k in range(CONV):
            tap = slice(CONV - 1 - k, CONV - k)
            dk = dz if k == 0 else jnp.where(segc[HALO - k : E - k, :] == here, dz, 0.0)
            small[pl.ds(CONV * step + CONV - 1 - k, 1), :] = jnp.sum(dk * pre_s[HALO - k : E - k, :], axis=0, keepdims=True)
            shift_s[HALO:E, :] = dk
            total = total + cw[tap, :] * shift_s[k : E + k, :]
        return total

    def emit(local, halo):
        local = local.astype(BF)
        hd_s[0:HALO, :] = halo.astype(BF)
        dw_o[0] = (nn(nt_s[...], local) + nn(ht_s[...], hd_s[...])).astype(BF)
        gn_o[...] += nt(local, w[...])
        gnh_o[...] += nt(hd_s[0:HALO, :], w[...])

    @pl.when(step < NCH - 1)
    def _():
        wides = []
        for j in range(CH // 128):
            cols = rows[2 * step + j, 8:16, :].T
            wides.append(lane_pair(cols[:, 0:1], cols[:, 1:2], T))
        wide = jnp.concatenate(wides, axis=1)
        x32 = act[...].astype(F32)
        g32 = g[...].astype(F32)
        wq = wide * nn(b[...], dst[...])
        dbs[...] += nt((x32 * wide).astype(BF), dst[...])
        base = 4 * step + jnp.where(flag[0] == 0, 0, HEADS)
        sel = (lax.div(iota((CH, 128), 0), 64) + base == iota((CH, 128), 1)).astype(BF)
        dls[...] += nn((x32 * wq).astype(BF), sel)
        heads = (lax.div(iota((CH, 128), 0), 64) + 4 * step == iota((CH, 128), 1)).astype(F32)
        both = jnp.broadcast_to(jnp.sum(g32 * x32, axis=0, keepdims=True), (8, CH))
        both = lax.dot_general(both, heads, (((1,), (0,)), ((), ())), precision=HI, preferred_element_type=F32)
        small[SMALL_AT + 10 : SMALL_AT + 11, 0:128] += both[0:1, :]
        total = through_conv(dx[...] + wq + skip[...] * g32)
        emit(total[HALO:], total[:HALO])

    @pl.when(step == NCH - 1)
    def _():
        dact = dbc[...] + jnp.concatenate([dbs[...], dcs[...]], axis=1)
        total = through_conv(jnp.concatenate([dact, jnp.zeros((T, 128), F32)], axis=1))
        v = pre_s[HALO:, 128:] + bias[...]
        dt = jnp.maximum(v, 0.0) + jnp.log1p(jnp.exp(-jnp.abs(v)))
        sg = sigm(v)
        a = -jnp.exp(alog[...])
        ratio = jnp.where(v < -15.0, 1.0, sg / jnp.maximum(dt, 1e-30))
        isf = iota((T, 128), 1) < HEADS
        rs = rsum[...].T
        cs = csum[...]
        first = flag[0] == 0
        seam = dls[...] + dlr[...]
        dp = jnp.where(isf, rs - cs, cs - rs) + jnp.where(first, -1.0, 1.0) * seam
        tot = jnp.where(first, 1.0, 0.0) * jnp.sum(seam, axis=0, keepdims=True)
        after = (iota((T, T), 0) <= iota((T, T), 1)).astype(F32)
        inc = lax.dot_general(after, dp, (((1,), (0,)), ((), ())), precision=HI, preferred_element_type=F32)
        dl = jnp.where(isf, inc, inc - dp) + tot
        dv = dl * a * sg + (cs + dls[...]) * ratio
        emit(jnp.concatenate([total[HALO:, :128], dv], axis=1), total[:HALO])

        def unit(v):
            v = v.astype(F32)
            return v * lax.rsqrt(jnp.mean(v * v, axis=1, keepdims=True) + EPS)

        at = SMALL_AT
        small[at : at + 1, 0:128] = jnp.sum(dv, axis=0, keepdims=True)
        small[at : at + 1, 128:] = jnp.sum(dl * dt * a, axis=0, keepdims=True)
        for q in range(INNER // CH):
            small[at + 1 + q : at + 2 + q, :] = ggain[:, CH * q : CH * (q + 1)]
        part = jnp.sum(gn_o[...] * unit(tok[...]), axis=0, keepdims=True)
        part = part + jnp.sum(gnh_o[...] * unit(halo[...]), axis=0, keepdims=True)
        for q in range(D // CH):
            small[at + 7 + q : at + 8 + q, :] = part[:, CH * q : CH * (q + 1)]
        small_o[...] = small[...].astype(BF)


def unproject(flag, dx, g, act, z, pre, w1, conv_w, rows, dst, b, normed, nh, skip, bias, alog,
              rsum, csum, dbc, dcs, dlr, gn, tok, halo, ggain):
    T = dx.shape[0]
    E = T + HALO
    col = lambda rows: pl.BlockSpec((rows, CH), lambda i: (0, i))
    xcol = lambda rows: pl.BlockSpec((rows, CH), lambda i: (0, jnp.minimum(i, NCH - 2)))
    shapes = [((NCH, D, CH), BF), ((T, D), F32), ((HALO, D), F32), ((SMALL, CH), BF)]
    return pl.pallas_call(
        functools.partial(unproject_kernel, T),
        grid=(NCH,),
        in_specs=[SMEM_SPEC, xcol(T), xcol(T), xcol(T), col(T), col(E), col(D), col(CONV), full((PAIRS, 16, T)),
                  xcol(64), full((T, 64)), full((T, D)), full((HALO, D)), xcol(1), full((1, 128)), full((1, 128)),
                  full((128, T)), full((T, 128)), full((T, 128)), full((T, 64)), full((T, 128)), full((T, D)),
                  full((T, D)), full((HALO, D)), full((1, INNER))],
        out_specs=[pl.BlockSpec((1, D, CH), lambda i: (i, 0, 0)), full((T, D)), full((HALO, D)),
                   full((SMALL, CH))],
        out_shape=[jax.ShapeDtypeStruct(s, d) for s, d in shapes],
        scratch_shapes=[pltpu.VMEM((D, T), BF), pltpu.VMEM((D, 128), BF), pltpu.VMEM((E, CH), F32),
                        pltpu.VMEM((E + 8, CH), F32), pltpu.VMEM((128, CH), BF), pltpu.VMEM((T, 64), F32),
                        pltpu.VMEM((T, 128), F32), pltpu.VMEM((SMALL, CH), F32), pltpu.VMEM((E, 1), jnp.int32)],
        compiler_params=params(),
        name="unproject",
    )(flag, dx, g, act, z, pre, w1, conv_w, rows, dst, b, normed, nh, skip, bias, alog, rsum, csum, dbc, dcs, dlr, gn, tok, halo, ggain)


BOTH = ("dir", "dp")


def width(axis):
    return lax.axis_size(axis).bit_length() - 1


def exchange(v, mask_even, mask_odd):
    size = lax.axis_size("dir") * lax.axis_size("dp")
    return lax.ppermute(v, BOTH, [(i, i ^ (mask_odd if i & 1 else mask_even)) for i in range(size)])


def side_of(mask_even, mask_odd):
    me = lax.axis_index(BOTH)
    return jnp.where(me % 2 == 0, me & mask_even, me & mask_odd) != 0


def swap(v):
    mask = lax.axis_size("dp")
    return exchange(v, mask, mask)


def gather_rows(shard, ready, rest):
    bits = width("dp")
    down = list(range(bits - 1, 0, -1))
    even, odd = down, down[-1:] + down[:-1]
    out = shard
    for done, (e, o) in enumerate(zip(even, odd)):
        out = grow(out, done, e, o)
        if done == 0:
            out, rest = lax.optimization_barrier((out, rest))
        if done == 1:
            out, ready = lax.optimization_barrier((out, ready))
    return gather_finish(out, shard.shape), ready, rest


def grow(out, done, e, o):
    other = exchange(out, 1 << e, 1 << o)
    high = side_of(1 << e, 1 << o)
    return jnp.stack([jnp.where(high, other, out), jnp.where(high, out, other)], axis=done)


def gather_finish(out, shape):
    bits = width("dp")
    if bits == 0:
        return out
    other = exchange(out, 1, 1)
    high = side_of(1, 1)
    first = jnp.where(high, other, out)
    second = jnp.where(high, out, other)
    lead = max(bits - 1, 0)
    if lead > 1:
        second = jnp.moveaxis(second, 0, lead - 1)
    return jnp.stack([first, second], axis=lead).reshape((-1,) + shape[1:])


def halves(v, high, axis=0):
    n = v.shape[axis] // 2
    at = jnp.where(high, n, 0)
    return lax.dynamic_slice_in_dim(v, at, n, axis), lax.dynamic_slice_in_dim(v, n - at, n, axis)


def add(p, q):
    return (p.astype(F32) + q.astype(F32)).astype(BF)


def reduce_all(main, small, beside):
    bits = width("dp")
    masks = [1 << b for b in [bits] * width("dir") + list(range(1, bits))]
    odd = list(masks)
    for i in range(0, len(masks) - 1, 2):
        odd[i], odd[i + 1] = masks[i + 1], masks[i]
    order = list(zip(masks, odd))
    core = side_of(1, 1)
    if bits:
        (keep, send), (keep_s, send_s) = halves(main, core, 1), halves(small, core)
        main, small = add(keep, exchange(send, 1, 1)), add(keep_s, exchange(send_s, 1, 1))
    buf = jnp.concatenate([main.reshape(-1, CH), small], axis=0)
    for pair in order:
        keep, send = halves(buf, side_of(*pair))
        buf = add(keep, exchange(send, *pair))
    for at, pair in enumerate(reversed(order)):
        if at == len(order) - 1:
            buf, beside = lax.optimization_barrier((buf, beside))
        got = exchange(buf, *pair)
        high = side_of(*pair)
        buf = jnp.concatenate([jnp.where(high, got, buf), jnp.where(high, buf, got)], axis=0)
    if not bits:
        rows = NCH * D
        both = buf[:rows].reshape(NCH, 2, D // 2, CH)
        parts = [jnp.concatenate([both[:, q].reshape(rows // 2, CH), buf[rows:]], axis=0) for q in range(2)]
        return parts[0], parts[1], jnp.zeros((1,), jnp.int32), beside
    return buf, exchange(buf, 1, 1), core.astype(jnp.int32)[None], beside


def late_kernel(core, own, other, own_s, other_s, zx_o, bc_o, dt_o, cw_o, cb_o, dtb_o, alog_o, skip_o, og_o, ng_o):
    step = pl.program_id(0)
    half = D // 2
    first = core[0] == 0
    upper = jnp.where(first, own[...], other[...]).astype(F32)
    lower = jnp.where(first, other[...], own[...]).astype(F32)

    @pl.when(step < NCH - 1)
    def _():
        zx_o[0:half, :] = upper
        zx_o[half:, :] = lower

    @pl.when(step == NCH - 1)
    def _():
        bc_o[0:half, :] = upper[:, :128]
        bc_o[half:, :] = lower[:, :128]
        dt_o[:, 0:half] = upper[:, 128:].T[: 2 * HEADS, :]
        dt_o[:, half:] = lower[:, 128:].T[: 2 * HEADS, :]

    @pl.when(step == 0)
    def _():
        sm = jnp.where(core[0] == 0, own_s[...], other_s[...]).astype(F32)
        for q in range(NCH):
            n = CH if q < NCH - 1 else 2 * STATE
            cw_o[:, CH * q : CH * q + n] = sm[CONV * q : CONV * (q + 1), :n]
            cb_o[CH * q : CH * q + n] = sm[CONV * NCH + q, :n]
        at = SMALL_AT
        dtb_o[...] = sm[at, : 2 * HEADS]
        alog_o[...] = sm[at, 128 : 128 + 2 * HEADS]
        for q in range(INNER // CH):
            og_o[CH * q : CH * (q + 1)] = sm[at + 1 + q, :]
        for q in range(D // CH):
            ng_o[CH * q : CH * (q + 1)] = sm[at + 7 + q, :]
        skip_o[...] = sm[at + 10, :HEADS]


def late(core, own, other):
    n = INNER // CH
    taps = INNER + 2 * STATE
    shapes = [(D, 2 * INNER), (D, 2 * STATE), (2 * HEADS, D), (CONV, taps), (taps,), (2 * HEADS,), (2 * HEADS,), (HEADS,),
              (INNER,), (D,)]
    half = pl.BlockSpec((D // 2, CH), lambda i: (i, 0))
    small = pl.BlockSpec((SMALL, CH), lambda i: (NCH * D // (2 * SMALL), 0))
    return pl.pallas_call(
        late_kernel,
        grid=(NCH,),
        in_specs=[SMEM_SPEC, half, half, small, small],
        out_specs=[pl.BlockSpec((D, CH), lambda i: (0, n + jnp.minimum(i, n - 1)))] + [full(v) for v in shapes[1:]],
        out_shape=[jax.ShapeDtypeStruct(v, F32) for v in shapes],
        compiler_params=params(),
        name="late",
    )(core, own, other, own, other)


def early_kernel(wg, wo, zx, zx_o, wo_o):
    zx_o[...] = wg[...].astype(F32)
    wo_o[...] = wo[...].astype(F32)


def early(wg, wo, zx):
    n = INNER // CH
    row = pl.BlockSpec((CH, D), lambda i: (i, 0))
    col = pl.BlockSpec((D, CH), lambda i: (0, i))
    return pl.pallas_call(
        early_kernel,
        grid=(n,),
        in_specs=[col, row, pl.BlockSpec(memory_space=pl.ANY)],
        out_specs=[col, row],
        out_shape=[jax.ShapeDtypeStruct((D, 2 * INNER), F32), jax.ShapeDtypeStruct((INNER, D), F32)],
        input_output_aliases={2: 0},
        compiler_params=params(),
        name="early",
    )(wg, wo, zx)


def apart(flag, part, args):
    def nothing(v):
        return jax.tree.map(lambda o: jnp.zeros(o.shape, o.dtype), jax.eval_shape(part, v))

    return lax.cond(flag[1] >= 1, part, nothing, args)


def body(tokens, norm_gain, w_zx, w_bc, w_dt, conv_w, conv_b, dt_bias, a_log, d_skip, out_gain, w_out, doc_lengths, out_grad):
    T = tokens.shape[1]
    devices = lax.axis_size("dir") * lax.axis_size("dp")
    side = lax.axis_index("dir")
    tok = tokens.reshape(T, D)
    og = out_grad.reshape(T, D)
    shard = w_zx.shape[0]
    half = INNER // 2
    mine = jnp.concatenate([w_zx[:, INNER:], w_bc, w_dt, jnp.zeros((shard, 128 - 2 * HEADS), BF)], axis=1)
    halo = lax.ppermute(tok[T - HALO :], "dir", [(0, 1)])
    flag = jnp.concatenate([side[None].astype(jnp.int32), doc_lengths[0]])
    wide = NCH * CH
    cw = jnp.pad(conv_w, ((0, 0), (0, wide - conv_w.shape[1])))
    cb = jnp.pad(conv_b, (0, wide - conv_b.shape[0]))[None]
    lanes = lambda v: jnp.pad(v, (0, 128 - v.shape[0]))[None]
    skip = jnp.repeat(d_skip, HEADDIM)[None]
    rest = jnp.concatenate([w_zx[:, :half], w_zx[:, half:INNER], w_out], axis=0)
    ready = (halo, flag, cw, cb, lanes(dt_bias), lanes(a_log), skip, norm_gain[None], out_gain[None])
    w1, ready, rest = gather_rows(mine, ready, rest)

    def finish(v):
        (flag, b, c, table, act, gm, z, pre, w1, cw, dst, normed, nh, skip, bias, alog, dcs, dlr, gn, tok, halo, ggain, og,
         gain_in) = v
        dst_in = swap(dst)
        dx, rsum, csum, dbc = unmix(flag, b, c, table, act, gm)
        dw1, gn, gnh, small = unproject(flag, dx, gm, act, z, pre, w1, cw, table, dst_in, b, normed, nh, skip, bias, alog,
                                        rsum, csum, dbc, dcs, dlr, gn, tok, halo, ggain)
        back = lax.ppermute(gnh, "dir", [(1, 0)])
        rows = NCH * D
        total = -(-(rows + SMALL) // (16 * devices)) * 16 * devices
        small = jnp.pad(small, ((0, total - rows - SMALL), (0, 0)))
        gn = gn + jnp.pad(back, ((T - HALO, 0), (0, 0)))
        x32 = tok.astype(F32)
        rho = lax.rsqrt(jnp.mean(x32 * x32, axis=1, keepdims=True) + EPS)
        e_in = gn * gain_in
        gx = rho * e_in - x32 * (rho * rho * rho * jnp.mean(e_in * x32, axis=1, keepdims=True))
        grad_tokens = (og.astype(F32) + gx).astype(BF)
        own, other, core, grad_tokens = reduce_all(dw1, small, grad_tokens)
        return (grad_tokens,) + tuple(late(core, own, other))

    def rest_of(v):
        w1, rest, (halo, flag, cw, cb, bias, alog, skip, gain_in, gain_out), tok, og = v
        rest = lax.all_gather(rest, "dp", axis=0, tiled=False)
        if shard % 16:
            rest = jnp.concatenate([rest[:, :shard].reshape(D, D), rest[:, shard : 2 * shard].reshape(D, D),
                                    rest[:, 2 * shard :].reshape(INNER, D)], axis=0)[None]
        normed, nh, pre, z, act, rows, wrc, b, bt, c, ct, st = project(flag, tok, halo, gain_in, w1, cw, cb, bias, alog)
        st_in = swap(st)
        y = mix(flag, b, c, rows, act, skip)
        no, bo, gg, gm, gn, dcs, dlr, dst, ggain = gate(flag, y, wrc, c, ct, st_in, normed, rest, tok, og, gain_out)
        tn = lambda p, q: lax.dot_general(p, q, (((0,), (0,)), ((), ())), preferred_element_type=F32).astype(BF)
        dwo, dwg = tn(no, og), tn(normed, gg)
        dwo, dwg, gm = lax.optimization_barrier((dwo, dwg, gm))
        dwo, dwg = lax.psum((dwo, dwg), BOTH)
        args = (flag, b, c, rows, act, gm, z, pre, w1, cw, dst, normed, nh, skip, bias, alog, dcs, dlr, gn, tok, halo, ggain,
                og, gain_in)
        grad_tokens, zx, g_bc, g_dt, g_cw, g_cb, g_dtb, g_alog, g_skip, g_og, g_ng = apart(flag, finish, args)
        zx, g_wo = early(dwg, dwo, zx)
        return bo, grad_tokens, g_ng, zx, g_bc, g_dt.T, g_cw, g_cb, g_dtb, g_alog, g_skip, g_og, g_wo

    outs = rest_of((w1, rest, ready, tok, og))
    return (outs[0].reshape(tokens.shape), outs[1].reshape(tokens.shape)) + tuple(outs[2:])


def solution(mesh):
    rows, weight, whole = P("dp", "dir", None), P("dp", None), P()
    placed = (rows, whole, weight, weight, weight, whole, whole, whole, whole, whole, whole, weight, weight, rows)
    return jax.shard_map(body, mesh=mesh, in_specs=placed, out_specs=(rows, rows) + (whole,) * 11, check_vma=False)
```

```python
import functools

import jax
import jax.numpy as jnp
from jax import lax
from jax.experimental import pallas as pl
from jax.experimental.pallas import tpu as pltpu
from jax.sharding import PartitionSpec as P

D = 768
HEADS = 24
HEADDIM = 64
STATE = 64
INNER = 1536
CONV = 4
NDOC = 4
PAIRS = HEADS // 2
HALO = 16
CH = 256
NCH = 7
Q = 128
GROUP = CH // HEADDIM
SMALL_AT = (CONV + 1) * NCH
SMALL = 64
EXTRA = 16
EPS = 1e-05
LOG2E = 1.4426950408889634
BF = jnp.bfloat16
F32 = jnp.float32
HI = lax.Precision.HIGHEST


def nn(a, b):
    return lax.dot_general(a, b, (((1,), (0,)), ((), ())), preferred_element_type=F32)


def nt(a, b):
    return lax.dot_general(a, b, (((1,), (1,)), ((), ())), preferred_element_type=F32)


def iota(shape, axis):
    return lax.broadcasted_iota(jnp.int32, shape, axis)


def sigm(v):
    return 1.0 / (1.0 + jnp.exp(-v))


def lane_pair(col_a, col_b, rows):
    return jnp.where(iota((rows, 128), 1) < 64, col_a, col_b)


def params(mib=60):
    return pltpu.CompilerParams(
        dimension_semantics=("arbitrary",), vmem_limit_bytes=mib * 1024 * 1024
    )


def full(shape):
    return pl.BlockSpec(shape, lambda i: tuple(0 for _ in shape))


SMEM_SPEC = pl.BlockSpec(memory_space=pltpu.SMEM)


def doc_ids(flag, places):
    total = jnp.zeros(places.shape, jnp.int32)
    end = 0
    for k in range(NDOC):
        end = end + flag[1 + k]
        total = total + jnp.where(places >= end, 1, 0)
    return jnp.where(places < 0, -1, total)


def doc_at(flag, place):
    total = 0
    end = 0
    for k in range(NDOC):
        end = end + flag[1 + k]
        total = total + jnp.where(place >= end, 1, 0)
    return total


def doc_col(flag, T, lead=0):
    return doc_ids(flag, iota((T + lead, 1), 0) + (flag[0] * T - lead))


def doc_row(flag, T):
    return doc_ids(flag, iota((1, T), 1) + flag[0] * T)


def project_kernel(T, flag, tok, halo, gain, w, cw, cb, bias, alog,
                   norm_o, normt_o, nh_o, pre_o, z_o, act_o, rows_o, wrc_o, uv_o, keep_o, b_o, bt_o, c_o, ct_o, st_o, ncat, pf, segc):
    step = pl.program_id(0)

    @pl.when(step == 0)
    def _():
        def norm(v):
            v = v.astype(F32)
            ms = jnp.mean(v * v, axis=1, keepdims=True)
            return (v * lax.rsqrt(ms + EPS) * gain[...]).astype(BF)

        nh = norm(halo[...])
        own = norm(tok[...])
        nh_o[...] = nh
        norm_o[...] = own
        normt_o[...] = own.astype(F32).T.astype(BF)
        ncat[0:HALO, :] = nh
        ncat[HALO:, :] = own
        segc[...] = doc_col(flag, T, HALO)

    proj = nn(ncat[...], w[...]).astype(BF)
    pre_o[...] = proj
    pf[...] = proj.astype(F32)
    segs = segc[...]
    here = segs[HALO:, :]
    z = cb[...] + cw[CONV - 1 : CONV, :] * pf[HALO:, :]
    for k in range(1, CONV):
        same = segs[HALO - k : HALO + T - k, :] == here
        z = z + jnp.where(same, cw[CONV - 1 - k : CONV - k, :] * pf[HALO - k : HALO + T - k, :], 0.0)
    z_o[...] = z.astype(BF)
    act = z * sigm(z)
    act_o[...] = act.astype(BF)

    @pl.when(step == 0)
    def _():
        bc = act[:, :128]
        b_o[...] = bc[:, :64].astype(BF)
        c_o[...] = bc[:, 64:].astype(BF)
        bct = bc.T
        bt_o[...] = bct[:64, :].astype(BF)
        ct_o[...] = bct[64:, :].astype(BF)
        v = pf[HALO:, 128:] + bias[...]
        dt = jnp.maximum(v, 0.0) + jnp.log1p(jnp.exp(-jnp.abs(v)))
        rate = dt * (-LOG2E * jnp.exp(alog[...]))
        rate_t = rate.T
        dt_t = dt.T
        upto = (iota((T, T), 0) <= iota((T, T), 1)).astype(F32)
        inc = lax.dot_general(rate_t, upto, (((1,), (0,)), ((), ())), precision=HI, preferred_element_type=F32)
        isf = iota((128, T), 0) < HEADS
        cum = jnp.where(isf, inc, inc - rate_t)
        ldt = jnp.log2(jnp.maximum(dt_t, 1e-37))
        key = jnp.where(isf, cum - ldt, cum + ldt)
        segv = doc_row(flag, T)
        left, right = doc_at(flag, T - 1), doc_at(flag, T)
        send_f = jnp.where(segv == left, jnp.exp2(cum[:, T - 1 :] - key), 0.0)
        send_b = jnp.where(segv == right, jnp.exp2(key), 0.0)
        recv_f = jnp.where(segv == left, jnp.exp2(cum), 0.0)
        recv_b = jnp.where(segv == right, jnp.exp2(inc[:, T - 1 :] - cum), 0.0)
        first = flag[0] == 0
        send = jnp.where(first, send_f[0:HEADS], send_b[HEADS : 2 * HEADS])
        recv = jnp.where(first, recv_b[HEADS : 2 * HEADS], recv_f[0:HEADS])
        for p in range(PAIRS):
            f, r = 2 * p, HEADS + 2 * p
            rows_o[p, 0:2, :] = cum[f : f + 2]
            rows_o[p, 2:4, :] = cum[r : r + 2]
            rows_o[p, 4:6, :] = key[f : f + 2]
            rows_o[p, 6:8, :] = key[r : r + 2]
            rows_o[p, 8:10, :] = send[f : f + 2]
            rows_o[p, 10:12, :] = recv[f : f + 2]
            rows_o[p, 12:16, :] = jnp.zeros((4, T), F32)
        recv_pad = jnp.concatenate([recv, jnp.zeros((128 - HEADS, T), F32)], axis=0)
        wrc_o[...] = recv_pad.T.astype(BF)
        cum_f, cum_r = cum[0:HEADS], cum[HEADS : 2 * HEADS]
        key_f, key_r = key[0:HEADS], key[HEADS : 2 * HEADS]
        quads = [[], [], [], []]
        none = jnp.zeros((HEADS, Q), F32)
        lane = iota((HEADS, 128), 1)
        keep_f = jnp.zeros((HEADS, 128), F32)
        keep_r = jnp.zeros((HEADS, 128), F32)
        for k in range(T // Q):
            lo, hi = k * Q, (k + 1) * Q
            sg = segv[:, lo:hi]
            before = cum_f[:, lo - 1 : lo] if k > 0 else None
            after = cum_r[:, hi : hi + 1] if hi < T else None
            quads[0].append(none if k == 0 else jnp.where(sg == segv[:, lo - 1 : lo], jnp.exp2(cum_f[:, lo:hi] - before), 0.0))
            quads[1].append(jnp.where(sg == segv[:, hi - 1 : hi], jnp.exp2(cum_f[:, hi - 1 : hi] - key_f[:, lo:hi]), 0.0))
            quads[2].append(none if hi == T else jnp.where(sg == segv[:, hi : hi + 1], jnp.exp2(after - cum_r[:, lo:hi]), 0.0))
            quads[3].append(jnp.where(sg == segv[:, lo : lo + 1], jnp.exp2(key_r[:, lo:hi] - cum_r[:, lo : lo + 1]), 0.0))
            if k > 0:
                through = jnp.where(segv[:, lo - 1 : lo] == segv[:, hi - 1 : hi], jnp.exp2(cum_f[:, hi - 1 : hi] - before), 0.0)
                keep_f = jnp.where(lane == k, through, keep_f)
            if hi < T:
                through = jnp.where(segv[:, lo : lo + 1] == segv[:, hi : hi + 1], jnp.exp2(after - cum_r[:, lo : lo + 1]), 0.0)
                keep_r = jnp.where(lane == k, through, keep_r)
        quads = [jnp.concatenate(v, axis=1) for v in quads]
        uv_o[...] = jnp.concatenate(quads + [jnp.zeros((128 - 4 * HEADS, T), F32)], axis=0).T.astype(BF)
        keeps = jnp.concatenate([keep_f, keep_r, jnp.zeros((128 - 2 * HEADS, 128), F32)], axis=0).T
        keep_o[...] = keeps[0:8, :]

    @pl.when(step > 0)
    def _():
        for j in range(CH // 128):
            cols = rows_o[2 * (step - 1) + j, 8:16, :].T
            wide = lane_pair(cols[:, 0:1], cols[:, 1:2], T)
            xw = (act[:, 128 * j : 128 * (j + 1)] * wide).astype(BF)
            st_o[:, 128 * j : 128 * (j + 1)] = nn(bt_o[...], xw).astype(BF)


def project(flag, tok, halo, gain, w1, conv_w, conv_b, bias, alog):
    T = tok.shape[0]
    E = T + HALO
    chunk = lambda i: lax.rem(i + NCH - 1, NCH)
    xchunk = lambda i: jnp.maximum(i - 1, 0)
    col = lambda rows: pl.BlockSpec((rows, CH), lambda i: (0, chunk(i)))
    shapes = [
        ((T, D), BF), ((D, T), BF), ((HALO, D), BF), ((E, NCH * CH), BF), ((T, NCH * CH), BF), ((T, NCH * CH), BF),
        ((PAIRS, 16, T), F32), ((T, 128), BF), ((T, 128), BF), ((8, 128), F32), ((T, 64), BF), ((64, T), BF), ((T, 64), BF), ((64, T), BF),
        ((64, INNER), BF),
    ]
    out_specs = [
        full((T, D)), full((D, T)), full((HALO, D)), col(E), col(T), col(T), full((PAIRS, 16, T)), full((T, 128)), full((T, 128)), full((8, 128)), full((T, 64)),
        full((64, T)), full((T, 64)), full((64, T)), pl.BlockSpec((64, CH), lambda i: (0, xchunk(i))),
    ]
    return pl.pallas_call(
        functools.partial(project_kernel, T),
        grid=(NCH,),
        in_specs=[SMEM_SPEC, full((T, D)), full((HALO, D)), full((1, D)), col(D), col(CONV), col(1),
                  full((1, 128)), full((1, 128))],
        out_specs=out_specs,
        out_shape=[jax.ShapeDtypeStruct(s, d) for s, d in shapes],
        scratch_shapes=[pltpu.VMEM((E, D), BF), pltpu.VMEM((E, CH), F32), pltpu.VMEM((E, 1), jnp.int32)],
        compiler_params=params(),
        name="project",
    )(flag, tok, halo, gain, w1, conv_w, conv_b, bias, alog)


def shift_matrix(flag, T, lo):
    first = flag[0] * T + lo
    own = doc_ids(flag, iota((Q, 1), 0) + first)
    from_doc = doc_ids(flag, iota((1, Q + HALO), 1) + (first - HALO))
    gap = iota((Q, Q + HALO), 0) + HALO - iota((Q, Q + HALO), 1)
    return jnp.concatenate([((gap == k) & (own == from_doc)).astype(F32) for k in range(1, CONV)], axis=0).astype(BF)


def shift_back_matrix(flag, T, lo):
    first = flag[0] * T + lo
    own = doc_ids(flag, iota((1, Q), 1) + first)
    from_doc = doc_ids(flag, iota((Q + HALO, 1), 0) + (first - HALO))
    gap = iota((Q + HALO, Q), 1) + HALO - iota((Q + HALO, Q), 0)
    return jnp.concatenate([((gap == k) & (own == from_doc)).astype(F32) for k in range(1, CONV)], axis=0).astype(BF)


def same_doc(flag, T, lo):
    first = flag[0] * T + lo
    a = doc_ids(flag, iota((Q, 1), 0) + first)
    b = doc_ids(flag, iota((1, Q), 1) + first)
    return (a == b) & (iota((Q, Q), 0) != iota((Q, Q), 1))


def spread_of(step, slot, dtype=BF):
    base = slot * HEADS + GROUP * step
    return (lax.div(iota((128, CH), 1), HEADDIM) + base == iota((128, CH), 0)).astype(dtype)


def exact(a, b):
    return lax.dot_general(a, b, (((1,), (0,)), ((), ())), precision=HI, preferred_element_type=F32)


def states(T, bt, vf, vr, keep_f, keep_r):
    n = T // Q
    ahead, back = [None] * n, [None] * n
    for k in range(1, n):
        new = nn(bt[:, (k - 1) * Q : k * Q], vf[(k - 1) * Q : k * Q])
        ahead[k] = new if k == 1 else new + keep_f[k - 1 : k] * ahead[k - 1]
    for k in reversed(range(n - 1)):
        new = nn(bt[:, (k + 1) * Q : (k + 2) * Q], vr[(k + 1) * Q : (k + 2) * Q])
        back[k] = new if k == n - 2 else new + keep_r[k + 1 : k + 2] * back[k + 1]
    return ahead, back


def mix_kernel(T, flag, b, bt, c, uv, keep, rows, x, skip, y_o, sc):
    step = pl.program_id(0)
    n = T // Q

    @pl.when(step == 0)
    def _():
        for i in range(n):
            lo, hi = i * Q, (i + 1) * Q
            sc[i] = jnp.where(same_doc(flag, T, lo), nt(c[lo:hi, :], b[lo:hi, :]), 0.0)

    x4 = x[...]
    x32 = x4.astype(F32)
    table = uv[...]
    uf, vf, ur, vr = [nn(table, spread_of(step, slot)) for slot in range(4)]
    keep_f = exact(keep[...], spread_of(step, 0, F32))
    keep_r = exact(keep[...], spread_of(step, 1, F32))
    ahead, back = states(T, bt, (vf * x32).astype(BF), (vr * x32).astype(BF), keep_f, keep_r)
    later = iota((Q, Q), 0) > iota((Q, Q), 1)
    lane = iota((Q, 128), 1) < HEADDIM
    cols = [rows[p][0:8].T for p in range(GROUP // 2)]
    for i in range(n):
        lo, hi = i * Q, (i + 1) * Q
        pieces = []
        for p in range(GROUP // 2):
            xs = x4[lo:hi, 128 * p : 128 * (p + 1)]
            outs = []
            for h in range(2):
                cf = cols[p][lo:hi, h : h + 1]
                cr = cols[p][lo:hi, 2 + h : 3 + h]
                kf = rows[p, 4 + h : 5 + h, lo:hi]
                kr = rows[p, 6 + h : 7 + h, lo:hi]
                m = sc[i] * jnp.exp2(jnp.where(later, cf - kf, kr - cr))
                outs.append(nn(m.astype(BF), xs))
            pieces.append(jnp.where(lane, outs[0], outs[1]))
        y = jnp.concatenate(pieces, axis=1) + skip[...] * x32[lo:hi]
        if i > 0:
            y = y + uf[lo:hi] * nn(c[lo:hi, :], ahead[i].astype(BF))
        if i < n - 1:
            y = y + ur[lo:hi] * nn(c[lo:hi, :], back[i].astype(BF))
        y_o[lo:hi, :] = y


def mix(flag, b, bt, c, uv, keep, rows, act, skip):
    T = b.shape[0]
    blk = pl.BlockSpec((T, CH), lambda i: (0, i))
    return pl.pallas_call(
        functools.partial(mix_kernel, T),
        grid=(INNER // CH,),
        in_specs=[SMEM_SPEC, full((T, 64)), full((64, T)), full((T, 64)), full((T, 128)), full((8, 128)),
                  pl.BlockSpec((GROUP // 2, 16, T), lambda i: (i, 0, 0)), blk, pl.BlockSpec((1, CH), lambda i: (0, i))],
        out_specs=blk,
        out_shape=jax.ShapeDtypeStruct((T, INNER), F32),
        scratch_shapes=[pltpu.VMEM((T // Q, Q, Q), F32)],
        compiler_params=params(),
        name="mix",
    )(flag, b, bt, c, uv, keep, rows, act, skip)


def seam_width(wrc):
    spread = (lax.div(iota((128, INNER), 1), HEADDIM) == iota((128, INNER), 0)).astype(BF)
    return nn(wrc[...], spread)


def gate_kernel(shard, y, wrc, c, st, normed, normt, rest, og, ogt, gain, no_o, gg_o, gm_o, dwg_o, dwo_o, ggain_o, acc_g, acc_o):
    step = pl.program_id(0)
    mixed = y[...] + nn(c[...], st[...]) * seam_width(wrc)
    half = INNER // 2
    own = normed[...]
    gz = jnp.concatenate([nn(own, rest[:, :shard, :].reshape(D, half)), nn(own, rest[:, shard : 2 * shard, :].reshape(D, half))],
                         axis=1)
    sig = sigm(gz)
    sil = gz * sig
    gated = mixed * sil
    rho = lax.rsqrt(jnp.mean(gated * gated, axis=1, keepdims=True) + EPS)
    no = (gated * rho * gain[...]).astype(BF)
    no_o[...] = no
    gno = nt(og[...], rest[:, 2 * shard :, :].reshape(INNER, D))
    e = gno * gain[...]
    part = jnp.sum(gno * gated * rho, axis=0, keepdims=True)
    mean_eg = jnp.mean(e * gated, axis=1, keepdims=True)
    ggated = rho * e - gated * (rho * rho * rho * mean_eg)
    gg = (ggated * mixed * sig * (1.0 + gz * (1.0 - sig))).astype(BF)
    gg_o[...] = gg
    gm_o[...] = (ggated * sil).astype(BF)
    dwg = nn(normt[...], gg)
    dwo = nn(ogt[...], no)

    @pl.when(step == 0)
    def _():
        acc_g[...] = dwg
        acc_o[...] = dwo
        ggain_o[...] = part

    @pl.when(step > 0)
    def _():
        dwg_o[...] = (acc_g[...] + dwg).astype(BF)
        dwo_o[...] = (acc_o[...] + dwo).astype(BF)
        ggain_o[...] += part


def gate(y, wrc, c, st, normed, normt, rest, og, ogt, gain):
    T = y.shape[0]
    rb = T // 2
    row = lambda n: pl.BlockSpec((rb, n), lambda i: (i, 0))
    col = lambda n: pl.BlockSpec((n, rb), lambda i: (0, i))
    shapes = [((T, INNER), BF), ((T, INNER), BF), ((T, INNER), BF), ((D, INNER), BF), ((D, INNER), BF), ((1, INNER), F32)]
    return pl.pallas_call(
        functools.partial(gate_kernel, rest.shape[1] // 4),
        grid=(2,),
        in_specs=[row(INNER), row(128), row(64), full((64, INNER)), row(D), col(D), full(rest.shape), row(D), col(D),
                  full((1, INNER))],
        out_specs=[row(INNER), row(INNER), row(INNER), full((D, INNER)), full((D, INNER)), full((1, INNER))],
        out_shape=[jax.ShapeDtypeStruct(v, d) for v, d in shapes],
        scratch_shapes=[pltpu.VMEM((D, INNER), F32), pltpu.VMEM((D, INNER), F32)],
        compiler_params=params(),
        name="gate",
    )(y, wrc, c, st, normed, normt, rest, og, ogt, gain)


def side_kernel(flag, gm, wrc, c, ct, st, dcs_o, dlr_o, dst_o, acc):
    step = pl.program_id(0)
    gw = gm[...].astype(F32) * seam_width(wrc)
    seam = gw * nn(c[...], st[...])
    gw = gw.astype(BF)
    dcs_o[...] = nt(gw, st[...])
    shift = jnp.where(flag[0] == 0, HEADS, 0)
    gather = (lax.div(iota((INNER, 128), 0), HEADDIM) + shift == iota((INNER, 128), 1)).astype(BF)
    dlr_o[...] = nn(seam.astype(BF), gather)
    dst = nn(ct[...], gw)

    @pl.when(step == 0)
    def _():
        acc[...] = dst

    @pl.when(step > 0)
    def _():
        dst_o[...] = (acc[...] + dst).astype(BF)


def aside(flag, gm, wrc, c, ct, st):
    T = gm.shape[0]
    rb = T // 2
    row = lambda n: pl.BlockSpec((rb, n), lambda i: (i, 0))
    shapes = [((T, 64), F32), ((T, 128), F32), ((64, INNER), BF)]
    return pl.pallas_call(
        side_kernel,
        grid=(2,),
        in_specs=[SMEM_SPEC, row(INNER), row(128), row(64), pl.BlockSpec((64, rb), lambda i: (0, i)), full((64, INNER))],
        out_specs=[row(64), row(128), full((64, INNER))],
        out_shape=[jax.ShapeDtypeStruct(v, d) for v, d in shapes],
        scratch_shapes=[pltpu.VMEM((64, INNER), F32)],
        compiler_params=params(),
        name="side",
    )(flag, gm, wrc, c, ct, st)


def deferred_kernel(shard, dpl, dph, w1, gg, no, rest, tok, halo, bo_o, gn_o, gnh_o, part_o, acc):
    step = pl.program_id(0)
    half = INNER // 2

    def unit(v):
        v = v.astype(F32)
        return v * lax.rsqrt(jnp.mean(v * v, axis=1, keepdims=True) + EPS)

    bo_o[...] = (tok[...].astype(F32) + nn(no[...], rest[:, 2 * shard :, :].reshape(INNER, D))).astype(BF)
    gn = nt(dpl[...], w1[...])
    gn = gn + nt(gg[:, :half], rest[:, :shard, :].reshape(D, half))
    gn = gn + nt(gg[:, half:], rest[:, shard : 2 * shard, :].reshape(D, half))
    gn_o[...] = gn
    part = jnp.sum(gn * unit(tok[...]), axis=0, keepdims=True)

    @pl.when(step == 0)
    def _():
        gnh = nt(dph[...], w1[...])
        gnh_o[...] = gnh
        acc[0:1, :] = part + jnp.sum(gnh * unit(halo[...]), axis=0, keepdims=True)

    @pl.when(step > 0)
    def _():
        total = acc[0:1, :] + part
        rows = [total[:, CH * q : CH * (q + 1)] for q in range(D // CH)]
        part_o[...] = jnp.concatenate(rows + [jnp.zeros((EXTRA - D // CH, CH), F32)], axis=0).astype(BF)


def deferred(dpl, dph, w1, gg, no, rest, tok, halo):
    T = dpl.shape[0]
    rb = T // 2
    wide = NCH * CH
    row = lambda n: pl.BlockSpec((rb, n), lambda i: (i, 0))
    shapes = [((T, D), BF), ((T, D), F32), ((HALO, D), F32), ((EXTRA, CH), BF)]
    return pl.pallas_call(
        functools.partial(deferred_kernel, rest.shape[1] // 4),
        grid=(2,),
        in_specs=[row(wide), full((HALO, wide)), full((D, wide)), row(INNER), row(INNER), full(rest.shape), row(D),
                  full((HALO, D))],
        out_specs=[row(D), row(D), full((HALO, D)), full((EXTRA, CH))],
        out_shape=[jax.ShapeDtypeStruct(v, d) for v, d in shapes],
        scratch_shapes=[pltpu.VMEM((8, D), F32)],
        compiler_params=params(),
        name="deferred",
    )(dpl, dph, w1, gg, no, rest, tok, halo)


def unmix_kernel(T, flag, b, bt, c, ct, uv, keep, rows, x, g, dx_o, rsum_o, csum_o, roff_o, coff_o, dkeep_o, dbc_o,
                 sc, dsc, db, dc):
    step = pl.program_id(0)
    n = T // Q

    @pl.when(step == 0)
    def _():
        for i in range(n):
            lo, hi = i * Q, (i + 1) * Q
            sc[i] = jnp.where(same_doc(flag, T, lo), nt(b[lo:hi, :], c[lo:hi, :]), 0.0)
        dsc[...] = jnp.zeros((n, Q, Q), F32)
        db[...] = jnp.zeros((T, 64), F32)
        dc[...] = jnp.zeros((T, 64), F32)
        rsum_o[...] = jnp.zeros((128, T), F32)
        csum_o[...] = jnp.zeros((T, 128), F32)
        roff_o[...] = jnp.zeros((T, 128), F32)
        coff_o[...] = jnp.zeros((T, 128), F32)
        dkeep_o[...] = jnp.zeros((8, 128), F32)

    x4 = x[...]
    g4 = g[...]
    x32 = x4.astype(F32)
    g32 = g4.astype(F32)
    wide = nn(uv[...], jnp.concatenate([spread_of(step, slot) for slot in range(4)], axis=1))
    uf, vf, ur, vr = [wide[:, CH * q : CH * (q + 1)] for q in range(4)]
    keep_f = exact(keep[...], spread_of(step, 0, F32))
    keep_r = exact(keep[...], spread_of(step, 1, F32))
    vxf, vxr = (vf * x32).astype(BF), (vr * x32).astype(BF)
    ugf, ugr = (uf * g32).astype(BF), (ur * g32).astype(BF)
    ahead, back = states(T, bt, vxf, vxr, keep_f, keep_r)
    lane = iota((Q, 128), 1)
    half = lane < HEADDIM
    earlier = iota((Q, Q), 0) < iota((Q, Q), 1)
    base = GROUP * step
    slot = lax.div(iota((2 * CH, 128), 0), HEADDIM)
    gather = (jnp.where(slot < GROUP, slot, slot + HEADS - GROUP) + base == iota((2 * CH, 128), 1)).astype(BF)
    cols = [rows[p][0:8].T for p in range(GROUP // 2)]
    dahead, dback = [None] * (n + 1), [None] * (n + 1)
    for k in reversed(range(1, n)):
        own = nn(ct[:, k * Q : (k + 1) * Q], ugf[k * Q : (k + 1) * Q])
        dahead[k] = own if k == n - 1 else own + keep_f[k : k + 1] * dahead[k + 1]
    for k in range(n - 1):
        own = nn(ct[:, k * Q : (k + 1) * Q], ugr[k * Q : (k + 1) * Q])
        dback[k] = own if k == 0 else own + keep_r[k : k + 1] * dback[k - 1]
    through = [jnp.zeros((1, 2 * CH), F32)] * 8
    for k in range(1, n - 1):
        pf = jnp.sum(keep_f[k : k + 1] * ahead[k] * dahead[k + 1], axis=0, keepdims=True)
        pr = jnp.sum(keep_r[k : k + 1] * back[k] * dback[k - 1], axis=0, keepdims=True)
        through[k] = jnp.concatenate([pf, pr], axis=1)
    dkeep_o[...] += nn(jnp.concatenate(through, axis=0).astype(BF), gather)
    totals = [[] for _ in range(2 * GROUP)]
    r_off, c_off = [], []
    none = jnp.zeros((Q, CH), F32)
    for j in range(n):
        lo, hi = j * Q, (j + 1) * Q
        pieces = []
        stat = jnp.zeros((Q, 128), F32)
        for p in range(GROUP // 2):
            xs = x4[lo:hi, 128 * p : 128 * (p + 1)]
            gs = g4[lo:hi, 128 * p : 128 * (p + 1)]
            zero = jnp.zeros_like(xs)
            gts = nt(jnp.concatenate([jnp.where(half, xs, zero), jnp.where(half, zero, xs)], axis=0), gs)
            ms = []
            for h in range(2):
                cf = rows[p, h : h + 1, lo:hi]
                cr = rows[p, 2 + h : 3 + h, lo:hi]
                kf = cols[p][lo:hi, 4 + h : 5 + h]
                kr = cols[p][lo:hi, 6 + h : 7 + h]
                gt = gts[h * Q : (h + 1) * Q]
                d = jnp.exp2(jnp.where(earlier, cf - kf, kr - cr))
                m = sc[j] * d
                ms.append(m.astype(BF))
                dsc[j] += gt * d
                w = gt * m
                wf = jnp.where(earlier, w, 0.0)
                wr = w - wf
                at = base + 2 * p + h
                stat = stat + jnp.where(lane == at, jnp.sum(wf, axis=1, keepdims=True), 0.0)
                stat = stat + jnp.where(lane == at + HEADS, jnp.sum(wr, axis=1, keepdims=True), 0.0)
                totals[2 * p + h].append(jnp.sum(wf, axis=0, keepdims=True))
                totals[GROUP + 2 * p + h].append(jnp.sum(wr, axis=0, keepdims=True))
            out = nn(jnp.concatenate(ms, axis=0), gs)
            pieces.append(jnp.where(half, out[:Q], out[Q:]))
        dx = jnp.concatenate(pieces, axis=1)
        zero = jnp.zeros((STATE, CH), BF)
        into = jnp.concatenate([ahead[j].astype(BF) if j > 0 else zero, back[j].astype(BF) if j < n - 1 else zero], axis=1)
        outof = jnp.concatenate([dahead[j + 1].astype(BF) if j < n - 1 else zero, dback[j - 1].astype(BF) if j > 0 else zero],
                                axis=1)
        both_u = jnp.concatenate([ugf[lo:hi], ugr[lo:hi]], axis=1)
        both_v = jnp.concatenate([vxf[lo:hi], vxr[lo:hi]], axis=1)
        r_off.append((both_u.astype(F32) * nn(c[lo:hi, :], into)).astype(BF))
        dv = nn(b[lo:hi, :], outof)
        c_off.append((both_v.astype(F32) * dv).astype(BF))
        dx_o[lo:hi, :] = dx + vf[lo:hi] * dv[:, :CH] + vr[lo:hi] * dv[:, CH:]
        dc[lo:hi, :] += nt(both_u, into)
        db[lo:hi, :] += nt(both_v, outof)
        csum_o[lo:hi, :] += stat
    off = nn(jnp.concatenate(r_off + c_off, axis=0), gather)
    roff_o[...] += off[:T]
    coff_o[...] += off[T:]
    for q in range(2):
        for h in range(GROUP):
            rsum_o[pl.ds(HEADS * q + base + h, 1), :] = jnp.concatenate(totals[GROUP * q + h], axis=1)

    @pl.when(step == INNER // CH - 1)
    def _():
        for j in range(n):
            lo, hi = j * Q, (j + 1) * Q
            ds = jnp.where(same_doc(flag, T, lo), dsc[j], 0.0)
            dbc_o[lo:hi, 0:64] = db[lo:hi, :] + nn(ds.astype(BF), c[lo:hi, :])
            dbc_o[lo:hi, 64:128] = dc[lo:hi, :] + nn(ds.T.astype(BF), b[lo:hi, :])


def unmix(flag, b, bt, c, ct, uv, keep, rows, act, g):
    T = b.shape[0]
    n = T // Q
    blk = pl.BlockSpec((T, CH), lambda i: (0, i))
    shapes = [(T, INNER), (128, T), (T, 128), (T, 128), (T, 128), (8, 128), (T, 128)]
    return pl.pallas_call(
        functools.partial(unmix_kernel, T),
        grid=(INNER // CH,),
        in_specs=[SMEM_SPEC, full((T, 64)), full((64, T)), full((T, 64)), full((64, T)), full((T, 128)), full((8, 128)),
                  pl.BlockSpec((GROUP // 2, 16, T), lambda i: (i, 0, 0)), blk, blk],
        out_specs=[blk] + [full(v) for v in shapes[1:]],
        out_shape=[jax.ShapeDtypeStruct(v, F32) for v in shapes],
        scratch_shapes=[pltpu.VMEM((n, Q, Q), F32), pltpu.VMEM((n, Q, Q), F32), pltpu.VMEM((T, 64), F32),
                        pltpu.VMEM((T, 64), F32)],
        compiler_params=params(),
        name="unmix",
    )(flag, b, bt, c, ct, uv, keep, rows, act, g)


def unproject_kernel(T, flag, dx, g, act, z, pre, cw, rows, dst, b, nt_s, nh, skip, bias, alog,
                     rsum, csum, roff, coff, dkeep, dbc, dcs, dlr, ggain,
                     dw_o, dpl_o, dph_o, small_o,
                     ht_s, tot, hd_s, dbs, dls, small, shifts, shifts_back):
    step = pl.program_id(0)
    E = T + HALO

    @pl.when(step == 0)
    def _():
        for i in range(T // Q):
            shifts[i] = shift_matrix(flag, T, i * Q)
            shifts_back[i] = shift_back_matrix(flag, T, i * Q)
        small[...] = jnp.zeros((SMALL, CH), F32)
        pad = jnp.concatenate([nh[...].astype(F32), jnp.zeros((128 - HALO, D), F32)], axis=0)
        ht_s[...] = pad.T.astype(BF)
        hd_s[...] = jnp.zeros((128, CH), BF)
        dbs[...] = jnp.zeros((T, 64), F32)
        dls[...] = jnp.zeros((T, 128), F32)

    def through_conv(dact):
        tot[...] = jnp.zeros((E, CH), F32)
        g_b = jnp.zeros((1, CH), F32)
        g_w = [jnp.zeros((1, CH), F32) for _ in range(CONV)]
        wide = Q + HALO
        for i in range(T // Q):
            lo, hi = i * Q, (i + 1) * Q
            zz = z[lo:hi, :].astype(F32)
            sg = sigm(zz)
            dz = dact[lo:hi] * sg * (1.0 + zz * (1.0 - sg))
            moved = nn(shifts[i], pre[lo : hi + HALO, :])
            back = nn(shifts_back[i], dz.astype(BF))
            g_b = g_b + jnp.sum(dz, axis=0, keepdims=True)
            g_w[0] = g_w[0] + jnp.sum(dz * pre[lo + HALO : hi + HALO, :].astype(F32), axis=0, keepdims=True)
            part = jnp.zeros((wide, CH), F32)
            for k in range(1, CONV):
                g_w[k] = g_w[k] + jnp.sum(dz * moved[(k - 1) * Q : k * Q], axis=0, keepdims=True)
                part = part + cw[CONV - 1 - k : CONV - k, :] * back[(k - 1) * wide : k * wide]
            tot[lo : hi + HALO, :] += part
            tot[lo + HALO : hi + HALO, :] += cw[CONV - 1 : CONV, :] * dz
        small[pl.ds(CONV * NCH + step, 1), :] = g_b
        for k in range(CONV):
            small[pl.ds(CONV * step + CONV - 1 - k, 1), :] = g_w[k]
        return tot[...]

    def emit(local, halo):
        local = local.astype(BF)
        hd_s[0:HALO, :] = halo.astype(BF)
        dw_o[0] = (nn(nt_s[...], local) + nn(ht_s[...], hd_s[...])).astype(BF)
        dpl_o[...] = local
        dph_o[...] = hd_s[0:HALO, :]

    @pl.when(step < NCH - 1)
    def _():
        wides = []
        for j in range(CH // 128):
            cols = rows[2 * step + j, 8:16, :].T
            wides.append(lane_pair(cols[:, 0:1], cols[:, 1:2], T))
        wide = jnp.concatenate(wides, axis=1)
        x32 = act[...].astype(F32)
        g32 = g[...].astype(F32)
        wq = wide * nn(b[...], dst[...])
        dbs[...] += nt((x32 * wide).astype(BF), dst[...])
        base = 4 * step + jnp.where(flag[0] == 0, 0, HEADS)
        sel = (lax.div(iota((CH, 128), 0), 64) + base == iota((CH, 128), 1)).astype(BF)
        dls[...] += nn((x32 * wq).astype(BF), sel)
        heads = (lax.div(iota((CH, 128), 0), 64) + 4 * step == iota((CH, 128), 1)).astype(F32)
        both = jnp.broadcast_to(jnp.sum(g32 * x32, axis=0, keepdims=True), (8, CH))
        both = lax.dot_general(both, heads, (((1,), (0,)), ((), ())), precision=HI, preferred_element_type=F32)
        small[SMALL_AT + 10 : SMALL_AT + 11, 0:128] += both[0:1, :]
        total = through_conv(dx[...] + wq + skip[...] * g32)
        emit(total[HALO:], total[:HALO])

    @pl.when(step == NCH - 1)
    def _():
        dact = dbc[...] + jnp.concatenate([dbs[...], dcs[...]], axis=1)
        total = through_conv(jnp.concatenate([dact, jnp.zeros((T, 128), F32)], axis=1))
        v = pre[HALO:, 128:].astype(F32) + bias[...]
        dt = jnp.maximum(v, 0.0) + jnp.log1p(jnp.exp(-jnp.abs(v)))
        sg = sigm(v)
        a = -jnp.exp(alog[...])
        ratio = jnp.where(v < -15.0, 1.0, sg / jnp.maximum(dt, 1e-30))
        isf = iota((T, 128), 1) < HEADS
        rs = rsum[...].T
        cs = csum[...]
        first = flag[0] == 0
        seam = dls[...] + dlr[...]
        dp = jnp.where(isf, rs - cs, cs - rs) + jnp.where(first, -1.0, 1.0) * seam
        tot = jnp.where(first, 1.0, 0.0) * jnp.sum(seam, axis=0, keepdims=True)
        inc = exact((iota((T, T), 0) <= iota((T, T), 1)).astype(F32), dp)
        dl = jnp.where(isf, inc, inc - dp) + tot
        suffix = (iota((Q, Q), 0) <= iota((Q, Q), 1)).astype(F32)
        head = iota((Q, 128), 1) < HEADS
        offs = []
        for k in range(T // Q):
            ro, co = roff[k * Q : (k + 1) * Q, :], coff[k * Q : (k + 1) * Q, :]
            sums = exact(suffix, jnp.concatenate([ro, co], axis=1))
            sr, sco = sums[:, :128], sums[:, 128:]
            fwd = sr + (sco[0:1] - sco)
            rev = (sr[0:1] - sr + ro) + (sco - co)
            offs.append(jnp.where(head, fwd, rev) + dkeep[k : k + 1, :])
        dl = dl + jnp.concatenate(offs, axis=0)
        dv = dl * a * sg + (cs + coff[...] + dls[...]) * ratio
        emit(jnp.concatenate([total[HALO:, :128], dv], axis=1), total[:HALO])

        at = SMALL_AT
        small[at : at + 1, 0:128] = jnp.sum(dv, axis=0, keepdims=True)
        small[at : at + 1, 128:] = jnp.sum(dl * dt * a, axis=0, keepdims=True)
        for q in range(INNER // CH):
            small[at + 1 + q : at + 2 + q, :] = ggain[:, CH * q : CH * (q + 1)]
        small_o[...] = small[...].astype(BF)


def unproject(flag, dx, g, act, z, pre, conv_w, rows, dst, b, normt, nh, skip, bias, alog,
              rsum, csum, roff, coff, dkeep, dbc, dcs, dlr, ggain):
    T = dx.shape[0]
    E = T + HALO
    col = lambda rows: pl.BlockSpec((rows, CH), lambda i: (0, i))
    xcol = lambda rows: pl.BlockSpec((rows, CH), lambda i: (0, jnp.minimum(i, NCH - 2)))
    shapes = [((NCH, D, CH), BF), ((T, NCH * CH), BF), ((HALO, NCH * CH), BF), ((SMALL, CH), BF)]
    return pl.pallas_call(
        functools.partial(unproject_kernel, T),
        grid=(NCH,),
        in_specs=[SMEM_SPEC, xcol(T), xcol(T), xcol(T), col(T), col(E), col(CONV), full((PAIRS, 16, T)),
                  xcol(64), full((T, 64)), full((D, T)), full((HALO, D)), xcol(1), full((1, 128)), full((1, 128)),
                  full((128, T)), full((T, 128)), full((T, 128)), full((T, 128)), full((8, 128)), full((T, 128)),
                  full((T, 64)), full((T, 128)), full((1, INNER))],
        out_specs=[pl.BlockSpec((1, D, CH), lambda i: (i, 0, 0)), col(T), col(HALO), full((SMALL, CH))],
        out_shape=[jax.ShapeDtypeStruct(s, d) for s, d in shapes],
        scratch_shapes=[pltpu.VMEM((D, 128), BF), pltpu.VMEM((E, CH), F32),
                        pltpu.VMEM((128, CH), BF), pltpu.VMEM((T, 64), F32), pltpu.VMEM((T, 128), F32),
                        pltpu.VMEM((SMALL, CH), F32), pltpu.VMEM((T // Q, (CONV - 1) * Q, Q + HALO), BF),
                        pltpu.VMEM((T // Q, (CONV - 1) * (Q + HALO), Q), BF)],
        compiler_params=params(),
        name="unproject",
    )(flag, dx, g, act, z, pre, conv_w, rows, dst, b, normt, nh, skip, bias, alog, rsum, csum, roff, coff, dkeep, dbc, dcs, dlr,
      ggain)


BOTH = ("dir", "dp")


def width(axis):
    return lax.axis_size(axis).bit_length() - 1


def exchange(v, mask_even, mask_odd):
    size = lax.axis_size("dir") * lax.axis_size("dp")
    return lax.ppermute(v, BOTH, [(i, i ^ (mask_odd if i & 1 else mask_even)) for i in range(size)])


def side_of(mask_even, mask_odd):
    me = lax.axis_index(BOTH)
    return jnp.where(me % 2 == 0, me & mask_even, me & mask_odd) != 0


def swap(v):
    mask = lax.axis_size("dp")
    return exchange(v, mask, mask)


def gather_rows(shard, ready, rest):
    bits = width("dp")
    down = list(range(bits - 1, 0, -1))
    even, odd = down, down[-1:] + down[:-1]
    out = shard
    for done, (e, o) in enumerate(zip(even, odd)):
        out = grow(out, done, e, o)
        if done == 0:
            out, rest = lax.optimization_barrier((out, rest))
        if done == 1:
            out, ready = lax.optimization_barrier((out, ready))
    return gather_finish(out, shard.shape), ready, rest


def grow(out, done, e, o):
    other = exchange(out, 1 << e, 1 << o)
    high = side_of(1 << e, 1 << o)
    return jnp.stack([jnp.where(high, other, out), jnp.where(high, out, other)], axis=done)


def gather_finish(out, shape):
    bits = width("dp")
    if bits == 0:
        return out
    other = exchange(out, 1, 1)
    high = side_of(1, 1)
    first = jnp.where(high, other, out)
    second = jnp.where(high, out, other)
    lead = max(bits - 1, 0)
    if lead > 1:
        second = jnp.moveaxis(second, 0, lead - 1)
    return jnp.stack([first, second], axis=lead).reshape((-1,) + shape[1:])


def halves(v, high, axis=0):
    n = v.shape[axis] // 2
    at = jnp.where(high, n, 0)
    return lax.dynamic_slice_in_dim(v, at, n, axis), lax.dynamic_slice_in_dim(v, n - at, n, axis)


def add(p, q):
    return (p.astype(F32) + q.astype(F32)).astype(BF)


def reduce_all(main, small, later, inputs):
    bits = width("dp")
    masks = [1 << b for b in [bits] * width("dir") + list(range(1, bits))]
    odd = list(masks)
    for i in range(0, len(masks) - 1, 2):
        odd[i], odd[i + 1] = masks[i + 1], masks[i]
    order = list(zip(masks, odd))
    core = side_of(1, 1)
    if bits:
        (keep, send), (keep_s, send_s) = halves(main, core, 1), halves(small, core)
        main, small = add(keep, exchange(send, 1, 1)), add(keep_s, exchange(send_s, 1, 1))
    buf = jnp.concatenate([main.reshape(-1, CH), small], axis=0)
    if order:
        keep, send = halves(buf, side_of(*order[0]))
        send, inputs = lax.optimization_barrier((send, inputs))
        got = exchange(send, *order[0])
    extra, beside = later(*inputs)
    if order:
        for at, pair in enumerate(order[1:]):
            high = side_of(*pair)
            (keep, send), (got, got_send) = halves(keep, high), halves(got, high)
            send = add(send, got_send)
            if at == 0:
                send, extra = lax.optimization_barrier((send, extra))
            keep, got = add(keep, got), exchange(send, *pair)
        buf = add(keep, got)
    for at, pair in enumerate(reversed(order)):
        n = buf.shape[0]
        if at == len(order) - 1:
            buf, beside = lax.optimization_barrier((buf, beside))
        got = exchange(jnp.concatenate([buf, extra], axis=0), *pair)
        extra = add(extra, got[n:])
        high = side_of(*pair)
        buf = jnp.concatenate([jnp.where(high, got[:n], buf), jnp.where(high, buf, got[:n])], axis=0)
    if not bits:
        rows = NCH * D
        both = buf[:rows].reshape(NCH, 2, D // 2, CH)
        parts = [jnp.concatenate([both[:, q].reshape(rows // 2, CH), buf[rows : rows + (buf.shape[0] - rows) // 2], e], axis=0)
                 for q, e in ((0, extra), (1, jnp.zeros_like(extra)))]
        return parts[0], parts[1], jnp.zeros((1,), jnp.int32), beside
    buf = jnp.concatenate([buf, extra], axis=0)
    return buf, exchange(buf, 1, 1), core.astype(jnp.int32)[None], beside


def late_kernel(core, own, other, own_l, other_l, own_s, other_s, own_e, other_e, zx_o, bc_o, dt_o, cw_o, cb_o, dtb_o, alog_o,
                skip_o, og_o, ng_o):
    half = D // 2
    first = core[0] == 0
    upper = jnp.where(first, own[...], other[...]).astype(F32)
    lower = jnp.where(first, other[...], own[...]).astype(F32)
    for q in range(2):
        zx_o[0:half, CH * q : CH * (q + 1)] = upper[half * q : half * (q + 1)]
        zx_o[half:, CH * q : CH * (q + 1)] = lower[half * q : half * (q + 1)]

    @pl.when(pl.program_id(0) == 0)
    def _():
        tail = jnp.concatenate([jnp.where(first, own_l[...], other_l[...]), jnp.where(first, other_l[...], own_l[...])], axis=0)
        tail = tail.astype(F32)
        bc_o[...] = tail[:, :128]
        dt_o[...] = tail[:, 128:].T[: 2 * HEADS, :]
        sm = jnp.where(first, own_s[...], other_s[...]).astype(F32)
        for q in range(NCH):
            n = CH if q < NCH - 1 else 2 * STATE
            cw_o[:, CH * q : CH * q + n] = sm[CONV * q : CONV * (q + 1), :n]
            cb_o[CH * q : CH * q + n] = sm[CONV * NCH + q, :n]
        at = SMALL_AT
        dtb_o[...] = sm[at, : 2 * HEADS]
        alog_o[...] = sm[at, 128 : 128 + 2 * HEADS]
        for q in range(INNER // CH):
            og_o[CH * q : CH * (q + 1)] = sm[at + 1 + q, :]
        ng = own_e[...].astype(F32) + other_e[...].astype(F32)
        for q in range(D // CH):
            ng_o[CH * q : CH * (q + 1)] = ng[q, :]
        skip_o[...] = sm[at + 10, :HEADS]


def late(core, own, other):
    n = INNER // CH // 2
    taps = INNER + 2 * STATE
    shapes = [(D, 2 * INNER), (D, 2 * STATE), (2 * HEADS, D), (CONV, taps), (taps,), (2 * HEADS,), (2 * HEADS,), (HEADS,),
              (INNER,), (D,)]
    two = pl.BlockSpec((D, CH), lambda i: (i, 0))
    last = pl.BlockSpec((D // 2, CH), lambda i: (NCH - 1, 0))
    small = pl.BlockSpec((SMALL, CH), lambda i: (NCH * D // (2 * SMALL), 0))
    end = own.shape[0] // EXTRA - 1
    extra = pl.BlockSpec((EXTRA, CH), lambda i: (end, 0))
    return pl.pallas_call(
        late_kernel,
        grid=(n,),
        in_specs=[SMEM_SPEC, two, two, last, last, small, small, extra, extra],
        out_specs=[pl.BlockSpec((D, 2 * CH), lambda i: (0, n + i))] + [full(v) for v in shapes[1:]],
        out_shape=[jax.ShapeDtypeStruct(v, F32) for v in shapes],
        compiler_params=params(),
        name="late",
    )(core, own, other, own, other, own, other, own, other)


def early_kernel(wg, wo, zx, zx_o, wo_o):
    zx_o[...] = wg[...].astype(F32)
    wo_o[...] = wo[...].astype(F32).T


def early(wg, wo, zx):
    n = INNER // CH // 2
    row = pl.BlockSpec((2 * CH, D), lambda i: (i, 0))
    col = pl.BlockSpec((D, 2 * CH), lambda i: (0, i))
    return pl.pallas_call(
        early_kernel,
        grid=(n,),
        in_specs=[col, col, pl.BlockSpec(memory_space=pl.ANY)],
        out_specs=[col, row],
        out_shape=[jax.ShapeDtypeStruct((D, 2 * INNER), F32), jax.ShapeDtypeStruct((INNER, D), F32)],
        input_output_aliases={2: 0},
        compiler_params=params(),
        name="early",
    )(wg, wo, zx)


def apart(flag, part, args):
    def nothing(v):
        return jax.tree.map(lambda o: jnp.zeros(o.shape, o.dtype), jax.eval_shape(part, v))

    return lax.cond(flag[1] >= 1, part, nothing, args)


def body(tokens, norm_gain, w_zx, w_bc, w_dt, conv_w, conv_b, dt_bias, a_log, d_skip, out_gain, w_out, doc_lengths, out_grad):
    T = tokens.shape[1]
    devices = lax.axis_size("dir") * lax.axis_size("dp")
    side = lax.axis_index("dir")
    tok = tokens.reshape(T, D)
    og = out_grad.reshape(T, D)
    shard = w_zx.shape[0]
    half = INNER // 2
    mine = jnp.concatenate([w_zx[:, INNER:], w_bc, w_dt, jnp.zeros((shard, 128 - 2 * HEADS), BF)], axis=1)
    halo = lax.ppermute(tok[T - HALO :], "dir", [(0, 1)])
    flag = jnp.concatenate([side[None].astype(jnp.int32), doc_lengths[0]])
    wide = NCH * CH
    cw = jnp.pad(conv_w, ((0, 0), (0, wide - conv_w.shape[1])))
    cb = jnp.pad(conv_b, (0, wide - conv_b.shape[0]))[None]
    lanes = lambda v: jnp.pad(v, (0, 128 - v.shape[0]))[None]
    skip = jnp.repeat(d_skip, HEADDIM)[None]
    rest = jnp.concatenate([w_zx[:, :half], w_zx[:, half:INNER], w_out], axis=0)
    ready = (halo, flag, cw, cb, lanes(dt_bias), lanes(a_log), skip, norm_gain[None], out_gain[None], og.T)
    w1, ready, rest = gather_rows(mine, ready, rest)

    def finish(v):
        (flag, b, bt, c, ct, uv, keep, table, act, gm, z, pre, w1, cw, normt, nh, skip, bias, alog, tok, halo, ggain, og, gain_in,
         no, gg, wrc, st_in, rest) = v
        dcs, dlr, dst = aside(flag, gm, wrc, c, ct, st_in)
        dst_in = swap(dst)
        dx, rsum, csum, roff, coff, dkeep, dbc = unmix(flag, b, bt, c, ct, uv, keep, table, act, gm)
        dw1, dpl, dph, small = unproject(flag, dx, gm, act, z, pre, cw, table, dst_in, b, normt, nh, skip, bias, alog,
                                         rsum, csum, roff, coff, dkeep, dbc, dcs, dlr, ggain)
        rows = NCH * D
        total = -(-(rows + SMALL) // (16 * devices)) * 16 * devices
        small = jnp.pad(small, ((0, total - rows - SMALL), (0, 0)))

        def later(dpl, dph):
            bo, gn, gnh, part = deferred(dpl, dph, w1, gg, no, rest, tok, halo)
            back = lax.ppermute(gnh, "dir", [(1, 0)])
            gn = gn + jnp.pad(back, ((T - HALO, 0), (0, 0)))
            x32 = tok.astype(F32)
            rho = lax.rsqrt(jnp.mean(x32 * x32, axis=1, keepdims=True) + EPS)
            e_in = gn * gain_in
            gx = rho * e_in - x32 * (rho * rho * rho * jnp.mean(e_in * x32, axis=1, keepdims=True))
            return part, (bo, (og.astype(F32) + gx).astype(BF))

        own, other, core, (bo, grad_tokens) = reduce_all(dw1, small, later, (dpl, dph))
        return (bo, grad_tokens) + tuple(late(core, own, other))

    def rest_of(v):
        w1, rest, (halo, flag, cw, cb, bias, alog, skip, gain_in, gain_out, ogt), tok, og = v
        rest = lax.all_gather(rest, "dp", axis=0, tiled=False)
        if shard % 16:
            rest = jnp.concatenate([rest[:, :shard].reshape(D, D), rest[:, shard : 2 * shard].reshape(D, D),
                                    rest[:, 2 * shard :].reshape(INNER, D)], axis=0)[None]
        normed, normt, nh, pre, z, act, rows, wrc, uv, keep, b, bt, c, ct, st = project(
            flag, tok, halo, gain_in, w1, cw, cb, bias, alog)
        st_in = swap(st)
        y = mix(flag, b, bt, c, uv, keep, rows, act, skip)
        no, gg, gm, dwg, dwo, ggain = gate(y, wrc, c, st_in, normed, normt, rest, og, ogt, gain_out)
        dwo, dwg = lax.psum((dwo, dwg), BOTH)
        args = (flag, b, bt, c, ct, uv, keep, rows, act, gm, z, pre, w1, cw, normt, nh, skip, bias, alog, tok, halo, ggain, og,
                gain_in, no, gg, wrc, st_in, rest)
        bo, grad_tokens, zx, g_bc, g_dt, g_cw, g_cb, g_dtb, g_alog, g_skip, g_og, g_ng = apart(flag, finish, args)
        zx, g_wo = early(dwg, dwo, zx)
        return bo, grad_tokens, g_ng, zx, g_bc, g_dt.T, g_cw, g_cb, g_dtb, g_alog, g_skip, g_og, g_wo

    outs = rest_of((w1, rest, ready, tok, og))
    return (outs[0].reshape(tokens.shape), outs[1].reshape(tokens.shape)) + tuple(outs[2:])


def solution(mesh):
    rows, weight, whole = P("dp", "dir", None), P("dp", None), P()
    placed = (rows, whole, weight, weight, weight, whole, whole, whole, whole, whole, whole, weight, weight, rows)
    return jax.shard_map(body, mesh=mesh, in_specs=placed, out_specs=(rows, rows) + (whole,) * 11, check_vma=False)
```

```python
import functools

import jax
import jax.numpy as jnp
from jax import lax
from jax.experimental import pallas as pl
from jax.experimental.pallas import tpu as pltpu
from jax.sharding import PartitionSpec as P

D = 768
HEADS = 24
HEADDIM = 64
STATE = 64
INNER = 1536
CONV = 4
NDOC = 4
PAIRS = HEADS // 2
HALO = 16
CH = 256
NCH = 7
Q = 128
GROUP = CH // HEADDIM
SMALL_AT = (CONV + 1) * NCH
SMALL = 64
EXTRA = 16
EPS = 1e-05
LOG2E = 1.4426950408889634
BF = jnp.bfloat16
F32 = jnp.float32
HI = lax.Precision.HIGHEST


def nn(a, b):
    return lax.dot_general(a, b, (((1,), (0,)), ((), ())), preferred_element_type=F32)


def nt(a, b):
    return lax.dot_general(a, b, (((1,), (1,)), ((), ())), preferred_element_type=F32)


def iota(shape, axis):
    return lax.broadcasted_iota(jnp.int32, shape, axis)


def sigm(v):
    return 1.0 / (1.0 + jnp.exp(-v))


def lane_pair(col_a, col_b, rows):
    return jnp.where(iota((rows, 128), 1) < 64, col_a, col_b)


def params(mib=60):
    return pltpu.CompilerParams(
        dimension_semantics=("arbitrary",), vmem_limit_bytes=mib * 1024 * 1024
    )


def full(shape):
    return pl.BlockSpec(shape, lambda i: tuple(0 for _ in shape))


SMEM_SPEC = pl.BlockSpec(memory_space=pltpu.SMEM)


def doc_ids(flag, places):
    total = jnp.zeros(places.shape, jnp.int32)
    end = 0
    for k in range(NDOC):
        end = end + flag[1 + k]
        total = total + jnp.where(places >= end, 1, 0)
    return jnp.where(places < 0, -1, total)


def doc_at(flag, place):
    total = 0
    end = 0
    for k in range(NDOC):
        end = end + flag[1 + k]
        total = total + jnp.where(place >= end, 1, 0)
    return total


def doc_col(flag, T, lead=0):
    return doc_ids(flag, iota((T + lead, 1), 0) + (flag[0] * T - lead))


def doc_row(flag, T):
    return doc_ids(flag, iota((1, T), 1) + flag[0] * T)


def project_kernel(T, flag, tok, halo, gain, w, cw, cb, bias, alog,
                   norm_o, normt_o, nh_o, pre_o, z_o, act_o, rows_o, wrc_o, uv_o, keep_o, b_o, bt_o, c_o, ct_o, st_o, ncat, pf, segc):
    step = pl.program_id(0)

    @pl.when(step == 0)
    def _():
        def norm(v):
            v = v.astype(F32)
            ms = jnp.mean(v * v, axis=1, keepdims=True)
            return (v * lax.rsqrt(ms + EPS) * gain[...]).astype(BF)

        nh = norm(halo[...])
        own = norm(tok[...])
        nh_o[...] = nh
        norm_o[...] = own
        normt_o[...] = own.astype(F32).T.astype(BF)
        ncat[0:HALO, :] = nh
        ncat[HALO:, :] = own
        segc[...] = doc_col(flag, T, HALO)

    proj = nn(ncat[...], w[...]).astype(BF)
    pre_o[...] = proj
    pf[...] = proj.astype(F32)
    segs = segc[...]
    here = segs[HALO:, :]
    z = cb[...] + cw[CONV - 1 : CONV, :] * pf[HALO:, :]
    for k in range(1, CONV):
        same = segs[HALO - k : HALO + T - k, :] == here
        z = z + jnp.where(same, cw[CONV - 1 - k : CONV - k, :] * pf[HALO - k : HALO + T - k, :], 0.0)
    z_o[...] = z.astype(BF)
    act = z * sigm(z)
    act_o[...] = act.astype(BF)

    @pl.when(step == 0)
    def _():
        bc = act[:, :128]
        b_o[...] = bc[:, :64].astype(BF)
        c_o[...] = bc[:, 64:].astype(BF)
        bct = bc.T
        bt_o[...] = bct[:64, :].astype(BF)
        ct_o[...] = bct[64:, :].astype(BF)
        v = pf[HALO:, 128:] + bias[...]
        dt = jnp.maximum(v, 0.0) + jnp.log1p(jnp.exp(-jnp.abs(v)))
        rate = dt * (-LOG2E * jnp.exp(alog[...]))
        rate_t = rate.T
        dt_t = dt.T
        upto = (iota((T, T), 0) <= iota((T, T), 1)).astype(F32)
        inc = lax.dot_general(rate_t, upto, (((1,), (0,)), ((), ())), precision=HI, preferred_element_type=F32)
        isf = iota((128, T), 0) < HEADS
        cum = jnp.where(isf, inc, inc - rate_t)
        ldt = jnp.log2(jnp.maximum(dt_t, 1e-37))
        key = jnp.where(isf, cum - ldt, cum + ldt)
        segv = doc_row(flag, T)
        left, right = doc_at(flag, T - 1), doc_at(flag, T)
        send_f = jnp.where(segv == left, jnp.exp2(cum[:, T - 1 :] - key), 0.0)
        send_b = jnp.where(segv == right, jnp.exp2(key), 0.0)
        recv_f = jnp.where(segv == left, jnp.exp2(cum), 0.0)
        recv_b = jnp.where(segv == right, jnp.exp2(inc[:, T - 1 :] - cum), 0.0)
        first = flag[0] == 0
        send = jnp.where(first, send_f[0:HEADS], send_b[HEADS : 2 * HEADS])
        recv = jnp.where(first, recv_b[HEADS : 2 * HEADS], recv_f[0:HEADS])
        for p in range(PAIRS):
            f, r = 2 * p, HEADS + 2 * p
            rows_o[p, 0:2, :] = cum[f : f + 2]
            rows_o[p, 2:4, :] = cum[r : r + 2]
            rows_o[p, 4:6, :] = key[f : f + 2]
            rows_o[p, 6:8, :] = key[r : r + 2]
            rows_o[p, 8:10, :] = send[f : f + 2]
            rows_o[p, 10:12, :] = recv[f : f + 2]
            rows_o[p, 12:16, :] = jnp.zeros((4, T), F32)
        recv_pad = jnp.concatenate([recv, jnp.zeros((128 - HEADS, T), F32)], axis=0)
        wrc_o[...] = recv_pad.T.astype(BF)
        cum_f, cum_r = cum[0:HEADS], cum[HEADS : 2 * HEADS]
        key_f, key_r = key[0:HEADS], key[HEADS : 2 * HEADS]
        quads = [[], [], [], []]
        none = jnp.zeros((HEADS, Q), F32)
        lane = iota((HEADS, 128), 1)
        keep_f = jnp.zeros((HEADS, 128), F32)
        keep_r = jnp.zeros((HEADS, 128), F32)
        for k in range(T // Q):
            lo, hi = k * Q, (k + 1) * Q
            sg = segv[:, lo:hi]
            before = cum_f[:, lo - 1 : lo] if k > 0 else None
            after = cum_r[:, hi : hi + 1] if hi < T else None
            quads[0].append(none if k == 0 else jnp.where(sg == segv[:, lo - 1 : lo], jnp.exp2(cum_f[:, lo:hi] - before), 0.0))
            quads[1].append(jnp.where(sg == segv[:, hi - 1 : hi], jnp.exp2(cum_f[:, hi - 1 : hi] - key_f[:, lo:hi]), 0.0))
            quads[2].append(none if hi == T else jnp.where(sg == segv[:, hi : hi + 1], jnp.exp2(after - cum_r[:, lo:hi]), 0.0))
            quads[3].append(jnp.where(sg == segv[:, lo : lo + 1], jnp.exp2(key_r[:, lo:hi] - cum_r[:, lo : lo + 1]), 0.0))
            if k > 0:
                through = jnp.where(segv[:, lo - 1 : lo] == segv[:, hi - 1 : hi], jnp.exp2(cum_f[:, hi - 1 : hi] - before), 0.0)
                keep_f = jnp.where(lane == k, through, keep_f)
            if hi < T:
                through = jnp.where(segv[:, lo : lo + 1] == segv[:, hi : hi + 1], jnp.exp2(after - cum_r[:, lo : lo + 1]), 0.0)
                keep_r = jnp.where(lane == k, through, keep_r)
        quads = [jnp.concatenate(v, axis=1) for v in quads]
        uv_o[...] = jnp.concatenate(quads + [jnp.zeros((128 - 4 * HEADS, T), F32)], axis=0).T.astype(BF)
        keeps = jnp.concatenate([keep_f, keep_r, jnp.zeros((128 - 2 * HEADS, 128), F32)], axis=0).T
        keep_o[...] = keeps[0:8, :]

    @pl.when(step > 0)
    def _():
        for j in range(CH // 128):
            cols = rows_o[2 * (step - 1) + j, 8:16, :].T
            wide = lane_pair(cols[:, 0:1], cols[:, 1:2], T)
            xw = (act[:, 128 * j : 128 * (j + 1)] * wide).astype(BF)
            st_o[:, 128 * j : 128 * (j + 1)] = nn(bt_o[...], xw).astype(BF)


def project(flag, tok, halo, gain, w1, conv_w, conv_b, bias, alog):
    T = tok.shape[0]
    E = T + HALO
    chunk = lambda i: lax.rem(i + NCH - 1, NCH)
    xchunk = lambda i: jnp.maximum(i - 1, 0)
    col = lambda rows: pl.BlockSpec((rows, CH), lambda i: (0, chunk(i)))
    shapes = [
        ((T, D), BF), ((D, T), BF), ((HALO, D), BF), ((E, NCH * CH), BF), ((T, NCH * CH), BF), ((T, NCH * CH), BF),
        ((PAIRS, 16, T), F32), ((T, 128), BF), ((T, 128), BF), ((8, 128), F32), ((T, 64), BF), ((64, T), BF), ((T, 64), BF), ((64, T), BF),
        ((64, INNER), BF),
    ]
    out_specs = [
        full((T, D)), full((D, T)), full((HALO, D)), col(E), col(T), col(T), full((PAIRS, 16, T)), full((T, 128)), full((T, 128)), full((8, 128)), full((T, 64)),
        full((64, T)), full((T, 64)), full((64, T)), pl.BlockSpec((64, CH), lambda i: (0, xchunk(i))),
    ]
    return pl.pallas_call(
        functools.partial(project_kernel, T),
        grid=(NCH,),
        in_specs=[SMEM_SPEC, full((T, D)), full((HALO, D)), full((1, D)), col(D), col(CONV), col(1),
                  full((1, 128)), full((1, 128))],
        out_specs=out_specs,
        out_shape=[jax.ShapeDtypeStruct(s, d) for s, d in shapes],
        scratch_shapes=[pltpu.VMEM((E, D), BF), pltpu.VMEM((E, CH), F32), pltpu.VMEM((E, 1), jnp.int32)],
        compiler_params=params(),
        name="project",
    )(flag, tok, halo, gain, w1, conv_w, conv_b, bias, alog)


def shift_matrix(flag, T, lo):
    first = flag[0] * T + lo
    own = doc_ids(flag, iota((Q, 1), 0) + first)
    from_doc = doc_ids(flag, iota((1, Q + HALO), 1) + (first - HALO))
    gap = iota((Q, Q + HALO), 0) + HALO - iota((Q, Q + HALO), 1)
    return jnp.concatenate([((gap == k) & (own == from_doc)).astype(F32) for k in range(1, CONV)], axis=0).astype(BF)


def shift_back_matrix(flag, T, lo):
    first = flag[0] * T + lo
    own = doc_ids(flag, iota((1, Q), 1) + first)
    from_doc = doc_ids(flag, iota((Q + HALO, 1), 0) + (first - HALO))
    gap = iota((Q + HALO, Q), 1) + HALO - iota((Q + HALO, Q), 0)
    return jnp.concatenate([((gap == k) & (own == from_doc)).astype(F32) for k in range(1, CONV)], axis=0).astype(BF)


def same_doc(flag, T, lo):
    first = flag[0] * T + lo
    a = doc_ids(flag, iota((Q, 1), 0) + first)
    b = doc_ids(flag, iota((1, Q), 1) + first)
    return (a == b) & (iota((Q, Q), 0) != iota((Q, Q), 1))


def spread_of(step, slot, dtype=BF):
    base = slot * HEADS + GROUP * step
    return (lax.div(iota((128, CH), 1), HEADDIM) + base == iota((128, CH), 0)).astype(dtype)


def exact(a, b):
    return lax.dot_general(a, b, (((1,), (0,)), ((), ())), precision=HI, preferred_element_type=F32)


def states(T, bt, vf, vr, keep_f, keep_r):
    n = T // Q
    ahead, back = [None] * n, [None] * n
    for k in range(1, n):
        new = nn(bt[:, (k - 1) * Q : k * Q], vf[(k - 1) * Q : k * Q])
        ahead[k] = new if k == 1 else new + keep_f[k - 1 : k] * ahead[k - 1]
    for k in reversed(range(n - 1)):
        new = nn(bt[:, (k + 1) * Q : (k + 2) * Q], vr[(k + 1) * Q : (k + 2) * Q])
        back[k] = new if k == n - 2 else new + keep_r[k + 1 : k + 2] * back[k + 1]
    return ahead, back


def mix_kernel(T, flag, b, bt, c, uv, keep, rows, x, skip, y_o, sc):
    step = pl.program_id(0)
    n = T // Q

    @pl.when(step == 0)
    def _():
        for i in range(n):
            lo, hi = i * Q, (i + 1) * Q
            sc[i] = jnp.where(same_doc(flag, T, lo), nt(c[lo:hi, :], b[lo:hi, :]), 0.0)

    x4 = x[...]
    x32 = x4.astype(F32)
    table = uv[...]
    uf, vf, ur, vr = [nn(table, spread_of(step, slot)) for slot in range(4)]
    keep_f = exact(keep[...], spread_of(step, 0, F32))
    keep_r = exact(keep[...], spread_of(step, 1, F32))
    ahead, back = states(T, bt, (vf * x32).astype(BF), (vr * x32).astype(BF), keep_f, keep_r)
    later = iota((Q, Q), 0) > iota((Q, Q), 1)
    lane = iota((Q, 128), 1) < HEADDIM
    cols = [rows[p][0:8].T for p in range(GROUP // 2)]
    for i in range(n):
        lo, hi = i * Q, (i + 1) * Q
        pieces = []
        for p in range(GROUP // 2):
            xs = x4[lo:hi, 128 * p : 128 * (p + 1)]
            outs = []
            for h in range(2):
                cf = cols[p][lo:hi, h : h + 1]
                cr = cols[p][lo:hi, 2 + h : 3 + h]
                kf = rows[p, 4 + h : 5 + h, lo:hi]
                kr = rows[p, 6 + h : 7 + h, lo:hi]
                m = sc[i] * jnp.exp2(jnp.where(later, cf - kf, kr - cr))
                outs.append(nn(m.astype(BF), xs))
            pieces.append(jnp.where(lane, outs[0], outs[1]))
        y = jnp.concatenate(pieces, axis=1) + skip[...] * x32[lo:hi]
        if i > 0:
            y = y + uf[lo:hi] * nn(c[lo:hi, :], ahead[i].astype(BF))
        if i < n - 1:
            y = y + ur[lo:hi] * nn(c[lo:hi, :], back[i].astype(BF))
        y_o[lo:hi, :] = y


def mix(flag, b, bt, c, uv, keep, rows, act, skip):
    T = b.shape[0]
    blk = pl.BlockSpec((T, CH), lambda i: (0, i))
    return pl.pallas_call(
        functools.partial(mix_kernel, T),
        grid=(INNER // CH,),
        in_specs=[SMEM_SPEC, full((T, 64)), full((64, T)), full((T, 64)), full((T, 128)), full((8, 128)),
                  pl.BlockSpec((GROUP // 2, 16, T), lambda i: (i, 0, 0)), blk, pl.BlockSpec((1, CH), lambda i: (0, i))],
        out_specs=blk,
        out_shape=jax.ShapeDtypeStruct((T, INNER), F32),
        scratch_shapes=[pltpu.VMEM((T // Q, Q, Q), F32)],
        compiler_params=params(),
        name="mix",
    )(flag, b, bt, c, uv, keep, rows, act, skip)


def seam_width(wrc):
    spread = (lax.div(iota((128, INNER), 1), HEADDIM) == iota((128, INNER), 0)).astype(BF)
    return nn(wrc[...], spread)


def gate_kernel(shard, y, wrc, c, st, normed, normt, rest, og, ogt, gain, no_o, gg_o, gm_o, dwg_o, dwo_o, ggain_o, acc_g, acc_o):
    step = pl.program_id(0)
    mixed = y[...] + nn(c[...], st[...]) * seam_width(wrc)
    half = INNER // 2
    own = normed[...]
    gz = jnp.concatenate([nn(own, rest[:, :shard, :].reshape(D, half)), nn(own, rest[:, shard : 2 * shard, :].reshape(D, half))],
                         axis=1)
    sig = sigm(gz)
    sil = gz * sig
    gated = mixed * sil
    rho = lax.rsqrt(jnp.mean(gated * gated, axis=1, keepdims=True) + EPS)
    no = (gated * rho * gain[...]).astype(BF)
    no_o[...] = no
    gno = nt(og[...], rest[:, 2 * shard :, :].reshape(INNER, D))
    e = gno * gain[...]
    part = jnp.sum(gno * gated * rho, axis=0, keepdims=True)
    mean_eg = jnp.mean(e * gated, axis=1, keepdims=True)
    ggated = rho * e - gated * (rho * rho * rho * mean_eg)
    gg = (ggated * mixed * sig * (1.0 + gz * (1.0 - sig))).astype(BF)
    gg_o[...] = gg
    gm_o[...] = (ggated * sil).astype(BF)
    dwg = nn(normt[...], gg)
    dwo = nn(ogt[...], no)

    @pl.when(step == 0)
    def _():
        acc_g[...] = dwg
        acc_o[...] = dwo
        ggain_o[...] = part

    @pl.when(step > 0)
    def _():
        dwg_o[...] = (acc_g[...] + dwg).astype(BF)
        dwo_o[...] = (acc_o[...] + dwo).astype(BF)
        ggain_o[...] += part


def gate(y, wrc, c, st, normed, normt, rest, og, ogt, gain):
    T = y.shape[0]
    rb = T // 2
    row = lambda n: pl.BlockSpec((rb, n), lambda i: (i, 0))
    col = lambda n: pl.BlockSpec((n, rb), lambda i: (0, i))
    shapes = [((T, INNER), BF), ((T, INNER), BF), ((T, INNER), BF), ((D, INNER), BF), ((D, INNER), BF), ((1, INNER), F32)]
    return pl.pallas_call(
        functools.partial(gate_kernel, rest.shape[1] // 4),
        grid=(2,),
        in_specs=[row(INNER), row(128), row(64), full((64, INNER)), row(D), col(D), full(rest.shape), row(D), col(D),
                  full((1, INNER))],
        out_specs=[row(INNER), row(INNER), row(INNER), full((D, INNER)), full((D, INNER)), full((1, INNER))],
        out_shape=[jax.ShapeDtypeStruct(v, d) for v, d in shapes],
        scratch_shapes=[pltpu.VMEM((D, INNER), F32), pltpu.VMEM((D, INNER), F32)],
        compiler_params=params(),
        name="gate",
    )(y, wrc, c, st, normed, normt, rest, og, ogt, gain)


def side_kernel(flag, gm, wrc, c, ct, st, dcs_o, dlr_o, dst_o, acc):
    step = pl.program_id(0)
    gw = gm[...].astype(F32) * seam_width(wrc)
    seam = gw * nn(c[...], st[...])
    gw = gw.astype(BF)
    dcs_o[...] = nt(gw, st[...])
    shift = jnp.where(flag[0] == 0, HEADS, 0)
    gather = (lax.div(iota((INNER, 128), 0), HEADDIM) + shift == iota((INNER, 128), 1)).astype(BF)
    dlr_o[...] = nn(seam.astype(BF), gather)
    dst = nn(ct[...], gw)

    @pl.when(step == 0)
    def _():
        acc[...] = dst

    @pl.when(step > 0)
    def _():
        dst_o[...] = (acc[...] + dst).astype(BF)


def aside(flag, gm, wrc, c, ct, st):
    T = gm.shape[0]
    rb = T // 2
    row = lambda n: pl.BlockSpec((rb, n), lambda i: (i, 0))
    shapes = [((T, 64), F32), ((T, 128), F32), ((64, INNER), BF)]
    return pl.pallas_call(
        side_kernel,
        grid=(2,),
        in_specs=[SMEM_SPEC, row(INNER), row(128), row(64), pl.BlockSpec((64, rb), lambda i: (0, i)), full((64, INNER))],
        out_specs=[row(64), row(128), full((64, INNER))],
        out_shape=[jax.ShapeDtypeStruct(v, d) for v, d in shapes],
        scratch_shapes=[pltpu.VMEM((64, INNER), F32)],
        compiler_params=params(),
        name="side",
    )(flag, gm, wrc, c, ct, st)


def deferred_kernel(shard, dpl, dph, w1, gg, no, rest, tok, halo, bo_o, gn_o, gnh_o, part_o, acc):
    step = pl.program_id(0)
    half = INNER // 2

    def unit(v):
        v = v.astype(F32)
        return v * lax.rsqrt(jnp.mean(v * v, axis=1, keepdims=True) + EPS)

    bo_o[...] = (tok[...].astype(F32) + nn(no[...], rest[:, 2 * shard :, :].reshape(INNER, D))).astype(BF)
    gn = nt(dpl[...], w1[...])
    gn = gn + nt(gg[:, :half], rest[:, :shard, :].reshape(D, half))
    gn = gn + nt(gg[:, half:], rest[:, shard : 2 * shard, :].reshape(D, half))
    gn_o[...] = gn
    part = jnp.sum(gn * unit(tok[...]), axis=0, keepdims=True)

    @pl.when(step == 0)
    def _():
        gnh = nt(dph[...], w1[...])
        gnh_o[...] = gnh
        acc[0:1, :] = part + jnp.sum(gnh * unit(halo[...]), axis=0, keepdims=True)

    @pl.when(step > 0)
    def _():
        total = acc[0:1, :] + part
        rows = [total[:, CH * q : CH * (q + 1)] for q in range(D // CH)]
        part_o[...] = jnp.concatenate(rows + [jnp.zeros((EXTRA - D // CH, CH), F32)], axis=0).astype(BF)


def deferred(dpl, dph, w1, gg, no, rest, tok, halo):
    T = dpl.shape[0]
    rb = T // 2
    wide = NCH * CH
    row = lambda n: pl.BlockSpec((rb, n), lambda i: (i, 0))
    shapes = [((T, D), BF), ((T, D), F32), ((HALO, D), F32), ((EXTRA, CH), BF)]
    return pl.pallas_call(
        functools.partial(deferred_kernel, rest.shape[1] // 4),
        grid=(2,),
        in_specs=[row(wide), full((HALO, wide)), full((D, wide)), row(INNER), row(INNER), full(rest.shape), row(D),
                  full((HALO, D))],
        out_specs=[row(D), row(D), full((HALO, D)), full((EXTRA, CH))],
        out_shape=[jax.ShapeDtypeStruct(v, d) for v, d in shapes],
        scratch_shapes=[pltpu.VMEM((8, D), F32)],
        compiler_params=params(),
        name="deferred",
    )(dpl, dph, w1, gg, no, rest, tok, halo)


def unmix_kernel(T, flag, b, bt, c, ct, uv, keep, rows, x, g, dx_o, rsum_o, csum_o, roff_o, coff_o, dkeep_o, dbc_o,
                 sc, dsc, db, dc):
    step = pl.program_id(0)
    n = T // Q

    @pl.when(step == 0)
    def _():
        for i in range(n):
            lo, hi = i * Q, (i + 1) * Q
            sc[i] = jnp.where(same_doc(flag, T, lo), nt(b[lo:hi, :], c[lo:hi, :]), 0.0)
        dsc[...] = jnp.zeros((n, Q, Q), F32)
        db[...] = jnp.zeros((T, 64), F32)
        dc[...] = jnp.zeros((T, 64), F32)
        rsum_o[...] = jnp.zeros((128, T), F32)
        csum_o[...] = jnp.zeros((T, 128), F32)
        roff_o[...] = jnp.zeros((T, 128), F32)
        coff_o[...] = jnp.zeros((T, 128), F32)
        dkeep_o[...] = jnp.zeros((8, 128), F32)

    x4 = x[...]
    g4 = g[...]
    x32 = x4.astype(F32)
    g32 = g4.astype(F32)
    wide = nn(uv[...], jnp.concatenate([spread_of(step, slot) for slot in range(4)], axis=1))
    uf, vf, ur, vr = [wide[:, CH * q : CH * (q + 1)] for q in range(4)]
    keep_f = exact(keep[...], spread_of(step, 0, F32))
    keep_r = exact(keep[...], spread_of(step, 1, F32))
    vxf, vxr = (vf * x32).astype(BF), (vr * x32).astype(BF)
    ugf, ugr = (uf * g32).astype(BF), (ur * g32).astype(BF)
    ahead, back = states(T, bt, vxf, vxr, keep_f, keep_r)
    lane = iota((Q, 128), 1)
    half = lane < HEADDIM
    earlier = iota((Q, Q), 0) < iota((Q, Q), 1)
    base = GROUP * step
    slot = lax.div(iota((2 * CH, 128), 0), HEADDIM)
    gather = (jnp.where(slot < GROUP, slot, slot + HEADS - GROUP) + base == iota((2 * CH, 128), 1)).astype(BF)
    cols = [rows[p][0:8].T for p in range(GROUP // 2)]
    dahead, dback = [None] * (n + 1), [None] * (n + 1)
    for k in reversed(range(1, n)):
        own = nn(ct[:, k * Q : (k + 1) * Q], ugf[k * Q : (k + 1) * Q])
        dahead[k] = own if k == n - 1 else own + keep_f[k : k + 1] * dahead[k + 1]
    for k in range(n - 1):
        own = nn(ct[:, k * Q : (k + 1) * Q], ugr[k * Q : (k + 1) * Q])
        dback[k] = own if k == 0 else own + keep_r[k : k + 1] * dback[k - 1]
    through = [jnp.zeros((1, 2 * CH), F32)] * 8
    for k in range(1, n - 1):
        pf = jnp.sum(keep_f[k : k + 1] * ahead[k] * dahead[k + 1], axis=0, keepdims=True)
        pr = jnp.sum(keep_r[k : k + 1] * back[k] * dback[k - 1], axis=0, keepdims=True)
        through[k] = jnp.concatenate([pf, pr], axis=1)
    dkeep_o[...] += nn(jnp.concatenate(through, axis=0).astype(BF), gather)
    totals = [[] for _ in range(2 * GROUP)]
    r_off, c_off = [], []
    none = jnp.zeros((Q, CH), F32)
    for j in range(n):
        lo, hi = j * Q, (j + 1) * Q
        pieces = []
        stat = jnp.zeros((Q, 128), F32)
        for p in range(GROUP // 2):
            xs = x4[lo:hi, 128 * p : 128 * (p + 1)]
            gs = g4[lo:hi, 128 * p : 128 * (p + 1)]
            zero = jnp.zeros_like(xs)
            gts = nt(jnp.concatenate([jnp.where(half, xs, zero), jnp.where(half, zero, xs)], axis=0), gs)
            ms = []
            for h in range(2):
                cf = rows[p, h : h + 1, lo:hi]
                cr = rows[p, 2 + h : 3 + h, lo:hi]
                kf = cols[p][lo:hi, 4 + h : 5 + h]
                kr = cols[p][lo:hi, 6 + h : 7 + h]
                gt = gts[h * Q : (h + 1) * Q]
                d = jnp.exp2(jnp.where(earlier, cf - kf, kr - cr))
                m = sc[j] * d
                ms.append(m.astype(BF))
                dsc[j] += gt * d
                w = gt * m
                wf = jnp.where(earlier, w, 0.0)
                wr = w - wf
                at = base + 2 * p + h
                stat = stat + jnp.where(lane == at, jnp.sum(wf, axis=1, keepdims=True), 0.0)
                stat = stat + jnp.where(lane == at + HEADS, jnp.sum(wr, axis=1, keepdims=True), 0.0)
                totals[2 * p + h].append(jnp.sum(wf, axis=0, keepdims=True))
                totals[GROUP + 2 * p + h].append(jnp.sum(wr, axis=0, keepdims=True))
            out = nn(jnp.concatenate(ms, axis=0), gs)
            pieces.append(jnp.where(half, out[:Q], out[Q:]))
        dx = jnp.concatenate(pieces, axis=1)
        zero = jnp.zeros((STATE, CH), BF)
        into = jnp.concatenate([ahead[j].astype(BF) if j > 0 else zero, back[j].astype(BF) if j < n - 1 else zero], axis=1)
        outof = jnp.concatenate([dahead[j + 1].astype(BF) if j < n - 1 else zero, dback[j - 1].astype(BF) if j > 0 else zero],
                                axis=1)
        both_u = jnp.concatenate([ugf[lo:hi], ugr[lo:hi]], axis=1)
        both_v = jnp.concatenate([vxf[lo:hi], vxr[lo:hi]], axis=1)
        r_off.append((both_u.astype(F32) * nn(c[lo:hi, :], into)).astype(BF))
        dv = nn(b[lo:hi, :], outof)
        c_off.append((both_v.astype(F32) * dv).astype(BF))
        dx_o[lo:hi, :] = dx + vf[lo:hi] * dv[:, :CH] + vr[lo:hi] * dv[:, CH:]
        dc[lo:hi, :] += nt(both_u, into)
        db[lo:hi, :] += nt(both_v, outof)
        csum_o[lo:hi, :] += stat
    off = nn(jnp.concatenate(r_off + c_off, axis=0), gather)
    roff_o[...] += off[:T]
    coff_o[...] += off[T:]
    for q in range(2):
        for h in range(GROUP):
            rsum_o[pl.ds(HEADS * q + base + h, 1), :] = jnp.concatenate(totals[GROUP * q + h], axis=1)

    @pl.when(step == INNER // CH - 1)
    def _():
        for j in range(n):
            lo, hi = j * Q, (j + 1) * Q
            ds = jnp.where(same_doc(flag, T, lo), dsc[j], 0.0)
            dbc_o[lo:hi, 0:64] = db[lo:hi, :] + nn(ds.astype(BF), c[lo:hi, :])
            dbc_o[lo:hi, 64:128] = dc[lo:hi, :] + nn(ds.T.astype(BF), b[lo:hi, :])


def unmix(flag, b, bt, c, ct, uv, keep, rows, act, g):
    T = b.shape[0]
    n = T // Q
    blk = pl.BlockSpec((T, CH), lambda i: (0, i))
    shapes = [(T, INNER), (128, T), (T, 128), (T, 128), (T, 128), (8, 128), (T, 128)]
    return pl.pallas_call(
        functools.partial(unmix_kernel, T),
        grid=(INNER // CH,),
        in_specs=[SMEM_SPEC, full((T, 64)), full((64, T)), full((T, 64)), full((64, T)), full((T, 128)), full((8, 128)),
                  pl.BlockSpec((GROUP // 2, 16, T), lambda i: (i, 0, 0)), blk, blk],
        out_specs=[blk] + [full(v) for v in shapes[1:]],
        out_shape=[jax.ShapeDtypeStruct(v, F32) for v in shapes],
        scratch_shapes=[pltpu.VMEM((n, Q, Q), F32), pltpu.VMEM((n, Q, Q), F32), pltpu.VMEM((T, 64), F32),
                        pltpu.VMEM((T, 64), F32)],
        compiler_params=params(),
        name="unmix",
    )(flag, b, bt, c, ct, uv, keep, rows, act, g)


def unproject_kernel(T, flag, dx, g, act, z, pre, cw, rows, dst, b, nt_s, nh, skip, bias, alog,
                     rsum, csum, roff, coff, dkeep, dbc, dcs, dlr, ggain,
                     keep_o, send_o, dpl_o, dph_o, skeep_o, ssend_o,
                     ht_s, tot, hd_s, dbs, dls, small, shifts, shifts_back):
    step = pl.program_id(0)
    E = T + HALO
    first_core = flag[5] == 0

    @pl.when(step == 0)
    def _():
        for i in range(T // Q):
            shifts[i] = shift_matrix(flag, T, i * Q)
            shifts_back[i] = shift_back_matrix(flag, T, i * Q)
        small[...] = jnp.zeros((SMALL, CH), F32)
        pad = jnp.concatenate([nh[...].astype(F32), jnp.zeros((128 - HALO, D), F32)], axis=0)
        ht_s[...] = pad.T.astype(BF)
        hd_s[...] = jnp.zeros((128, CH), BF)
        dbs[...] = jnp.zeros((T, 64), F32)
        dls[...] = jnp.zeros((T, 128), F32)

    def through_conv(dact):
        tot[...] = jnp.zeros((E, CH), F32)
        g_b = jnp.zeros((1, CH), F32)
        g_w = [jnp.zeros((1, CH), F32) for _ in range(CONV)]
        wide = Q + HALO
        for i in range(T // Q):
            lo, hi = i * Q, (i + 1) * Q
            zz = z[lo:hi, :].astype(F32)
            sg = sigm(zz)
            dz = dact[lo:hi] * sg * (1.0 + zz * (1.0 - sg))
            moved = nn(shifts[i], pre[lo : hi + HALO, :])
            back = nn(shifts_back[i], dz.astype(BF))
            g_b = g_b + jnp.sum(dz, axis=0, keepdims=True)
            g_w[0] = g_w[0] + jnp.sum(dz * pre[lo + HALO : hi + HALO, :].astype(F32), axis=0, keepdims=True)
            part = jnp.zeros((wide, CH), F32)
            for k in range(1, CONV):
                g_w[k] = g_w[k] + jnp.sum(dz * moved[(k - 1) * Q : k * Q], axis=0, keepdims=True)
                part = part + cw[CONV - 1 - k : CONV - k, :] * back[(k - 1) * wide : k * wide]
            tot[lo : hi + HALO, :] += part
            tot[lo + HALO : hi + HALO, :] += cw[CONV - 1 : CONV, :] * dz
        small[pl.ds(CONV * NCH + step, 1), :] = g_b
        for k in range(CONV):
            small[pl.ds(CONV * step + CONV - 1 - k, 1), :] = g_w[k]
        return tot[...]

    def emit(local, halo):
        local = local.astype(BF)
        hd_s[0:HALO, :] = halo.astype(BF)
        dw = (nn(nt_s[...], local) + nn(ht_s[...], hd_s[...])).astype(BF)
        top, bottom = dw[: D // 2], dw[D // 2 :]
        keep_o[0] = jnp.where(first_core, top, bottom)
        send_o[0] = jnp.where(first_core, bottom, top)
        dpl_o[...] = local
        dph_o[...] = hd_s[0:HALO, :]

    @pl.when(step < NCH - 1)
    def _():
        wides = []
        for j in range(CH // 128):
            cols = rows[2 * step + j, 8:16, :].T
            wides.append(lane_pair(cols[:, 0:1], cols[:, 1:2], T))
        wide = jnp.concatenate(wides, axis=1)
        x32 = act[...].astype(F32)
        g32 = g[...].astype(F32)
        wq = wide * nn(b[...], dst[...])
        dbs[...] += nt((x32 * wide).astype(BF), dst[...])
        base = 4 * step + jnp.where(flag[0] == 0, 0, HEADS)
        sel = (lax.div(iota((CH, 128), 0), 64) + base == iota((CH, 128), 1)).astype(BF)
        dls[...] += nn((x32 * wq).astype(BF), sel)
        heads = (lax.div(iota((CH, 128), 0), 64) + 4 * step == iota((CH, 128), 1)).astype(F32)
        both = jnp.broadcast_to(jnp.sum(g32 * x32, axis=0, keepdims=True), (8, CH))
        both = lax.dot_general(both, heads, (((1,), (0,)), ((), ())), precision=HI, preferred_element_type=F32)
        small[SMALL_AT + 10 : SMALL_AT + 11, 0:128] += both[0:1, :]
        total = through_conv(dx[...] + wq + skip[...] * g32)
        emit(total[HALO:], total[:HALO])

    @pl.when(step == NCH - 1)
    def _():
        dact = dbc[...] + jnp.concatenate([dbs[...], dcs[...]], axis=1)
        total = through_conv(jnp.concatenate([dact, jnp.zeros((T, 128), F32)], axis=1))
        v = pre[HALO:, 128:].astype(F32) + bias[...]
        dt = jnp.maximum(v, 0.0) + jnp.log1p(jnp.exp(-jnp.abs(v)))
        sg = sigm(v)
        a = -jnp.exp(alog[...])
        ratio = jnp.where(v < -15.0, 1.0, sg / jnp.maximum(dt, 1e-30))
        isf = iota((T, 128), 1) < HEADS
        rs = rsum[...].T
        cs = csum[...]
        first = flag[0] == 0
        seam = dls[...] + dlr[...]
        dp = jnp.where(isf, rs - cs, cs - rs) + jnp.where(first, -1.0, 1.0) * seam
        tot = jnp.where(first, 1.0, 0.0) * jnp.sum(seam, axis=0, keepdims=True)
        inc = exact((iota((T, T), 0) <= iota((T, T), 1)).astype(F32), dp)
        dl = jnp.where(isf, inc, inc - dp) + tot
        suffix = (iota((Q, Q), 0) <= iota((Q, Q), 1)).astype(F32)
        head = iota((Q, 128), 1) < HEADS
        offs = []
        for k in range(T // Q):
            ro, co = roff[k * Q : (k + 1) * Q, :], coff[k * Q : (k + 1) * Q, :]
            sums = exact(suffix, jnp.concatenate([ro, co], axis=1))
            sr, sco = sums[:, :128], sums[:, 128:]
            fwd = sr + (sco[0:1] - sco)
            rev = (sr[0:1] - sr + ro) + (sco - co)
            offs.append(jnp.where(head, fwd, rev) + dkeep[k : k + 1, :])
        dl = dl + jnp.concatenate(offs, axis=0)
        dv = dl * a * sg + (cs + coff[...] + dls[...]) * ratio
        emit(jnp.concatenate([total[HALO:, :128], dv], axis=1), total[:HALO])

        at = SMALL_AT
        small[at : at + 1, 0:128] = jnp.sum(dv, axis=0, keepdims=True)
        small[at : at + 1, 128:] = jnp.sum(dl * dt * a, axis=0, keepdims=True)
        for q in range(INNER // CH):
            small[at + 1 + q : at + 2 + q, :] = ggain[:, CH * q : CH * (q + 1)]
        data = small[...].astype(BF)
        skeep_o[...] = jnp.where(first_core, data, jnp.zeros_like(data))
        ssend_o[...] = jnp.where(first_core, jnp.zeros_like(data), data)


def unproject(flag, dx, g, act, z, pre, conv_w, rows, dst, b, normt, nh, skip, bias, alog,
              rsum, csum, roff, coff, dkeep, dbc, dcs, dlr, ggain):
    T = dx.shape[0]
    E = T + HALO
    col = lambda rows: pl.BlockSpec((rows, CH), lambda i: (0, i))
    xcol = lambda rows: pl.BlockSpec((rows, CH), lambda i: (0, jnp.minimum(i, NCH - 2)))
    shapes = [((NCH, D // 2, CH), BF), ((NCH, D // 2, CH), BF), ((T, NCH * CH), BF), ((HALO, NCH * CH), BF),
              ((SMALL, CH), BF), ((SMALL, CH), BF)]
    return pl.pallas_call(
        functools.partial(unproject_kernel, T),
        grid=(NCH,),
        in_specs=[SMEM_SPEC, xcol(T), xcol(T), xcol(T), col(T), col(E), col(CONV), full((PAIRS, 16, T)),
                  xcol(64), full((T, 64)), full((D, T)), full((HALO, D)), xcol(1), full((1, 128)), full((1, 128)),
                  full((128, T)), full((T, 128)), full((T, 128)), full((T, 128)), full((8, 128)), full((T, 128)),
                  full((T, 64)), full((T, 128)), full((1, INNER))],
        out_specs=[pl.BlockSpec((1, D // 2, CH), lambda i: (i, 0, 0))] * 2 + [col(T), col(HALO)] + [full((SMALL, CH))] * 2,
        out_shape=[jax.ShapeDtypeStruct(s, d) for s, d in shapes],
        scratch_shapes=[pltpu.VMEM((D, 128), BF), pltpu.VMEM((E, CH), F32),
                        pltpu.VMEM((128, CH), BF), pltpu.VMEM((T, 64), F32), pltpu.VMEM((T, 128), F32),
                        pltpu.VMEM((SMALL, CH), F32), pltpu.VMEM((T // Q, (CONV - 1) * Q, Q + HALO), BF),
                        pltpu.VMEM((T // Q, (CONV - 1) * (Q + HALO), Q), BF)],
        compiler_params=params(),
        name="unproject",
    )(flag, dx, g, act, z, pre, conv_w, rows, dst, b, normt, nh, skip, bias, alog, rsum, csum, roff, coff, dkeep, dbc, dcs, dlr,
      ggain)


BOTH = ("dir", "dp")


def width(axis):
    return lax.axis_size(axis).bit_length() - 1


def exchange(v, mask_even, mask_odd):
    size = lax.axis_size("dir") * lax.axis_size("dp")
    return lax.ppermute(v, BOTH, [(i, i ^ (mask_odd if i & 1 else mask_even)) for i in range(size)])


def side_of(mask_even, mask_odd):
    me = lax.axis_index(BOTH)
    return jnp.where(me % 2 == 0, me & mask_even, me & mask_odd) != 0


def swap(v):
    mask = lax.axis_size("dp")
    return exchange(v, mask, mask)


def gather_rows(shard, ready, rest):
    bits = width("dp")
    down = list(range(bits - 1, 0, -1))
    even, odd = down, down[-1:] + down[:-1]
    out = shard
    for done, (e, o) in enumerate(zip(even, odd)):
        out = grow(out, done, e, o)
        if done == 0:
            out, rest = lax.optimization_barrier((out, rest))
        if done == 1:
            out, ready = lax.optimization_barrier((out, ready))
    return gather_finish(out, shard.shape), ready, rest


def grow(out, done, e, o):
    other = exchange(out, 1 << e, 1 << o)
    high = side_of(1 << e, 1 << o)
    return jnp.stack([jnp.where(high, other, out), jnp.where(high, out, other)], axis=done)


def gather_finish(out, shape):
    bits = width("dp")
    if bits == 0:
        return out
    other = exchange(out, 1, 1)
    high = side_of(1, 1)
    first = jnp.where(high, other, out)
    second = jnp.where(high, out, other)
    lead = max(bits - 1, 0)
    if lead > 1:
        second = jnp.moveaxis(second, 0, lead - 1)
    return jnp.stack([first, second], axis=lead).reshape((-1,) + shape[1:])


def halves(v, high, axis=0):
    n = v.shape[axis] // 2
    at = jnp.where(high, n, 0)
    return lax.dynamic_slice_in_dim(v, at, n, axis), lax.dynamic_slice_in_dim(v, n - at, n, axis)


def add(p, q):
    return (p.astype(F32) + q.astype(F32)).astype(BF)


def reduce_all(keep, send, keep_s, send_s, rows_s, later, inputs):
    bits = width("dp")
    masks = [1 << b for b in [bits] * width("dir") + list(range(1, bits))]
    odd = list(masks)
    for i in range(0, len(masks) - 1, 2):
        odd[i], odd[i + 1] = masks[i + 1], masks[i]
    order = list(zip(masks, odd))
    got, got_s = exchange(send, 1, 1), exchange(send_s, 1, 1)
    small = jnp.pad(add(keep_s, got_s), ((0, rows_s - SMALL), (0, 0)))
    high = side_of(*order[0])
    (keep, send), (got, got_send) = halves(keep, high, 1), halves(got, high, 1)
    none = jnp.zeros_like(small)
    send = jnp.concatenate([add(send, got_send).reshape(-1, CH), jnp.where(high, small, none)], axis=0)
    send, inputs = lax.optimization_barrier((send, inputs))
    keep = jnp.concatenate([add(keep, got).reshape(-1, CH), jnp.where(high, none, small)], axis=0)
    got = exchange(send, *order[0])
    extra, beside = later(*inputs)
    for at, pair in enumerate(order[1:]):
        high = side_of(*pair)
        (keep, send), (got, got_send) = halves(keep, high), halves(got, high)
        send = add(send, got_send)
        if at == 0:
            send, extra = lax.optimization_barrier((send, extra))
        keep, got = add(keep, got), exchange(send, *pair)
    buf = add(keep, got)
    for at, pair in enumerate(reversed(order)):
        n = buf.shape[0]
        if at == len(order) - 1:
            buf, beside = lax.optimization_barrier((buf, beside))
        got = exchange(jnp.concatenate([buf, extra], axis=0), *pair)
        extra = add(extra, got[n:])
        high = side_of(*pair)
        buf = jnp.concatenate([jnp.where(high, got[:n], buf), jnp.where(high, buf, got[:n])], axis=0)
    own = buf.reshape(2, -1, CH)
    return own, exchange(own, 1, 1), extra, exchange(extra, 1, 1), beside


def late_kernel(flag, own, other, own_l, other_l, own_s, other_s, own_e, other_e, zx_o, bc_o, dt_o, cw_o, cb_o, dtb_o, alog_o,
                skip_o, og_o, ng_o):
    half, part = D // 2, D // 4
    first = flag[5] == 0
    upper = jnp.where(first, own[...], other[...]).astype(F32)
    lower = jnp.where(first, other[...], own[...]).astype(F32)
    for q in range(2):
        for r in range(2):
            zx_o[part * r : part * (r + 1), CH * q : CH * (q + 1)] = upper[r, part * q : part * (q + 1)]
            zx_o[half + part * r : half + part * (r + 1), CH * q : CH * (q + 1)] = lower[r, part * q : part * (q + 1)]

    @pl.when(pl.program_id(0) == 0)
    def _():
        tops, bottoms = jnp.where(first, own_l[...], other_l[...]), jnp.where(first, other_l[...], own_l[...])
        tail = jnp.concatenate([tops[0], tops[1], bottoms[0], bottoms[1]], axis=0).astype(F32)
        bc_o[...] = tail[:, :128]
        dt_o[...] = tail[:, 128:].T[: 2 * HEADS, :]
        sm = jnp.where(first, own_s[0], other_s[0]).astype(F32)
        for q in range(NCH):
            n = CH if q < NCH - 1 else 2 * STATE
            cw_o[:, CH * q : CH * q + n] = sm[CONV * q : CONV * (q + 1), :n]
            cb_o[CH * q : CH * q + n] = sm[CONV * NCH + q, :n]
        at = SMALL_AT
        dtb_o[...] = sm[at, : 2 * HEADS]
        alog_o[...] = sm[at, 128 : 128 + 2 * HEADS]
        for q in range(INNER // CH):
            og_o[CH * q : CH * (q + 1)] = sm[at + 1 + q, :]
        ng = own_e[...].astype(F32) + other_e[...].astype(F32)
        for q in range(D // CH):
            ng_o[CH * q : CH * (q + 1)] = ng[q, :]
        skip_o[...] = sm[at + 10, :HEADS]


def late(flag, own, other, own_e, other_e):
    n = INNER // CH // 2
    taps = INNER + 2 * STATE
    shapes = [(D, 2 * INNER), (D, 2 * STATE), (2 * HEADS, D), (CONV, taps), (taps,), (2 * HEADS,), (2 * HEADS,), (HEADS,),
              (INNER,), (D,)]
    two = pl.BlockSpec((2, D // 2, CH), lambda i: (0, i, 0))
    last = pl.BlockSpec((2, D // 4, CH), lambda i: (0, NCH - 1, 0))
    small = pl.BlockSpec((1, SMALL, CH), lambda i: (0, NCH * D // (4 * SMALL), 0))
    extra = full((EXTRA, CH))
    return pl.pallas_call(
        late_kernel,
        grid=(n,),
        in_specs=[SMEM_SPEC, two, two, last, last, small, small, extra, extra],
        out_specs=[pl.BlockSpec((D, 2 * CH), lambda i: (0, n + i))] + [full(v) for v in shapes[1:]],
        out_shape=[jax.ShapeDtypeStruct(v, F32) for v in shapes],
        compiler_params=params(),
        name="late",
    )(flag, own, other, own, other, own, other, own_e, other_e)


def early_kernel(wg, wo, zx, zx_o, wo_o):
    zx_o[...] = wg[...].astype(F32)
    wo_o[...] = wo[...].astype(F32).T


def early(wg, wo, zx):
    n = INNER // CH // 2
    col = pl.BlockSpec((D, 2 * CH), lambda i: (0, i))
    return pl.pallas_call(
        early_kernel,
        grid=(n,),
        in_specs=[col, col, pl.BlockSpec(memory_space=pl.ANY)],
        out_specs=[col, pl.BlockSpec((2 * CH, D), lambda i: (i, 0))],
        out_shape=[jax.ShapeDtypeStruct((D, 2 * INNER), F32), jax.ShapeDtypeStruct((INNER, D), F32)],
        input_output_aliases={2: 0},
        compiler_params=params(),
        name="early",
    )(wg, wo, zx)


def apart(flag, part, args):
    def nothing(v):
        return jax.tree.map(lambda o: jnp.zeros(o.shape, o.dtype), jax.eval_shape(part, v))

    return lax.cond(flag[1] >= 1, part, nothing, args)


def body(tokens, norm_gain, w_zx, w_bc, w_dt, conv_w, conv_b, dt_bias, a_log, d_skip, out_gain, w_out, doc_lengths, out_grad):
    T = tokens.shape[1]
    devices = lax.axis_size("dir") * lax.axis_size("dp")
    side = lax.axis_index("dir")
    tok = tokens.reshape(T, D)
    og = out_grad.reshape(T, D)
    shard = w_zx.shape[0]
    half = INNER // 2
    mine = jnp.concatenate([w_zx[:, INNER:], w_bc, w_dt, jnp.zeros((shard, 128 - 2 * HEADS), BF)], axis=1)
    halo = lax.ppermute(tok[T - HALO :], "dir", [(0, 1)])
    flag = jnp.concatenate([side[None].astype(jnp.int32), doc_lengths[0], lax.rem(lax.axis_index("dp"), 2)[None].astype(jnp.int32)])
    wide = NCH * CH
    cw = jnp.pad(conv_w, ((0, 0), (0, wide - conv_w.shape[1])))
    cb = jnp.pad(conv_b, (0, wide - conv_b.shape[0]))[None]
    lanes = lambda v: jnp.pad(v, (0, 128 - v.shape[0]))[None]
    skip = jnp.repeat(d_skip, HEADDIM)[None]
    rest = jnp.concatenate([w_zx[:, :half], w_zx[:, half:INNER], w_out], axis=0)
    ready = (halo, flag, cw, cb, lanes(dt_bias), lanes(a_log), skip, norm_gain[None], out_gain[None], og.T)
    w1, ready, rest = gather_rows(mine, ready, rest)

    def finish(v):
        (flag, b, bt, c, ct, uv, keep, table, act, gm, z, pre, w1, cw, normt, nh, skip, bias, alog, tok, halo, ggain, og, gain_in,
         no, gg, wrc, st_in, rest) = v
        dcs, dlr, dst = aside(flag, gm, wrc, c, ct, st_in)
        dst_in = swap(dst)
        dx, rsum, csum, roff, coff, dkeep, dbc = unmix(flag, b, bt, c, ct, uv, keep, table, act, gm)
        keep_w, send_w, dpl, dph, keep_s, send_s = unproject(
            flag, dx, gm, act, z, pre, cw, table, dst_in, b, normt, nh, skip, bias, alog, rsum, csum, roff, coff, dkeep, dbc,
            dcs, dlr, ggain)
        rows = NCH * D
        total = -(-(rows + 4 * SMALL) // (16 * devices)) * 16 * devices

        def later(dpl, dph):
            bo, gn, gnh, part = deferred(dpl, dph, w1, gg, no, rest, tok, halo)
            back = lax.ppermute(gnh, "dir", [(1, 0)])
            gn = gn + jnp.pad(back, ((T - HALO, 0), (0, 0)))
            x32 = tok.astype(F32)
            rho = lax.rsqrt(jnp.mean(x32 * x32, axis=1, keepdims=True) + EPS)
            e_in = gn * gain_in
            gx = rho * e_in - x32 * (rho * rho * rho * jnp.mean(e_in * x32, axis=1, keepdims=True))
            return part, (bo, (og.astype(F32) + gx).astype(BF))

        own, other, own_e, other_e, (bo, grad_tokens) = reduce_all(
            keep_w, send_w, keep_s, send_s, (total - rows) // 4, later, (dpl, dph))
        return (bo, grad_tokens) + tuple(late(flag, own, other, own_e, other_e))

    def rest_of(v):
        w1, rest, (halo, flag, cw, cb, bias, alog, skip, gain_in, gain_out, ogt), tok, og = v
        rest = lax.all_gather(rest, "dp", axis=0, tiled=False)
        if shard % 16:
            rest = jnp.concatenate([rest[:, :shard].reshape(D, D), rest[:, shard : 2 * shard].reshape(D, D),
                                    rest[:, 2 * shard :].reshape(INNER, D)], axis=0)[None]
        normed, normt, nh, pre, z, act, rows, wrc, uv, keep, b, bt, c, ct, st = project(
            flag, tok, halo, gain_in, w1, cw, cb, bias, alog)
        st_in = swap(st)
        y = mix(flag, b, bt, c, uv, keep, rows, act, skip)
        no, gg, gm, dwg, dwo, ggain = gate(y, wrc, c, st_in, normed, normt, rest, og, ogt, gain_out)
        dwo, dwg = lax.psum((dwo, dwg), BOTH)
        args = (flag, b, bt, c, ct, uv, keep, rows, act, gm, z, pre, w1, cw, normt, nh, skip, bias, alog, tok, halo, ggain, og,
                gain_in, no, gg, wrc, st_in, rest)
        bo, grad_tokens, zx, g_bc, g_dt, g_cw, g_cb, g_dtb, g_alog, g_skip, g_og, g_ng = apart(flag, finish, args)
        zx, g_wo = early(dwg, dwo, zx)
        return bo, grad_tokens, g_ng, zx, g_bc, g_dt.T, g_cw, g_cb, g_dtb, g_alog, g_skip, g_og, g_wo

    outs = rest_of((w1, rest, ready, tok, og))
    return (outs[0].reshape(tokens.shape), outs[1].reshape(tokens.shape)) + tuple(outs[2:])


def solution(mesh):
    rows, weight, whole = P("dp", "dir", None), P("dp", None), P()
    placed = (rows, whole, weight, weight, weight, whole, whole, whole, whole, whole, whole, weight, weight, rows)
    return jax.shard_map(body, mesh=mesh, in_specs=placed, out_specs=(rows, rows) + (whole,) * 11, check_vma=False)
```

```python
import functools

import jax
import jax.numpy as jnp
from jax import lax
from jax.experimental import pallas as pl
from jax.experimental.pallas import tpu as pltpu
from jax.sharding import PartitionSpec as P

D = 768
HEADS = 24
HEADDIM = 64
STATE = 64
INNER = 1536
CONV = 4
NDOC = 4
PAIRS = HEADS // 2
HALO = 16
CH = 256
NCH = 7
Q = 128
GROUP = CH // HEADDIM
SMALL_AT = (CONV + 1) * NCH
SMALL = 64
EXTRA = 16
EPS = 1e-05
LOG2E = 1.4426950408889634
BF = jnp.bfloat16
F32 = jnp.float32
HI = lax.Precision.HIGHEST


def nn(a, b):
    return lax.dot_general(a, b, (((1,), (0,)), ((), ())), preferred_element_type=F32)


def nt(a, b):
    return lax.dot_general(a, b, (((1,), (1,)), ((), ())), preferred_element_type=F32)


def iota(shape, axis):
    return lax.broadcasted_iota(jnp.int32, shape, axis)


def sigm(v):
    return 1.0 / (1.0 + jnp.exp(-v))


def lane_pair(col_a, col_b, rows):
    return jnp.where(iota((rows, 128), 1) < 64, col_a, col_b)


def params(mib=60):
    return pltpu.CompilerParams(
        dimension_semantics=("arbitrary",), vmem_limit_bytes=mib * 1024 * 1024
    )


def full(shape):
    return pl.BlockSpec(shape, lambda i: tuple(0 for _ in shape))


SMEM_SPEC = pl.BlockSpec(memory_space=pltpu.SMEM)


def doc_ids(flag, places):
    total = jnp.zeros(places.shape, jnp.int32)
    end = 0
    for k in range(NDOC):
        end = end + flag[1 + k]
        total = total + jnp.where(places >= end, 1, 0)
    return jnp.where(places < 0, -1, total)


def doc_at(flag, place):
    total = 0
    end = 0
    for k in range(NDOC):
        end = end + flag[1 + k]
        total = total + jnp.where(place >= end, 1, 0)
    return total


def doc_col(flag, T, lead=0):
    return doc_ids(flag, iota((T + lead, 1), 0) + (flag[0] * T - lead))


def doc_row(flag, T):
    return doc_ids(flag, iota((1, T), 1) + flag[0] * T)


def project_kernel(T, flag, tok, halo, gain, w, cw, cb, bias, alog,
                   norm_o, normt_o, nh_o, pre_o, z_o, act_o, rows_o, wrc_o, uv_o, keep_o, b_o, bt_o, c_o, ct_o, st_o, ncat, pf, segc):
    step = pl.program_id(0)

    @pl.when(step == 0)
    def _():
        def norm(v):
            v = v.astype(F32)
            ms = jnp.mean(v * v, axis=1, keepdims=True)
            return (v * lax.rsqrt(ms + EPS) * gain[...]).astype(BF)

        nh = norm(halo[...])
        own = norm(tok[...])
        nh_o[...] = nh
        norm_o[...] = own
        normt_o[...] = own.astype(F32).T.astype(BF)
        ncat[0:HALO, :] = nh
        ncat[HALO:, :] = own
        segc[...] = doc_col(flag, T, HALO)

    proj = nn(ncat[...], w[...]).astype(BF)
    pre_o[...] = proj
    pf[...] = proj.astype(F32)
    segs = segc[...]
    here = segs[HALO:, :]
    z = cb[...] + cw[CONV - 1 : CONV, :] * pf[HALO:, :]
    for k in range(1, CONV):
        same = segs[HALO - k : HALO + T - k, :] == here
        z = z + jnp.where(same, cw[CONV - 1 - k : CONV - k, :] * pf[HALO - k : HALO + T - k, :], 0.0)
    z_o[...] = z.astype(BF)
    act = z * sigm(z)
    act_o[...] = act.astype(BF)

    @pl.when(step == 0)
    def _():
        bc = act[:, :128]
        b_o[...] = bc[:, :64].astype(BF)
        c_o[...] = bc[:, 64:].astype(BF)
        bct = bc.T
        bt_o[...] = bct[:64, :].astype(BF)
        ct_o[...] = bct[64:, :].astype(BF)
        v = pf[HALO:, 128:] + bias[...]
        dt = jnp.maximum(v, 0.0) + jnp.log1p(jnp.exp(-jnp.abs(v)))
        rate = dt * (-LOG2E * jnp.exp(alog[...]))
        rate_t = rate.T
        dt_t = dt.T
        upto = (iota((T, T), 0) <= iota((T, T), 1)).astype(F32)
        inc = lax.dot_general(rate_t, upto, (((1,), (0,)), ((), ())), precision=HI, preferred_element_type=F32)
        isf = iota((128, T), 0) < HEADS
        cum = jnp.where(isf, inc, inc - rate_t)
        ldt = jnp.log2(jnp.maximum(dt_t, 1e-37))
        key = jnp.where(isf, cum - ldt, cum + ldt)
        segv = doc_row(flag, T)
        left, right = doc_at(flag, T - 1), doc_at(flag, T)
        send_f = jnp.where(segv == left, jnp.exp2(cum[:, T - 1 :] - key), 0.0)
        send_b = jnp.where(segv == right, jnp.exp2(key), 0.0)
        recv_f = jnp.where(segv == left, jnp.exp2(cum), 0.0)
        recv_b = jnp.where(segv == right, jnp.exp2(inc[:, T - 1 :] - cum), 0.0)
        first = flag[0] == 0
        send = jnp.where(first, send_f[0:HEADS], send_b[HEADS : 2 * HEADS])
        recv = jnp.where(first, recv_b[HEADS : 2 * HEADS], recv_f[0:HEADS])
        for p in range(PAIRS):
            f, r = 2 * p, HEADS + 2 * p
            rows_o[p, 0:2, :] = cum[f : f + 2]
            rows_o[p, 2:4, :] = cum[r : r + 2]
            rows_o[p, 4:6, :] = key[f : f + 2]
            rows_o[p, 6:8, :] = key[r : r + 2]
            rows_o[p, 8:10, :] = send[f : f + 2]
            rows_o[p, 10:12, :] = recv[f : f + 2]
            rows_o[p, 12:16, :] = jnp.zeros((4, T), F32)
        recv_pad = jnp.concatenate([recv, jnp.zeros((128 - HEADS, T), F32)], axis=0)
        wrc_o[...] = recv_pad.T.astype(BF)
        cum_f, cum_r = cum[0:HEADS], cum[HEADS : 2 * HEADS]
        key_f, key_r = key[0:HEADS], key[HEADS : 2 * HEADS]
        quads = [[], [], [], []]
        none = jnp.zeros((HEADS, Q), F32)
        lane = iota((HEADS, 128), 1)
        keep_f = jnp.zeros((HEADS, 128), F32)
        keep_r = jnp.zeros((HEADS, 128), F32)
        for k in range(T // Q):
            lo, hi = k * Q, (k + 1) * Q
            sg = segv[:, lo:hi]
            before = cum_f[:, lo - 1 : lo] if k > 0 else None
            after = cum_r[:, hi : hi + 1] if hi < T else None
            quads[0].append(none if k == 0 else jnp.where(sg == segv[:, lo - 1 : lo], jnp.exp2(cum_f[:, lo:hi] - before), 0.0))
            quads[1].append(jnp.where(sg == segv[:, hi - 1 : hi], jnp.exp2(cum_f[:, hi - 1 : hi] - key_f[:, lo:hi]), 0.0))
            quads[2].append(none if hi == T else jnp.where(sg == segv[:, hi : hi + 1], jnp.exp2(after - cum_r[:, lo:hi]), 0.0))
            quads[3].append(jnp.where(sg == segv[:, lo : lo + 1], jnp.exp2(key_r[:, lo:hi] - cum_r[:, lo : lo + 1]), 0.0))
            if k > 0:
                through = jnp.where(segv[:, lo - 1 : lo] == segv[:, hi - 1 : hi], jnp.exp2(cum_f[:, hi - 1 : hi] - before), 0.0)
                keep_f = jnp.where(lane == k, through, keep_f)
            if hi < T:
                through = jnp.where(segv[:, lo : lo + 1] == segv[:, hi : hi + 1], jnp.exp2(after - cum_r[:, lo : lo + 1]), 0.0)
                keep_r = jnp.where(lane == k, through, keep_r)
        quads = [jnp.concatenate(v, axis=1) for v in quads]
        uv_o[...] = jnp.concatenate(quads + [jnp.zeros((128 - 4 * HEADS, T), F32)], axis=0).T.astype(BF)
        keeps = jnp.concatenate([keep_f, keep_r, jnp.zeros((128 - 2 * HEADS, 128), F32)], axis=0).T
        keep_o[...] = keeps[0:8, :]

    @pl.when(step > 0)
    def _():
        for j in range(CH // 128):
            cols = rows_o[2 * (step - 1) + j, 8:16, :].T
            wide = lane_pair(cols[:, 0:1], cols[:, 1:2], T)
            xw = (act[:, 128 * j : 128 * (j + 1)] * wide).astype(BF)
            st_o[:, 128 * j : 128 * (j + 1)] = nn(bt_o[...], xw).astype(BF)


def project(flag, tok, halo, gain, w1, conv_w, conv_b, bias, alog):
    T = tok.shape[0]
    E = T + HALO
    chunk = lambda i: lax.rem(i + NCH - 1, NCH)
    xchunk = lambda i: jnp.maximum(i - 1, 0)
    col = lambda rows: pl.BlockSpec((rows, CH), lambda i: (0, chunk(i)))
    shapes = [
        ((T, D), BF), ((D, T), BF), ((HALO, D), BF), ((E, NCH * CH), BF), ((T, NCH * CH), BF), ((T, NCH * CH), BF),
        ((PAIRS, 16, T), F32), ((T, 128), BF), ((T, 128), BF), ((8, 128), F32), ((T, 64), BF), ((64, T), BF), ((T, 64), BF), ((64, T), BF),
        ((64, INNER), BF),
    ]
    out_specs = [
        full((T, D)), full((D, T)), full((HALO, D)), col(E), col(T), col(T), full((PAIRS, 16, T)), full((T, 128)), full((T, 128)), full((8, 128)), full((T, 64)),
        full((64, T)), full((T, 64)), full((64, T)), pl.BlockSpec((64, CH), lambda i: (0, xchunk(i))),
    ]
    return pl.pallas_call(
        functools.partial(project_kernel, T),
        grid=(NCH,),
        in_specs=[SMEM_SPEC, full((T, D)), full((HALO, D)), full((1, D)), col(D), col(CONV), col(1),
                  full((1, 128)), full((1, 128))],
        out_specs=out_specs,
        out_shape=[jax.ShapeDtypeStruct(s, d) for s, d in shapes],
        scratch_shapes=[pltpu.VMEM((E, D), BF), pltpu.VMEM((E, CH), F32), pltpu.VMEM((E, 1), jnp.int32)],
        compiler_params=params(),
        name="project",
    )(flag, tok, halo, gain, w1, conv_w, conv_b, bias, alog)


def shift_matrix(flag, T, lo):
    first = flag[0] * T + lo
    own = doc_ids(flag, iota((Q, 1), 0) + first)
    from_doc = doc_ids(flag, iota((1, Q + HALO), 1) + (first - HALO))
    gap = iota((Q, Q + HALO), 0) + HALO - iota((Q, Q + HALO), 1)
    return jnp.concatenate([((gap == k) & (own == from_doc)).astype(F32) for k in range(1, CONV)], axis=0).astype(BF)


def shift_back_matrix(flag, T, lo):
    first = flag[0] * T + lo
    own = doc_ids(flag, iota((1, Q), 1) + first)
    from_doc = doc_ids(flag, iota((Q + HALO, 1), 0) + (first - HALO))
    gap = iota((Q + HALO, Q), 1) + HALO - iota((Q + HALO, Q), 0)
    return jnp.concatenate([((gap == k) & (own == from_doc)).astype(F32) for k in range(1, CONV)], axis=0).astype(BF)


def same_doc(flag, T, lo):
    first = flag[0] * T + lo
    a = doc_ids(flag, iota((Q, 1), 0) + first)
    b = doc_ids(flag, iota((1, Q), 1) + first)
    return (a == b) & (iota((Q, Q), 0) != iota((Q, Q), 1))


def spread_of(step, slot, dtype=BF):
    base = slot * HEADS + GROUP * step
    return (lax.div(iota((128, CH), 1), HEADDIM) + base == iota((128, CH), 0)).astype(dtype)


def exact(a, b):
    return lax.dot_general(a, b, (((1,), (0,)), ((), ())), precision=HI, preferred_element_type=F32)


def states(T, bt, vf, vr, keep_f, keep_r):
    n = T // Q
    ahead, back = [None] * n, [None] * n
    for k in range(1, n):
        new = nn(bt[:, (k - 1) * Q : k * Q], vf[(k - 1) * Q : k * Q])
        ahead[k] = new if k == 1 else new + keep_f[k - 1 : k] * ahead[k - 1]
    for k in reversed(range(n - 1)):
        new = nn(bt[:, (k + 1) * Q : (k + 2) * Q], vr[(k + 1) * Q : (k + 2) * Q])
        back[k] = new if k == n - 2 else new + keep_r[k + 1 : k + 2] * back[k + 1]
    return ahead, back


def mix_kernel(T, flag, b, bt, c, uv, keep, rows, x, skip, y_o, sc):
    step = pl.program_id(0)
    n = T // Q

    @pl.when(step == 0)
    def _():
        for i in range(n):
            lo, hi = i * Q, (i + 1) * Q
            sc[i] = jnp.where(same_doc(flag, T, lo), nt(c[lo:hi, :], b[lo:hi, :]), 0.0)

    x4 = x[...]
    x32 = x4.astype(F32)
    table = uv[...]
    uf, vf, ur, vr = [nn(table, spread_of(step, slot)) for slot in range(4)]
    keep_f = exact(keep[...], spread_of(step, 0, F32))
    keep_r = exact(keep[...], spread_of(step, 1, F32))
    ahead, back = states(T, bt, (vf * x32).astype(BF), (vr * x32).astype(BF), keep_f, keep_r)
    later = iota((Q, Q), 0) > iota((Q, Q), 1)
    lane = iota((Q, 128), 1) < HEADDIM
    cols = [rows[p][0:8].T for p in range(GROUP // 2)]
    for i in range(n):
        lo, hi = i * Q, (i + 1) * Q
        pieces = []
        for p in range(GROUP // 2):
            xs = x4[lo:hi, 128 * p : 128 * (p + 1)]
            outs = []
            for h in range(2):
                cf = cols[p][lo:hi, h : h + 1]
                cr = cols[p][lo:hi, 2 + h : 3 + h]
                kf = rows[p, 4 + h : 5 + h, lo:hi]
                kr = rows[p, 6 + h : 7 + h, lo:hi]
                m = sc[i] * jnp.exp2(jnp.where(later, cf - kf, kr - cr))
                outs.append(nn(m.astype(BF), xs))
            pieces.append(jnp.where(lane, outs[0], outs[1]))
        y = jnp.concatenate(pieces, axis=1) + skip[...] * x32[lo:hi]
        if i > 0:
            y = y + uf[lo:hi] * nn(c[lo:hi, :], ahead[i].astype(BF))
        if i < n - 1:
            y = y + ur[lo:hi] * nn(c[lo:hi, :], back[i].astype(BF))
        y_o[lo:hi, :] = y.astype(BF)


def mix(flag, b, bt, c, uv, keep, rows, act, skip):
    T = b.shape[0]
    blk = pl.BlockSpec((T, CH), lambda i: (0, i))
    return pl.pallas_call(
        functools.partial(mix_kernel, T),
        grid=(INNER // CH,),
        in_specs=[SMEM_SPEC, full((T, 64)), full((64, T)), full((T, 64)), full((T, 128)), full((8, 128)),
                  pl.BlockSpec((GROUP // 2, 16, T), lambda i: (i, 0, 0)), blk, pl.BlockSpec((1, CH), lambda i: (0, i))],
        out_specs=blk,
        out_shape=jax.ShapeDtypeStruct((T, INNER), BF),
        scratch_shapes=[pltpu.VMEM((T // Q, Q, Q), F32)],
        compiler_params=params(),
        name="mix",
    )(flag, b, bt, c, uv, keep, rows, act, skip)


def seam_width(wrc):
    spread = (lax.div(iota((128, INNER), 1), HEADDIM) == iota((128, INNER), 0)).astype(BF)
    return nn(wrc[...], spread)


def gate_kernel(shard, y, wrc, c, st, normed, normt, rest, og, ogt, gain, no_o, gg_o, gm_o, dwg_o, dwo_o, ggain_o, acc_g, acc_o):
    step = pl.program_id(0)
    mixed = y[...].astype(F32) + nn(c[...], st[...]) * seam_width(wrc)
    half = INNER // 2
    own = normed[...]
    gz = jnp.concatenate([nn(own, rest[:, :shard, :].reshape(D, half)), nn(own, rest[:, shard : 2 * shard, :].reshape(D, half))],
                         axis=1)
    sig = sigm(gz)
    sil = gz * sig
    gated = mixed * sil
    rho = lax.rsqrt(jnp.mean(gated * gated, axis=1, keepdims=True) + EPS)
    no = (gated * rho * gain[...]).astype(BF)
    no_o[...] = no
    gno = nt(og[...], rest[:, 2 * shard :, :].reshape(INNER, D))
    e = gno * gain[...]
    part = jnp.sum(gno * gated * rho, axis=0, keepdims=True)
    mean_eg = jnp.mean(e * gated, axis=1, keepdims=True)
    ggated = rho * e - gated * (rho * rho * rho * mean_eg)
    gg = (ggated * mixed * sig * (1.0 + gz * (1.0 - sig))).astype(BF)
    gg_o[...] = gg
    gm_o[...] = (ggated * sil).astype(BF)
    dwg = nn(normt[...], gg)
    dwo = nn(ogt[...], no)

    @pl.when(step == 0)
    def _():
        acc_g[...] = dwg
        acc_o[...] = dwo
        ggain_o[...] = part

    @pl.when(step > 0)
    def _():
        dwg_o[...] = (acc_g[...] + dwg).astype(BF)
        dwo_o[...] = (acc_o[...] + dwo).astype(BF)
        ggain_o[...] += part


def gate(y, wrc, c, st, normed, normt, rest, og, ogt, gain):
    T = y.shape[0]
    rb = T // 2
    row = lambda n: pl.BlockSpec((rb, n), lambda i: (i, 0))
    col = lambda n: pl.BlockSpec((n, rb), lambda i: (0, i))
    shapes = [((T, INNER), BF), ((T, INNER), BF), ((T, INNER), BF), ((D, INNER), BF), ((D, INNER), BF), ((1, INNER), F32)]
    return pl.pallas_call(
        functools.partial(gate_kernel, rest.shape[1] // 4),
        grid=(2,),
        in_specs=[row(INNER), row(128), row(64), full((64, INNER)), row(D), col(D), full(rest.shape), row(D), col(D),
                  full((1, INNER))],
        out_specs=[row(INNER), row(INNER), row(INNER), full((D, INNER)), full((D, INNER)), full((1, INNER))],
        out_shape=[jax.ShapeDtypeStruct(v, d) for v, d in shapes],
        scratch_shapes=[pltpu.VMEM((D, INNER), F32), pltpu.VMEM((D, INNER), F32)],
        compiler_params=params(),
        name="gate",
    )(y, wrc, c, st, normed, normt, rest, og, ogt, gain)


def side_kernel(flag, gm, wrc, c, ct, st, dcs_o, dlr_o, dst_o, acc):
    step = pl.program_id(0)
    gw = gm[...].astype(F32) * seam_width(wrc)
    seam = gw * nn(c[...], st[...])
    gw = gw.astype(BF)
    dcs_o[...] = nt(gw, st[...])
    shift = jnp.where(flag[0] == 0, HEADS, 0)
    gather = (lax.div(iota((INNER, 128), 0), HEADDIM) + shift == iota((INNER, 128), 1)).astype(BF)
    dlr_o[...] = nn(seam.astype(BF), gather)
    dst = nn(ct[...], gw)

    @pl.when(step == 0)
    def _():
        acc[...] = dst

    @pl.when(step > 0)
    def _():
        dst_o[...] = (acc[...] + dst).astype(BF)


def aside(flag, gm, wrc, c, ct, st):
    T = gm.shape[0]
    rb = T // 2
    row = lambda n: pl.BlockSpec((rb, n), lambda i: (i, 0))
    shapes = [((T, 64), F32), ((T, 128), F32), ((64, INNER), BF)]
    return pl.pallas_call(
        side_kernel,
        grid=(2,),
        in_specs=[SMEM_SPEC, row(INNER), row(128), row(64), pl.BlockSpec((64, rb), lambda i: (0, i)), full((64, INNER))],
        out_specs=[row(64), row(128), full((64, INNER))],
        out_shape=[jax.ShapeDtypeStruct(v, d) for v, d in shapes],
        scratch_shapes=[pltpu.VMEM((64, INNER), F32)],
        compiler_params=params(),
        name="side",
    )(flag, gm, wrc, c, ct, st)


def deferred_kernel(shard, dpl, dph, w1, gg, no, rest, tok, halo, bo_o, gn_o, gnh_o, part_o, acc):
    step = pl.program_id(0)
    half = INNER // 2

    def unit(v):
        v = v.astype(F32)
        return v * lax.rsqrt(jnp.mean(v * v, axis=1, keepdims=True) + EPS)

    bo_o[...] = (tok[...].astype(F32) + nn(no[...], rest[:, 2 * shard :, :].reshape(INNER, D))).astype(BF)
    gn = nt(dpl[...], w1[...])
    gn = gn + nt(gg[:, :half], rest[:, :shard, :].reshape(D, half))
    gn = gn + nt(gg[:, half:], rest[:, shard : 2 * shard, :].reshape(D, half))
    gn_o[...] = gn
    part = jnp.sum(gn * unit(tok[...]), axis=0, keepdims=True)

    @pl.when(step == 0)
    def _():
        gnh = nt(dph[...], w1[...])
        gnh_o[...] = gnh
        acc[0:1, :] = part + jnp.sum(gnh * unit(halo[...]), axis=0, keepdims=True)

    @pl.when(step > 0)
    def _():
        total = acc[0:1, :] + part
        rows = [total[:, CH * q : CH * (q + 1)] for q in range(D // CH)]
        part_o[...] = jnp.concatenate(rows + [jnp.zeros((EXTRA - D // CH, CH), F32)], axis=0).astype(BF)


def deferred(dpl, dph, w1, gg, no, rest, tok, halo):
    T = dpl.shape[0]
    rb = T // 2
    wide = NCH * CH
    row = lambda n: pl.BlockSpec((rb, n), lambda i: (i, 0))
    shapes = [((T, D), BF), ((T, D), F32), ((HALO, D), F32), ((EXTRA, CH), BF)]
    return pl.pallas_call(
        functools.partial(deferred_kernel, rest.shape[1] // 4),
        grid=(2,),
        in_specs=[row(wide), full((HALO, wide)), full((D, wide)), row(INNER), row(INNER), full(rest.shape), row(D),
                  full((HALO, D))],
        out_specs=[row(D), row(D), full((HALO, D)), full((EXTRA, CH))],
        out_shape=[jax.ShapeDtypeStruct(v, d) for v, d in shapes],
        scratch_shapes=[pltpu.VMEM((8, D), F32)],
        compiler_params=params(),
        name="deferred",
    )(dpl, dph, w1, gg, no, rest, tok, halo)


def unmix_kernel(T, flag, b, bt, c, ct, uv, keep, rows, x, g, dx_o, rsum_o, csum_o, roff_o, coff_o, dkeep_o, dbc_o,
                 sc, dsc, db, dc):
    step = pl.program_id(0)
    n = T // Q

    @pl.when(step == 0)
    def _():
        for i in range(n):
            lo, hi = i * Q, (i + 1) * Q
            sc[i] = jnp.where(same_doc(flag, T, lo), nt(b[lo:hi, :], c[lo:hi, :]), 0.0)
        dsc[...] = jnp.zeros((n, Q, Q), F32)
        db[...] = jnp.zeros((T, 64), F32)
        dc[...] = jnp.zeros((T, 64), F32)
        rsum_o[...] = jnp.zeros((128, T), F32)
        csum_o[...] = jnp.zeros((T, 128), F32)
        roff_o[...] = jnp.zeros((T, 128), F32)
        coff_o[...] = jnp.zeros((T, 128), F32)
        dkeep_o[...] = jnp.zeros((8, 128), F32)

    x4 = x[...]
    g4 = g[...]
    wide = nn(uv[...], jnp.concatenate([spread_of(step, slot) for slot in (0, 2, 1, 3)], axis=1)).astype(BF)
    x8 = jnp.concatenate([x4, x4], axis=1)
    v8 = wide[:, 2 * CH :]
    vx = v8 * x8
    ug = wide[:, : 2 * CH] * jnp.concatenate([g4, g4], axis=1)
    keep_f = exact(keep[...], spread_of(step, 0, F32))
    keep_r = exact(keep[...], spread_of(step, 1, F32))
    vxf, vxr, ugf, ugr = vx[:, :CH], vx[:, CH:], ug[:, :CH], ug[:, CH:]
    ahead, back = states(T, bt, vxf, vxr, keep_f, keep_r)
    lane = iota((Q, 128), 1)
    half = lane < HEADDIM
    earlier = iota((Q, Q), 0) < iota((Q, Q), 1)
    base = GROUP * step
    slot = lax.div(iota((2 * CH, 128), 0), HEADDIM)
    gather = (jnp.where(slot < GROUP, slot, slot + HEADS - GROUP) + base == iota((2 * CH, 128), 1)).astype(BF)
    cols = [rows[p][0:8].T for p in range(GROUP // 2)]
    dahead, dback = [None] * (n + 1), [None] * (n + 1)
    for k in reversed(range(1, n)):
        own = nn(ct[:, k * Q : (k + 1) * Q], ugf[k * Q : (k + 1) * Q])
        dahead[k] = own if k == n - 1 else own + keep_f[k : k + 1] * dahead[k + 1]
    for k in range(n - 1):
        own = nn(ct[:, k * Q : (k + 1) * Q], ugr[k * Q : (k + 1) * Q])
        dback[k] = own if k == 0 else own + keep_r[k : k + 1] * dback[k - 1]
    through = [jnp.zeros((1, 2 * CH), F32)] * 8
    for k in range(1, n - 1):
        pf = jnp.sum(keep_f[k : k + 1] * ahead[k] * dahead[k + 1], axis=0, keepdims=True)
        pr = jnp.sum(keep_r[k : k + 1] * back[k] * dback[k - 1], axis=0, keepdims=True)
        through[k] = jnp.concatenate([pf, pr], axis=1)
    dkeep_o[...] += nn(jnp.concatenate(through, axis=0).astype(BF), gather)
    totals = [[] for _ in range(2 * GROUP)]
    r_off, c_off = [], []
    none = jnp.zeros((Q, CH), F32)
    for j in range(n):
        lo, hi = j * Q, (j + 1) * Q
        pieces = []
        stat = jnp.zeros((Q, 128), F32)
        for p in range(GROUP // 2):
            xs = x4[lo:hi, 128 * p : 128 * (p + 1)]
            gs = g4[lo:hi, 128 * p : 128 * (p + 1)]
            zero = jnp.zeros_like(xs)
            gts = nt(jnp.concatenate([jnp.where(half, xs, zero), jnp.where(half, zero, xs)], axis=0), gs)
            ms = []
            for h in range(2):
                cf = rows[p, h : h + 1, lo:hi]
                cr = rows[p, 2 + h : 3 + h, lo:hi]
                kf = cols[p][lo:hi, 4 + h : 5 + h]
                kr = cols[p][lo:hi, 6 + h : 7 + h]
                gt = gts[h * Q : (h + 1) * Q]
                d = jnp.exp2(jnp.where(earlier, cf - kf, kr - cr))
                m = sc[j] * d
                ms.append(m.astype(BF))
                dsc[j] += gt * d
                w = gt * m
                wf = jnp.where(earlier, w, 0.0)
                wr = w - wf
                at = base + 2 * p + h
                stat = stat + jnp.where(lane == at, jnp.sum(wf, axis=1, keepdims=True), 0.0)
                stat = stat + jnp.where(lane == at + HEADS, jnp.sum(wr, axis=1, keepdims=True), 0.0)
                totals[2 * p + h].append(jnp.sum(wf, axis=0, keepdims=True))
                totals[GROUP + 2 * p + h].append(jnp.sum(wr, axis=0, keepdims=True))
            out = nn(jnp.concatenate(ms, axis=0), gs)
            pieces.append(jnp.where(half, out[:Q], out[Q:]))
        dx = jnp.concatenate(pieces, axis=1)
        zero = jnp.zeros((STATE, CH), BF)
        into = jnp.concatenate([ahead[j].astype(BF) if j > 0 else zero, back[j].astype(BF) if j < n - 1 else zero], axis=1)
        outof = jnp.concatenate([dahead[j + 1].astype(BF) if j < n - 1 else zero, dback[j - 1].astype(BF) if j > 0 else zero],
                                axis=1)
        r_off.append(ug[lo:hi] * nn(c[lo:hi, :], into).astype(BF))
        dv = v8[lo:hi] * nn(b[lo:hi, :], outof).astype(BF)
        c_off.append(x8[lo:hi] * dv)
        dx_o[lo:hi, :] = (dx + dv[:, :CH].astype(F32) + dv[:, CH:].astype(F32)).astype(BF)
        dc[lo:hi, :] += nt(ug[lo:hi], into)
        db[lo:hi, :] += nt(vx[lo:hi], outof)
        csum_o[lo:hi, :] += stat
    off = nn(jnp.concatenate(r_off + c_off, axis=0), gather)
    roff_o[...] += off[:T]
    coff_o[...] += off[T:]
    for q in range(2):
        for h in range(GROUP):
            rsum_o[pl.ds(HEADS * q + base + h, 1), :] = jnp.concatenate(totals[GROUP * q + h], axis=1)

    @pl.when(step == INNER // CH - 1)
    def _():
        for j in range(n):
            lo, hi = j * Q, (j + 1) * Q
            ds = jnp.where(same_doc(flag, T, lo), dsc[j], 0.0)
            dbc_o[lo:hi, 0:64] = db[lo:hi, :] + nn(ds.astype(BF), c[lo:hi, :])
            dbc_o[lo:hi, 64:128] = dc[lo:hi, :] + nn(ds.T.astype(BF), b[lo:hi, :])


def unmix(flag, b, bt, c, ct, uv, keep, rows, act, g):
    T = b.shape[0]
    n = T // Q
    blk = pl.BlockSpec((T, CH), lambda i: (0, i))
    shapes = [(T, INNER), (128, T), (T, 128), (T, 128), (T, 128), (8, 128), (T, 128)]
    return pl.pallas_call(
        functools.partial(unmix_kernel, T),
        grid=(INNER // CH,),
        in_specs=[SMEM_SPEC, full((T, 64)), full((64, T)), full((T, 64)), full((64, T)), full((T, 128)), full((8, 128)),
                  pl.BlockSpec((GROUP // 2, 16, T), lambda i: (i, 0, 0)), blk, blk],
        out_specs=[blk] + [full(v) for v in shapes[1:]],
        out_shape=[jax.ShapeDtypeStruct(v, F32 if k else BF) for k, v in enumerate(shapes)],
        scratch_shapes=[pltpu.VMEM((n, Q, Q), F32), pltpu.VMEM((n, Q, Q), F32), pltpu.VMEM((T, 64), F32),
                        pltpu.VMEM((T, 64), F32)],
        compiler_params=params(),
        name="unmix",
    )(flag, b, bt, c, ct, uv, keep, rows, act, g)


def unproject_kernel(T, flag, dx, g, act, z, pre, cw, rows, dst, b, nt_s, nh, skip, bias, alog,
                     rsum, csum, roff, coff, dkeep, dbc, dcs, dlr, ggain,
                     keep_o, send_o, dpl_o, dph_o, skeep_o, ssend_o,
                     ht_s, tot, hd_s, dbs, dls, small, shifts, shifts_back):
    step = pl.program_id(0)
    E = T + HALO
    first_core = flag[5] == 0

    @pl.when(step == 0)
    def _():
        for i in range(T // Q):
            shifts[i] = shift_matrix(flag, T, i * Q)
            shifts_back[i] = shift_back_matrix(flag, T, i * Q)
        small[...] = jnp.zeros((SMALL, CH), F32)
        pad = jnp.concatenate([nh[...].astype(F32), jnp.zeros((128 - HALO, D), F32)], axis=0)
        ht_s[...] = pad.T.astype(BF)
        hd_s[...] = jnp.zeros((128, CH), BF)
        dbs[...] = jnp.zeros((T, 64), F32)
        dls[...] = jnp.zeros((T, 128), F32)

    def through_conv(dact):
        tot[...] = jnp.zeros((E, CH), F32)
        g_b = jnp.zeros((1, CH), F32)
        g_w = [jnp.zeros((1, CH), F32) for _ in range(CONV)]
        wide = Q + HALO
        for i in range(T // Q):
            lo, hi = i * Q, (i + 1) * Q
            zz = z[lo:hi, :].astype(F32)
            sg = sigm(zz)
            dz = dact[lo:hi] * sg * (1.0 + zz * (1.0 - sg))
            moved = nn(shifts[i], pre[lo : hi + HALO, :])
            back = nn(shifts_back[i], dz.astype(BF))
            g_b = g_b + jnp.sum(dz, axis=0, keepdims=True)
            g_w[0] = g_w[0] + jnp.sum(dz * pre[lo + HALO : hi + HALO, :].astype(F32), axis=0, keepdims=True)
            part = jnp.zeros((wide, CH), F32)
            for k in range(1, CONV):
                g_w[k] = g_w[k] + jnp.sum(dz * moved[(k - 1) * Q : k * Q], axis=0, keepdims=True)
                part = part + cw[CONV - 1 - k : CONV - k, :] * back[(k - 1) * wide : k * wide]
            tot[lo : hi + HALO, :] += part
            tot[lo + HALO : hi + HALO, :] += cw[CONV - 1 : CONV, :] * dz
        small[pl.ds(CONV * NCH + step, 1), :] = g_b
        for k in range(CONV):
            small[pl.ds(CONV * step + CONV - 1 - k, 1), :] = g_w[k]
        return tot[...]

    def emit(local, halo):
        local = local.astype(BF)
        hd_s[0:HALO, :] = halo.astype(BF)
        dw = (nn(nt_s[...], local) + nn(ht_s[...], hd_s[...])).astype(BF)
        top, bottom = dw[: D // 2], dw[D // 2 :]
        keep_o[0] = jnp.where(first_core, top, bottom)
        send_o[0] = jnp.where(first_core, bottom, top)
        dpl_o[...] = local
        dph_o[...] = hd_s[0:HALO, :]

    @pl.when(step < NCH - 1)
    def _():
        wides = []
        for j in range(CH // 128):
            cols = rows[2 * step + j, 8:16, :].T
            wides.append(lane_pair(cols[:, 0:1], cols[:, 1:2], T))
        wide = jnp.concatenate(wides, axis=1)
        x32 = act[...].astype(F32)
        g32 = g[...].astype(F32)
        wq = wide * nn(b[...], dst[...])
        dbs[...] += nt((x32 * wide).astype(BF), dst[...])
        base = 4 * step + jnp.where(flag[0] == 0, 0, HEADS)
        sel = (lax.div(iota((CH, 128), 0), 64) + base == iota((CH, 128), 1)).astype(BF)
        dls[...] += nn((x32 * wq).astype(BF), sel)
        heads = (lax.div(iota((CH, 128), 0), 64) + 4 * step == iota((CH, 128), 1)).astype(F32)
        both = jnp.broadcast_to(jnp.sum(g32 * x32, axis=0, keepdims=True), (8, CH))
        both = lax.dot_general(both, heads, (((1,), (0,)), ((), ())), precision=HI, preferred_element_type=F32)
        small[SMALL_AT + 10 : SMALL_AT + 11, 0:128] += both[0:1, :]
        total = through_conv(dx[...].astype(F32) + wq + skip[...] * g32)
        emit(total[HALO:], total[:HALO])

    @pl.when(step == NCH - 1)
    def _():
        dact = dbc[...] + jnp.concatenate([dbs[...], dcs[...]], axis=1)
        total = through_conv(jnp.concatenate([dact, jnp.zeros((T, 128), F32)], axis=1))
        v = pre[HALO:, 128:].astype(F32) + bias[...]
        dt = jnp.maximum(v, 0.0) + jnp.log1p(jnp.exp(-jnp.abs(v)))
        sg = sigm(v)
        a = -jnp.exp(alog[...])
        ratio = jnp.where(v < -15.0, 1.0, sg / jnp.maximum(dt, 1e-30))
        isf = iota((T, 128), 1) < HEADS
        rs = rsum[...].T
        cs = csum[...]
        first = flag[0] == 0
        seam = dls[...] + dlr[...]
        dp = jnp.where(isf, rs - cs, cs - rs) + jnp.where(first, -1.0, 1.0) * seam
        tot = jnp.where(first, 1.0, 0.0) * jnp.sum(seam, axis=0, keepdims=True)
        inc = exact((iota((T, T), 0) <= iota((T, T), 1)).astype(F32), dp)
        dl = jnp.where(isf, inc, inc - dp) + tot
        suffix = (iota((Q, Q), 0) <= iota((Q, Q), 1)).astype(F32)
        head = iota((Q, 128), 1) < HEADS
        offs = []
        for k in range(T // Q):
            ro, co = roff[k * Q : (k + 1) * Q, :], coff[k * Q : (k + 1) * Q, :]
            sums = exact(suffix, jnp.concatenate([ro, co], axis=1))
            sr, sco = sums[:, :128], sums[:, 128:]
            fwd = sr + (sco[0:1] - sco)
            rev = (sr[0:1] - sr + ro) + (sco - co)
            offs.append(jnp.where(head, fwd, rev) + dkeep[k : k + 1, :])
        dl = dl + jnp.concatenate(offs, axis=0)
        dv = dl * a * sg + (cs + coff[...] + dls[...]) * ratio
        emit(jnp.concatenate([total[HALO:, :128], dv], axis=1), total[:HALO])

        at = SMALL_AT
        small[at : at + 1, 0:128] = jnp.sum(dv, axis=0, keepdims=True)
        small[at : at + 1, 128:] = jnp.sum(dl * dt * a, axis=0, keepdims=True)
        for q in range(INNER // CH):
            small[at + 1 + q : at + 2 + q, :] = ggain[:, CH * q : CH * (q + 1)]
        data = small[...].astype(BF)
        skeep_o[...] = jnp.where(first_core, data, jnp.zeros_like(data))
        ssend_o[...] = jnp.where(first_core, jnp.zeros_like(data), data)


def unproject(flag, dx, g, act, z, pre, conv_w, rows, dst, b, normt, nh, skip, bias, alog,
              rsum, csum, roff, coff, dkeep, dbc, dcs, dlr, ggain):
    T = dx.shape[0]
    E = T + HALO
    col = lambda rows: pl.BlockSpec((rows, CH), lambda i: (0, i))
    xcol = lambda rows: pl.BlockSpec((rows, CH), lambda i: (0, jnp.minimum(i, NCH - 2)))
    shapes = [((NCH, D // 2, CH), BF), ((NCH, D // 2, CH), BF), ((T, NCH * CH), BF), ((HALO, NCH * CH), BF),
              ((SMALL, CH), BF), ((SMALL, CH), BF)]
    return pl.pallas_call(
        functools.partial(unproject_kernel, T),
        grid=(NCH,),
        in_specs=[SMEM_SPEC, xcol(T), xcol(T), xcol(T), col(T), col(E), col(CONV), full((PAIRS, 16, T)),
                  xcol(64), full((T, 64)), full((D, T)), full((HALO, D)), xcol(1), full((1, 128)), full((1, 128)),
                  full((128, T)), full((T, 128)), full((T, 128)), full((T, 128)), full((8, 128)), full((T, 128)),
                  full((T, 64)), full((T, 128)), full((1, INNER))],
        out_specs=[pl.BlockSpec((1, D // 2, CH), lambda i: (i, 0, 0))] * 2 + [col(T), col(HALO)] + [full((SMALL, CH))] * 2,
        out_shape=[jax.ShapeDtypeStruct(s, d) for s, d in shapes],
        scratch_shapes=[pltpu.VMEM((D, 128), BF), pltpu.VMEM((E, CH), F32),
                        pltpu.VMEM((128, CH), BF), pltpu.VMEM((T, 64), F32), pltpu.VMEM((T, 128), F32),
                        pltpu.VMEM((SMALL, CH), F32), pltpu.VMEM((T // Q, (CONV - 1) * Q, Q + HALO), BF),
                        pltpu.VMEM((T // Q, (CONV - 1) * (Q + HALO), Q), BF)],
        compiler_params=params(),
        name="unproject",
    )(flag, dx, g, act, z, pre, conv_w, rows, dst, b, normt, nh, skip, bias, alog, rsum, csum, roff, coff, dkeep, dbc, dcs, dlr,
      ggain)


BOTH = ("dir", "dp")


def width(axis):
    return lax.axis_size(axis).bit_length() - 1


def exchange(v, mask_even, mask_odd):
    size = lax.axis_size("dir") * lax.axis_size("dp")
    return lax.ppermute(v, BOTH, [(i, i ^ (mask_odd if i & 1 else mask_even)) for i in range(size)])


def side_of(mask_even, mask_odd):
    me = lax.axis_index(BOTH)
    return jnp.where(me % 2 == 0, me & mask_even, me & mask_odd) != 0


def swap(v):
    mask = lax.axis_size("dp")
    return exchange(v, mask, mask)


def gather_rows(shard, ready, rest):
    bits = width("dp")
    down = list(range(bits - 1, 0, -1))
    even, odd = down, down[-1:] + down[:-1]
    out = shard
    for done, (e, o) in enumerate(zip(even, odd)):
        out = grow(out, done, e, o)
        if done == 0:
            out, rest = lax.optimization_barrier((out, rest))
        if done == 1:
            out, ready = lax.optimization_barrier((out, ready))
    return gather_finish(out, shard.shape), ready, rest


def grow(out, done, e, o):
    other = exchange(out, 1 << e, 1 << o)
    high = side_of(1 << e, 1 << o)
    return jnp.stack([jnp.where(high, other, out), jnp.where(high, out, other)], axis=done)


def gather_finish(out, shape):
    bits = width("dp")
    if bits == 0:
        return out
    other = exchange(out, 1, 1)
    high = side_of(1, 1)
    first = jnp.where(high, other, out)
    second = jnp.where(high, out, other)
    lead = max(bits - 1, 0)
    if lead > 1:
        second = jnp.moveaxis(second, 0, lead - 1)
    return jnp.stack([first, second], axis=lead).reshape((-1,) + shape[1:])


def halves(v, high, axis=0):
    n = v.shape[axis] // 2
    at = jnp.where(high, n, 0)
    return lax.dynamic_slice_in_dim(v, at, n, axis), lax.dynamic_slice_in_dim(v, n - at, n, axis)


def add(p, q):
    return (p.astype(F32) + q.astype(F32)).astype(BF)


def reduce_all(keep, send, keep_s, send_s, rows_s, later, inputs):
    bits = width("dp")
    masks = [1 << b for b in [bits] * width("dir") + list(range(1, bits))]
    odd = list(masks)
    for i in range(0, len(masks) - 1, 2):
        odd[i], odd[i + 1] = masks[i + 1], masks[i]
    order = list(zip(masks, odd))
    got, got_s = exchange(send, 1, 1), exchange(send_s, 1, 1)
    small = jnp.pad(add(keep_s, got_s), ((0, rows_s - SMALL), (0, 0)))
    high = side_of(*order[0])
    (keep, send), (got, got_send) = halves(keep, high, 1), halves(got, high, 1)
    none = jnp.zeros_like(small)
    send = jnp.concatenate([add(send, got_send).reshape(-1, CH), jnp.where(high, small, none)], axis=0)
    send, inputs = lax.optimization_barrier((send, inputs))
    keep = jnp.concatenate([add(keep, got).reshape(-1, CH), jnp.where(high, none, small)], axis=0)
    got = exchange(send, *order[0])
    extra, beside = later(*inputs)
    for at, pair in enumerate(order[1:]):
        high = side_of(*pair)
        (keep, send), (got, got_send) = halves(keep, high), halves(got, high)
        send = add(send, got_send)
        if at == 0:
            send, extra = lax.optimization_barrier((send, extra))
        keep, got = add(keep, got), exchange(send, *pair)
    buf = add(keep, got)
    for at, pair in enumerate(reversed(order)):
        n = buf.shape[0]
        if at == len(order) - 1:
            buf, beside = lax.optimization_barrier((buf, beside))
        got = exchange(jnp.concatenate([buf, extra], axis=0), *pair)
        extra = add(extra, got[n:])
        high = side_of(*pair)
        buf = jnp.concatenate([jnp.where(high, got[:n], buf), jnp.where(high, buf, got[:n])], axis=0)
    own = buf.reshape(2, -1, CH)
    return own, exchange(own, 1, 1), extra, exchange(extra, 1, 1), beside


def late_kernel(flag, own, other, own_l, other_l, own_s, other_s, own_e, other_e, zx_o, bc_o, dt_o, cw_o, cb_o, dtb_o, alog_o,
                skip_o, og_o, ng_o):
    half, part = D // 2, D // 4
    first = flag[5] == 0
    upper = jnp.where(first, own[...], other[...]).astype(F32)
    lower = jnp.where(first, other[...], own[...]).astype(F32)
    for q in range(2):
        for r in range(2):
            zx_o[part * r : part * (r + 1), CH * q : CH * (q + 1)] = upper[r, part * q : part * (q + 1)]
            zx_o[half + part * r : half + part * (r + 1), CH * q : CH * (q + 1)] = lower[r, part * q : part * (q + 1)]

    @pl.when(pl.program_id(0) == 0)
    def _():
        tops, bottoms = jnp.where(first, own_l[...], other_l[...]), jnp.where(first, other_l[...], own_l[...])
        tail = jnp.concatenate([tops[0], tops[1], bottoms[0], bottoms[1]], axis=0).astype(F32)
        bc_o[...] = tail[:, :128]
        dt_o[...] = tail[:, 128:].T[: 2 * HEADS, :]
        sm = jnp.where(first, own_s[0], other_s[0]).astype(F32)
        for q in range(NCH):
            n = CH if q < NCH - 1 else 2 * STATE
            cw_o[:, CH * q : CH * q + n] = sm[CONV * q : CONV * (q + 1), :n]
            cb_o[CH * q : CH * q + n] = sm[CONV * NCH + q, :n]
        at = SMALL_AT
        dtb_o[...] = sm[at, : 2 * HEADS]
        alog_o[...] = sm[at, 128 : 128 + 2 * HEADS]
        for q in range(INNER // CH):
            og_o[CH * q : CH * (q + 1)] = sm[at + 1 + q, :]
        ng = own_e[...].astype(F32) + other_e[...].astype(F32)
        for q in range(D // CH):
            ng_o[CH * q : CH * (q + 1)] = ng[q, :]
        skip_o[...] = sm[at + 10, :HEADS]


def late(flag, own, other, own_e, other_e):
    n = INNER // CH // 2
    taps = INNER + 2 * STATE
    shapes = [(D, 2 * INNER), (D, 2 * STATE), (2 * HEADS, D), (CONV, taps), (taps,), (2 * HEADS,), (2 * HEADS,), (HEADS,),
              (INNER,), (D,)]
    two = pl.BlockSpec((2, D // 2, CH), lambda i: (0, i, 0))
    last = pl.BlockSpec((2, D // 4, CH), lambda i: (0, NCH - 1, 0))
    small = pl.BlockSpec((1, SMALL, CH), lambda i: (0, NCH * D // (4 * SMALL), 0))
    extra = full((EXTRA, CH))
    return pl.pallas_call(
        late_kernel,
        grid=(n,),
        in_specs=[SMEM_SPEC, two, two, last, last, small, small, extra, extra],
        out_specs=[pl.BlockSpec((D, 2 * CH), lambda i: (0, n + i))] + [full(v) for v in shapes[1:]],
        out_shape=[jax.ShapeDtypeStruct(v, F32) for v in shapes],
        compiler_params=params(),
        name="late",
    )(flag, own, other, own, other, own, other, own_e, other_e)


def early_kernel(wg, wo, zx, zx_o, wo_o):
    zx_o[...] = wg[...].astype(F32)
    wo_o[...] = wo[...].astype(F32).T


def early(wg, wo, zx):
    n = INNER // CH // 2
    col = pl.BlockSpec((D, 2 * CH), lambda i: (0, i))
    return pl.pallas_call(
        early_kernel,
        grid=(n,),
        in_specs=[col, col, pl.BlockSpec(memory_space=pl.ANY)],
        out_specs=[col, pl.BlockSpec((2 * CH, D), lambda i: (i, 0))],
        out_shape=[jax.ShapeDtypeStruct((D, 2 * INNER), F32), jax.ShapeDtypeStruct((INNER, D), F32)],
        input_output_aliases={2: 0},
        compiler_params=params(),
        name="early",
    )(wg, wo, zx)


def apart(go, part, args):
    def nothing(v):
        return jax.tree.map(lambda o: jnp.zeros(o.shape, o.dtype), jax.eval_shape(part, v))

    return lax.cond(go, part, nothing, args)


def body(tokens, norm_gain, w_zx, w_bc, w_dt, conv_w, conv_b, dt_bias, a_log, d_skip, out_gain, w_out, doc_lengths, out_grad):
    T = tokens.shape[1]
    devices = lax.axis_size("dir") * lax.axis_size("dp")
    side = lax.axis_index("dir")
    tok = tokens.reshape(T, D)
    og = out_grad.reshape(T, D)
    shard = w_zx.shape[0]
    half = INNER // 2
    mine = jnp.concatenate([w_zx[:, INNER:], w_bc, w_dt, jnp.zeros((shard, 128 - 2 * HEADS), BF)], axis=1)
    halo = lax.ppermute(tok[T - HALO :], "dir", [(0, 1)])
    flag = jnp.concatenate([side[None].astype(jnp.int32), doc_lengths[0], lax.rem(lax.axis_index("dp"), 2)[None].astype(jnp.int32)])
    wide = NCH * CH
    cw = jnp.pad(conv_w, ((0, 0), (0, wide - conv_w.shape[1])))
    cb = jnp.pad(conv_b, (0, wide - conv_b.shape[0]))[None]
    lanes = lambda v: jnp.pad(v, (0, 128 - v.shape[0]))[None]
    skip = jnp.repeat(d_skip, HEADDIM)[None]
    rest = jnp.concatenate([w_zx[:, :half], w_zx[:, half:INNER], w_out], axis=0)
    ready = (halo, flag, cw, cb, lanes(dt_bias), lanes(a_log), skip, norm_gain[None], out_gain[None], og.T, doc_lengths[0, 0] >= 1)
    w1, ready, rest = gather_rows(mine, ready, rest)

    def finish(v):
        (flag, b, bt, c, ct, uv, keep, table, act, gm, z, pre, w1, cw, normt, nh, skip, bias, alog, tok, halo, ggain, og, gain_in,
         no, gg, wrc, st_in, rest) = v
        dcs, dlr, dst = aside(flag, gm, wrc, c, ct, st_in)
        dst_in = swap(dst)
        dx, rsum, csum, roff, coff, dkeep, dbc = unmix(flag, b, bt, c, ct, uv, keep, table, act, gm)
        keep_w, send_w, dpl, dph, keep_s, send_s = unproject(
            flag, dx, gm, act, z, pre, cw, table, dst_in, b, normt, nh, skip, bias, alog, rsum, csum, roff, coff, dkeep, dbc,
            dcs, dlr, ggain)
        rows = NCH * D
        total = -(-(rows + 4 * SMALL) // (16 * devices)) * 16 * devices

        def later(dpl, dph):
            bo, gn, gnh, part = deferred(dpl, dph, w1, gg, no, rest, tok, halo)
            back = lax.ppermute(gnh, "dir", [(1, 0)])
            gn = gn + jnp.pad(back, ((T - HALO, 0), (0, 0)))
            x32 = tok.astype(F32)
            rho = lax.rsqrt(jnp.mean(x32 * x32, axis=1, keepdims=True) + EPS)
            e_in = gn * gain_in
            gx = rho * e_in - x32 * (rho * rho * rho * jnp.mean(e_in * x32, axis=1, keepdims=True))
            return part, (bo, (og.astype(F32) + gx).astype(BF))

        own, other, own_e, other_e, (bo, grad_tokens) = reduce_all(
            keep_w, send_w, keep_s, send_s, (total - rows) // 4, later, (dpl, dph))
        return (bo, grad_tokens) + tuple(late(flag, own, other, own_e, other_e))

    def rest_of(v):
        w1, rest, (halo, flag, cw, cb, bias, alog, skip, gain_in, gain_out, ogt, go), tok, og = v
        rest = lax.all_gather(rest, "dp", axis=0, tiled=False)
        if shard % 16:
            rest = jnp.concatenate([rest[:, :shard].reshape(D, D), rest[:, shard : 2 * shard].reshape(D, D),
                                    rest[:, 2 * shard :].reshape(INNER, D)], axis=0)[None]
        normed, normt, nh, pre, z, act, rows, wrc, uv, keep, b, bt, c, ct, st = project(
            flag, tok, halo, gain_in, w1, cw, cb, bias, alog)
        st_in = swap(st)
        y = mix(flag, b, bt, c, uv, keep, rows, act, skip)
        no, gg, gm, dwg, dwo, ggain = gate(y, wrc, c, st_in, normed, normt, rest, og, ogt, gain_out)
        dwo, dwg = lax.psum((dwo, dwg), BOTH)
        args = (flag, b, bt, c, ct, uv, keep, rows, act, gm, z, pre, w1, cw, normt, nh, skip, bias, alog, tok, halo, ggain, og,
                gain_in, no, gg, wrc, st_in, rest)
        bo, grad_tokens, zx, g_bc, g_dt, g_cw, g_cb, g_dtb, g_alog, g_skip, g_og, g_ng = apart(go, finish, args)
        zx, g_wo = early(dwg, dwo, zx)
        return bo, grad_tokens, g_ng, zx, g_bc, g_dt.T, g_cw, g_cb, g_dtb, g_alog, g_skip, g_og, g_wo

    outs = rest_of((w1, rest, ready, tok, og))
    return (outs[0].reshape(tokens.shape), outs[1].reshape(tokens.shape)) + tuple(outs[2:])


def solution(mesh):
    rows, weight, whole = P("dp", "dir", None), P("dp", None), P()
    placed = (rows, whole, weight, weight, weight, whole, whole, whole, whole, whole, whole, weight, weight, rows)
    return jax.shard_map(body, mesh=mesh, in_specs=placed, out_specs=(rows, rows) + (whole,) * 11, check_vma=False)
```
